32 devices in a mesh: tower: 2 (over core), dp: 16 (over z, y, x).
Axes of the slice: x: 2, y: 2, z: 4, core: 2. Of those that a mesh axis runs over, the one named last changes fastest.
Arguments:
- embeddings: bfloat16 [2, 128, 128, 768], P('tower', 'dp'), may hold values from -6 to 6
- lengths: int32 [2, 128], P('tower', 'dp'), may hold values from 5 to 128, as said below
- labels: int32 [128], P('dp'), may hold values from 0 to 2
- qkv_weight: bfloat16 [768, 2304], P('dp'), may hold values from -0.21875 to 0.21875
- query_bias: bfloat16 [768], P('dp'), may hold values from -3 to 3
- value_bias: bfloat16 [768], P('dp'), may hold values from -3 to 3
- out_weight: bfloat16 [768, 768], P('dp'), may hold values from -0.625 to 0.625
- out_bias: bfloat16 [768], P('dp'), may hold values from -3 to 3
- attn_gain: bfloat16 [768], P('dp'), may hold values from 0.5 to 1.5
- attn_shift: bfloat16 [768], P('dp'), may hold values from -3 to 3
- up_weight: bfloat16 [768, 3072], P('dp'), may hold values from -0.21875 to 0.21875
- up_bias: bfloat16 [3072], P('dp'), may hold values from -3 to 3
- down_weight: bfloat16 [3072, 768], P('dp'), may hold values from -0.109375 to 0.109375
- down_bias: bfloat16 [768], P('dp'), may hold values from -3 to 3
- ffn_gain: bfloat16 [768], P('dp'), may hold values from 0.5 to 1.5
- ffn_shift: bfloat16 [768], P('dp'), may hold values from -3 to 3
- head_weight: bfloat16 [2304, 3], P('dp'), may hold values from -0.21875 to 0.21875
- head_bias: bfloat16 [3], replicated, may hold values from -3 to 3
Outputs:
- pooled: float32 [2, 128, 768], P('tower', 'dp')
- grad_embeddings: float32 [2, 128, 128, 768], P('tower', 'dp')
- grad_qkv_weight: float32 [768, 2304], P(('tower', 'dp'))
- grad_query_bias: float32 [768], P(('tower', 'dp'))
- grad_value_bias: float32 [768], P(('tower', 'dp'))
- grad_out_weight: float32 [768, 768], P(('tower', 'dp'))
- grad_out_bias: float32 [768], P(('tower', 'dp'))
- grad_attn_gain: float32 [768], P(('tower', 'dp'))
- grad_attn_shift: float32 [768], P(('tower', 'dp'))
- grad_up_weight: float32 [768, 3072], P(('tower', 'dp'))
- grad_up_bias: float32 [3072], P(('tower', 'dp'))
- grad_down_weight: float32 [3072, 768], P(('tower', 'dp'))
- grad_down_bias: float32 [768], P(('tower', 'dp'))
- grad_ffn_gain: float32 [768], P(('tower', 'dp'))
- grad_ffn_shift: float32 [768], P(('tower', 'dp'))
- grad_head_weight: float32 [2304, 3], P(('tower', 'dp'))
- grad_head_bias: float32 [3], replicated
The draws below stay inside these ranges and needn't reach their ends.
Inputs may be any that keep to these rules, and one draw needn't show every extreme that they name: `lengths`: a sentence's real tokens fill its first slots, the rest are padding; some sentence has all 128.
All inputs are finite; a program needn't handle non-finite values.
Results may differ from the reference program's by a relative error of at most 0.008.
Values may be sent and summed in bfloat16 or wider, within the bound.
No kernel may reach another device: no remote copies, remote signals or barrier semaphores. Data moves between devices by JAX's collectives and lax.ppermute only.
A program may use at most 192 MiB of HBM per device.

```python
import jax
import jax.numpy as jnp
from jax import lax

D = 768
HEADS = 12
HEAD_DIM = 64
FF = 3072
SEQ_LEN = 128
NCLASS = 3
PAIRS = 128


def draw_lengths(key, part):
    first_key, second_key, third_key = jax.random.split(key, 3)
    span = SEQ_LEN - 5
    left_draw = jax.random.randint(first_key, (2, PAIRS), 0, span + 1)
    right_draw = jax.random.randint(second_key, (2, PAIRS), 0, span + 1)
    base = 5 + left_draw * right_draw // span
    full_spot = jax.random.randint(third_key, (), 0, 2 * PAIRS)
    places = jnp.arange(2 * PAIRS).reshape(2, PAIRS)
    return jnp.where(places == full_spot, SEQ_LEN, base).astype(jnp.int32)


def set_ends(entries, own_key, smallest, high):
    longest = entries.shape.index(max(entries.shape))
    spots = []
    for shift in (0, 1):
        where = [jax.random.randint(jax.random.fold_in(own_key, axis), (), 0, length) for axis, length in enumerate(entries.shape)]
        where[longest] = (where[longest] + shift) % entries.shape[longest]
        spots.append(tuple(where))
    return entries.at[spots[0]].set(smallest).at[spots[1]].set(high)


def level_of(stream_key, dims, cuts, smallest, high):
    level, own = 1.0, jax.random.fold_in(stream_key, 6)
    for axis_at, blocks in cuts:
        draws = jnp.exp(jax.random.uniform(jax.random.fold_in(own, axis_at), (blocks,), jnp.float32, smallest / len(cuts), high / len(cuts)))
        level = level * jnp.repeat(draws, dims[axis_at] // blocks).reshape([-1 if axis == axis_at else 1 for axis in range(len(dims))])
    return level


def noise(stream_key, shape, scale, bound, pieces=(), held_as=jnp.bfloat16):
    factor_of = level_of(stream_key, shape, pieces, -0.22, 0.18) if pieces else 1.0
    result = jax.random.normal(stream_key, shape, jnp.float32) * scale * factor_of
    return jnp.minimum(jnp.maximum(result, -bound), bound).astype(held_as)


def setup_inputs(seed: int = 0) -> dict:
    key_of = jax.random.split(jax.random.key(seed), 19)
    return {
        "embeddings": noise(key_of[0], (2, PAIRS, SEQ_LEN, D), 1.0, 6.0, ((0, 2), (1, 16))),
        "lengths": draw_lengths(jax.random.fold_in(key_of[18], 71), 0),
        "labels": set_ends(jax.random.randint(key_of[2], (PAIRS,), 0, NCLASS), jax.random.fold_in(key_of[2], 1), 0, NCLASS - 1).astype(jnp.int32),
        "qkv_weight": noise(key_of[3], (D, 3 * D), D ** -0.5, 0.21875, ((0, 16),)),
        "query_bias": noise(key_of[4], (D,), 0.5, 3.0, ((0, 16),)),
        "value_bias": noise(key_of[5], (D,), 0.5, 3.0, ((0, 16),)),
        "out_weight": noise(key_of[6], (D, D), (D // 8) ** -0.5, 0.625, ((0, 16),)),
        "out_bias": noise(key_of[7], (D,), 0.5, 3.0, ((0, 16),)),
        "attn_gain": jnp.clip(1.0 + 0.1 * jax.random.normal(key_of[8], (D,), jnp.float32), 0.5, 1.5).astype(jnp.bfloat16),
        "attn_shift": noise(key_of[9], (D,), 0.3, 3.0, ((0, 16),)),
        "up_weight": noise(key_of[10], (D, FF), D ** -0.5, 0.21875, ((0, 16),)),
        "up_bias": noise(key_of[11], (FF,), 0.5, 3.0, ((0, 16),)),
        "down_weight": noise(key_of[12], (FF, D), FF ** -0.5, 0.109375, ((0, 16),)),
        "down_bias": noise(key_of[13], (D,), 0.3, 3.0, ((0, 16),)),
        "ffn_gain": jnp.clip(1.0 + 0.1 * jax.random.normal(key_of[14], (D,), jnp.float32), 0.5, 1.5).astype(jnp.bfloat16),
        "ffn_shift": noise(key_of[15], (D,), 0.3, 3.0, ((0, 16),)),
        "head_weight": noise(key_of[16], (3 * D, NCLASS), D ** -0.5, 0.21875, ((0, 16),)),
        "head_bias": noise(key_of[17], (NCLASS,), 1.0, 3.0),
    }


@jax.custom_vjp
def low(v):
    return lax.optimization_barrier(v.astype(jnp.bfloat16)).astype(jnp.float32)

@jax.custom_vjp
def low_back(v):
    return v

def low_keep(v):
    return (low(v), None)

def low_pass(kept, grad):
    return (grad,)

def back_keep(v):
    return (v, None)

def back_low(kept, grad):
    return (low(grad),)
low.defvjp(low_keep, low_pass)
low_back.defvjp(back_keep, back_low)
highest = lax.Precision.HIGHEST
eps_norm = 1e-12
gap_soft = 0.01

def matmul(left, right):
    return jnp.dot(left, right, precision=highest, preferred_element_type=jnp.float32)

def layer_norm(hidden, gain, shift):
    center = hidden - lax.optimization_barrier(jnp.mean(hidden, axis=-1, keepdims=True))
    spread = lax.optimization_barrier(jnp.mean(center * center, axis=-1, keepdims=True))
    return center * lax.rsqrt(spread + eps_norm) * gain + shift

def encode(rows_in, sent_len, params):
    qkv_weight, query_bias, value_bias, out_weight, out_bias, attn_gain, attn_shift, up_weight, up_bias, down_weight, down_bias, ffn_gain, ffn_shift = params
    count = rows_in.shape[0]
    width = rows_in.shape[-1]
    heads_shape = (count, SEQ_LEN, HEADS, HEAD_DIM)
    flat = rows_in.reshape(count * SEQ_LEN, width)
    joined = matmul(flat, qkv_weight)
    queries = low_back(low(joined[:, :width] + query_bias)).reshape(heads_shape)
    key_rows = low_back(low(joined[:, width:2 * width])).reshape(heads_shape)
    values = low_back(low(joined[:, 2 * width:] + value_bias)).reshape(heads_shape)
    raw = low_back(jnp.einsum('bqhd,bkhd->bhqk', queries, key_rows, precision=highest))
    valid = jnp.arange(SEQ_LEN)[None, :] < sent_len[:, None]
    scores = jnp.where(valid[:, None, None, :], raw * HEAD_DIM ** (-0.5), -1000000000.0)
    top = lax.optimization_barrier(jnp.max(scores, axis=-1, keepdims=True))
    total = jnp.log(lax.optimization_barrier(jnp.sum(jnp.exp(scores - top), axis=-1, keepdims=True))) + top
    probs = jnp.exp(scores - total)
    context = jnp.einsum('bhqk,bkhd->bqhd', low(probs), values, precision=highest)
    context = low_back(low(context.reshape(count * SEQ_LEN, width)))
    attended = low_back(matmul(context, out_weight)) + out_bias
    first = layer_norm(flat + attended, attn_gain, attn_shift)
    pre_act = low_back(matmul(low(first), up_weight)) + up_bias
    activated = low(jax.nn.gelu(pre_act, approximate=False))
    second = low_back(matmul(activated, down_weight)) + down_bias
    output = layer_norm(first + second, ffn_gain, ffn_shift).reshape(count, SEQ_LEN, width)
    mask = valid.astype(jnp.float32)
    summed = lax.optimization_barrier(jnp.sum(output * mask[:, :, None], axis=1))
    return summed / sent_len.astype(jnp.float32)[:, None]

def group_loss(params, head, block):
    tokens, sent_len, label = block
    count = label.shape[0]
    pooled = encode(tokens.reshape((2 * count,) + tokens.shape[2:]), sent_len.reshape(2 * count), params)
    pooled = pooled.reshape(2, count, pooled.shape[-1])
    left = pooled[0]
    right = pooled[1]
    gap = left - right
    feats = jnp.concatenate([left, right, jnp.sqrt(gap * gap + gap_soft)], axis=1)
    logits = matmul(feats, head[0]) + head[1]
    top = lax.optimization_barrier(jnp.max(logits, axis=1, keepdims=True))
    shifted = logits - top
    log_total = jnp.log(lax.optimization_barrier(jnp.sum(jnp.exp(shifted), axis=1)))
    onehot = (label[:, None] == jnp.arange(NCLASS)[None, :]).astype(jnp.float32)
    picked = lax.optimization_barrier(jnp.sum(shifted * onehot, axis=1))
    return (jnp.sum(log_total - picked), pooled)

def reference(embeddings, lengths, labels, qkv_weight, query_bias, value_bias, out_weight, out_bias, attn_gain, attn_shift, up_weight, up_bias, down_weight, down_bias, ffn_gain, ffn_shift, head_weight, head_bias):
    params = tuple((weight.astype(jnp.float32) for weight in (qkv_weight, query_bias, value_bias, out_weight, out_bias, attn_gain, attn_shift, up_weight, up_bias, down_weight, down_bias, ffn_gain, ffn_shift)))
    head = (head_weight.astype(jnp.float32), head_bias.astype(jnp.float32))
    tokens = embeddings.astype(jnp.float32)
    group = 16 if PAIRS % 16 == 0 else PAIRS
    blocks = PAIRS // group

    def total_loss(params, head, tokens):
        stacked = tokens.reshape(2, blocks, group, SEQ_LEN, D).transpose(1, 0, 2, 3, 4)
        lens = lengths.reshape(2, blocks, group).transpose(1, 0, 2)
        labs = labels.reshape(blocks, group)

        def one_block(carry, block):
            loss, pooled = group_loss(params, head, block)
            return (carry + loss, pooled)
        loss, pooled = lax.scan(jax.checkpoint(one_block), jnp.zeros((), jnp.float32), (stacked, lens, labs))
        return (loss, pooled.transpose(1, 0, 2, 3).reshape(2, PAIRS, D))
    loss, backward, pooled = jax.vjp(total_loss, params, head, tokens, has_aux=True)
    grad_params, grad_head, grad_tokens = backward(jnp.ones((), jnp.float32))
    return (pooled, grad_tokens, grad_params[0], grad_params[1], grad_params[2], grad_params[3], grad_params[4], grad_params[5], grad_params[6], grad_params[7], grad_params[8], grad_params[9], grad_params[10], grad_params[11], grad_params[12], grad_head[0], grad_head[1])
```

```python
from functools import partial

import jax
import jax.numpy as jnp
from jax import lax
from jax.sharding import PartitionSpec as P

HEADS = 12
HEAD_DIM = 64
NCLASS = 3
CHUNK = 384
FAR = 4

eps_norm = 1e-12
gap_soft = 0.01
highest = lax.Precision.HIGHEST
f32 = jnp.float32
b16 = jnp.bfloat16


def swap(x, axis, k):
    return lax.ppermute(x, axis, [(i, i ^ k) for i in range(lax.axis_size(axis))])


def places():
    low = lax.axis_size("dp") // FAR
    me = lax.axis_index("dp")
    return low, me // low, me % low


def in_order(pieces, me, axis):
    stack = jnp.stack(pieces, axis)
    return jnp.concatenate(
        [lax.dynamic_index_in_dim(stack, me ^ j, axis) for j in range(len(pieces))], axis
    )


def gather_rows(part):
    low, far, near = places()
    block = in_order([part] + [swap(part, "dp", j * low) for j in range(1, FAR)], far, 0)
    if low == 4:
        half = FAR // 2
        by_one, by_two = swap(block, "dp", 1), swap(block, "dp", 2)
        both = jnp.concatenate(
            [swap(by_one[:half], "dp", 2), swap(by_two[half:], "dp", 1)], 0
        )
        pieces = [block, by_one, by_two, both]
    else:
        pieces, bit = [block], 1
        while bit < low:
            pieces = pieces + [swap(p, "dp", bit) for p in pieces]
            bit *= 2
    return in_order(pieces, near, 1)


def to_chunks(shard):
    rows, cols = shard.shape
    half = cols // 2
    mine = lax.dynamic_slice_in_dim(shard, lax.axis_index("tower") * half, half, 1)
    return mine.reshape(rows, half // CHUNK, CHUNK).transpose(1, 0, 2).reshape(-1, CHUNK)


def from_chunks(mine, other, rows):
    low_half = lax.axis_index("tower") == 0
    a, b = jnp.where(low_half, mine, other), jnp.where(low_half, other, mine)
    both = jnp.stack([a, b])
    far, low, total = mine.shape[:3]
    n = total // rows
    both = both.reshape(2, far, low, n, rows, CHUNK).transpose(1, 2, 4, 0, 3, 5)
    return both.reshape(far * low * rows, 2 * n * CHUNK)


def tower_half(grad):
    tower = lax.axis_index("tower")
    low, _, _ = places()
    halves = grad.reshape((2, FAR, low, -1) + grad.shape[1:])
    got = swap(lax.dynamic_index_in_dim(halves, 1 - tower, 0, keepdims=False), "tower", 1)
    mine = lax.dynamic_index_in_dim(halves, tower, 0, keepdims=False)
    return (mine.astype(f32) + got.astype(f32)).astype(b16)


def add_low(a, b):
    return (a.astype(f32) + b.astype(f32)).astype(b16)


def scatter_rows(data):
    low, far, near = places()

    def at(k):
        return lax.dynamic_index_in_dim(data, near ^ k, 1, keepdims=False)

    if low == 4:
        half = FAR // 2
        corner = at(3)
        got_one, got_two = swap(corner[:half], "dp", 1), swap(corner[half:], "dp", 2)
        one, two = at(1), at(2)
        one = jnp.concatenate([one[:half], add_low(one[half:], got_two)], 0)
        two = jnp.concatenate([add_low(two[:half], got_one), two[half:]], 0)
        own = at(0).astype(f32) + swap(one, "dp", 1).astype(f32) + swap(two, "dp", 2).astype(f32)
    else:
        blocks, bit = [at(k) for k in range(low)], low // 2
        while bit:
            blocks = [
                add_low(blocks[k], swap(blocks[k + bit], "dp", bit)) for k in range(bit)
            ]
            bit //= 2
        own = blocks[0].astype(f32)
    total = lax.dynamic_index_in_dim(own, far, 0, keepdims=False)
    for j in range(1, FAR):
        sent = lax.dynamic_index_in_dim(own, far ^ j, 0, keepdims=False).astype(b16)
        total = total + swap(sent, "dp", j * low).astype(f32)
    return total


def sum_all(x):
    x = x + swap(x, "tower", 1)
    bit = 1
    while bit < lax.axis_size("dp"):
        x = x + swap(x, "dp", bit)
        bit *= 2
    return x


def contract_rows(left, right):
    return lax.dot_general(left, right, (((0,), (0,)), ((), ())), preferred_element_type=f32)


def contract_cols(left, right):
    return lax.dot_general(left, right, (((1,), (1,)), ((), ())), preferred_element_type=f32)


def norm_forward(hidden, gain, shift):
    center = hidden - jnp.mean(hidden, axis=-1, keepdims=True)
    inverse = lax.rsqrt(jnp.mean(center * center, axis=-1, keepdims=True) + eps_norm)
    normal = center * inverse
    return (normal * gain + shift, normal, inverse)


def norm_backward(upstream, normal, inverse, gain):
    scaled = upstream * gain
    inner = scaled - jnp.mean(scaled, axis=-1, keepdims=True)
    inner = inner - normal * jnp.mean(scaled * normal, axis=-1, keepdims=True)
    return (inverse * inner, jnp.sum(upstream * normal, axis=0), jnp.sum(upstream, axis=0))


def body(
    embeddings, lengths, labels, qkv_weight, query_bias, value_bias, out_weight, out_bias, attn_gain,
    attn_shift, up_weight, up_bias, down_weight, down_bias, ffn_gain, ffn_shift, head_weight, head_bias,
):
    width = embeddings.shape[-1]
    seq_len = embeddings.shape[2]
    count = embeddings.shape[1]
    rows = count * seq_len
    scale = HEAD_DIM ** (-0.5)
    heads_shape = (count, seq_len, HEADS, HEAD_DIM)
    leading = lax.axis_index("tower") == 0
    gelu_exact = partial(jax.nn.gelu, approximate=False)
    groups = lax.axis_size("dp")

    small = (
        query_bias, value_bias, out_bias, attn_gain, attn_shift, down_bias, ffn_gain, ffn_shift, up_bias,
        head_weight.reshape(-1),
    )
    small_sizes = [s.shape[0] for s in small]
    packed = jnp.concatenate(small)
    pad_rows = -(-packed.shape[0] // (8 * CHUNK)) * 8
    packed = jnp.pad(packed, (0, pad_rows * CHUNK - packed.shape[0])).reshape(pad_rows, CHUNK)
    shard_rows = qkv_weight.shape[0]
    first_part = jnp.concatenate([to_chunks(qkv_weight), to_chunks(out_weight), packed], 0)
    cut = first_part.shape[0] - pad_rows
    near_first = gather_rows(first_part)
    other_first = swap(near_first[:, :, :cut], "tower", 1)
    near_up = gather_rows(to_chunks(up_weight))
    other_up = swap(near_up, "tower", 1)
    proj_down = lax.all_gather(
        lax.dynamic_slice_in_dim(
            down_weight, lax.axis_index("tower") * (down_weight.shape[0] // 2), down_weight.shape[0] // 2, 0
        ),
        ("dp", "tower"), axis=0, tiled=True,
    )
    n_qkv = qkv_weight.shape[1] // 2 // CHUNK * shard_rows
    proj_qkv = from_chunks(near_first[:, :, :n_qkv], other_first[:, :, :n_qkv], shard_rows)
    proj_out = from_chunks(near_first[:, :, n_qkv:cut], other_first[:, :, n_qkv:cut], shard_rows)
    proj_up = from_chunks(near_up, other_up, shard_rows)
    flat_small = near_first[:, :, cut:].reshape(groups, pad_rows * CHUNK)
    whole, at = [], 0
    for size in small_sizes:
        whole.append(flat_small[:, at : at + size].reshape(-1).astype(f32))
        at += size
    (bias_query, bias_value, bias_out, gain_one, shift_one, bias_down, gain_two, shift_two, bias_up, head_full) = whole
    head_full = head_full.reshape(-1, NCLASS)

    flat = embeddings[0].reshape(rows, width)
    sent_len = lengths[0]
    joined = jnp.dot(flat, proj_qkv, preferred_element_type=f32)
    query_heads = (joined[:, :width] + bias_query).astype(b16).reshape(heads_shape)
    key_heads = joined[:, width : 2 * width].astype(b16).reshape(heads_shape)
    value_heads = (joined[:, 2 * width :] + bias_value).astype(b16).reshape(heads_shape)
    valid = jnp.arange(seq_len)[None, :] < sent_len[:, None]
    raw = jnp.einsum("bqhd,bkhd->bhqk", query_heads, key_heads, preferred_element_type=f32)
    scores = jnp.where(valid[:, None, None, :], raw * scale, -1000000000.0)
    top = jnp.max(scores, axis=-1, keepdims=True)
    total = jnp.log(jnp.sum(jnp.exp(scores - top), axis=-1, keepdims=True)) + top
    probs = jnp.exp(scores - total)
    probs_low = probs.astype(b16)
    context = jnp.einsum("bhqk,bkhd->bqhd", probs_low, value_heads, preferred_element_type=f32)
    context = context.reshape(rows, width).astype(b16)
    attended = jnp.dot(context, proj_out, preferred_element_type=f32) + bias_out
    first, first_norm, first_inv = norm_forward(flat.astype(f32) + attended, gain_one, shift_one)
    first_low = first.astype(b16)
    pre_act = jnp.dot(first_low, proj_up, preferred_element_type=f32) + bias_up
    activated = gelu_exact(pre_act).astype(b16)
    second = jnp.dot(activated, proj_down, preferred_element_type=f32) + bias_down
    output, second_norm, second_inv = norm_forward(first + second, gain_two, shift_two)
    mask = valid.astype(f32)
    length_f = sent_len.astype(f32)[:, None]
    pooled = jnp.sum(output.reshape(count, seq_len, width) * mask[:, :, None], axis=1) / length_f

    partner = swap(pooled, "tower", 1)
    left = jnp.where(leading, pooled, partner)
    right = jnp.where(leading, partner, pooled)
    gap = left - right
    soft_gap = jnp.sqrt(gap * gap + gap_soft)
    feats = jnp.concatenate([left, right, soft_gap], axis=1)
    logits = jnp.dot(feats, head_full, precision=highest) + head_bias.astype(f32)
    onehot = (labels[:, None] == jnp.arange(NCLASS)[None, :]).astype(f32)
    logit_grad = jax.nn.softmax(logits, axis=-1) - onehot
    head_grad = 0.5 * jnp.dot(feats.T, logit_grad, precision=highest)
    class_grad = 0.5 * jnp.sum(logit_grad, axis=0)
    feat_grad = jnp.dot(logit_grad, head_full.T, precision=highest)
    slope = gap / soft_gap
    left_grad = feat_grad[:, :width] + slope * feat_grad[:, 2 * width :]
    right_grad = feat_grad[:, width : 2 * width] - slope * feat_grad[:, 2 * width :]
    pooled_grad = jnp.where(leading, left_grad, right_grad)

    output_grad = ((pooled_grad / length_f)[:, None, :] * mask[:, :, None]).reshape(rows, width)
    sum_grad, gain_two_grad, shift_two_grad = norm_backward(output_grad, second_norm, second_inv, gain_two)
    down_bias_grad = jnp.sum(sum_grad, axis=0)
    sum_low = sum_grad.astype(b16)
    down_grad = contract_rows(activated, sum_low).astype(b16)
    down_out = scatter_rows(tower_half(down_grad))
    act_grad = contract_cols(sum_low, proj_down)
    pre_grad = jax.vjp(gelu_exact, pre_act)[1](act_grad)[0]
    up_bias_grad = jnp.sum(pre_grad, axis=0)
    pre_low = pre_grad.astype(b16)
    up_grad = contract_rows(first_low, pre_low).astype(b16)
    up_out = scatter_rows(tower_half(up_grad))
    first_grad = sum_grad + contract_cols(pre_low, proj_up)
    mid_grad, gain_one_grad, shift_one_grad = norm_backward(first_grad, first_norm, first_inv, gain_one)
    out_bias_grad = jnp.sum(mid_grad, axis=0)
    mid_low = mid_grad.astype(b16)
    out_grad = contract_rows(context, mid_low).astype(b16)
    context_grad = contract_cols(mid_low, proj_out).astype(b16).reshape(heads_shape)
    prob_grad = jnp.einsum("bqhd,bkhd->bhqk", context_grad, value_heads, preferred_element_type=f32)
    value_grad = jnp.einsum("bhqk,bqhd->bkhd", probs_low, context_grad, preferred_element_type=f32)
    score_grad = probs * (prob_grad - jnp.sum(prob_grad * probs, axis=-1, keepdims=True)) * scale
    score_low = score_grad.astype(b16)
    query_grad = jnp.einsum("bhqk,bkhd->bqhd", score_low, key_heads, preferred_element_type=f32)
    key_grad = jnp.einsum("bhqk,bqhd->bkhd", score_low, query_heads, preferred_element_type=f32)
    qkv_grad = jnp.concatenate(
        [query_grad.reshape(rows, width), key_grad.reshape(rows, width), value_grad.reshape(rows, width)], axis=1
    ).astype(b16)
    query_bias_grad = jnp.sum(qkv_grad[:, :width].astype(f32), axis=0)
    value_bias_grad = jnp.sum(qkv_grad[:, 2 * width :].astype(f32), axis=0)
    qkv_full_grad = contract_rows(flat, qkv_grad).astype(b16)
    last_out = scatter_rows(tower_half(jnp.concatenate([qkv_full_grad, out_grad], 1)))
    input_grad = contract_cols(qkv_grad, proj_qkv) + mid_grad

    vectors = (
        query_bias_grad, value_bias_grad, out_bias_grad, gain_one_grad, shift_one_grad, up_bias_grad, down_bias_grad,
        gain_two_grad, shift_two_grad, head_grad.reshape(-1), class_grad,
    )
    sizes = [v.shape[0] for v in vectors]
    flat_vec = jnp.concatenate(vectors)
    padded = -(-flat_vec.shape[0] // 1024) * 1024
    summed = sum_all(jnp.pad(flat_vec, (0, padded - flat_vec.shape[0])).reshape(-1, 128)).reshape(-1)
    place = lax.axis_index("tower") * groups + lax.axis_index("dp")
    outs, at = [], 0
    for size in sizes[:-1]:
        mine = size // (2 * groups)
        outs.append(lax.dynamic_slice_in_dim(summed, at + place * mine, mine))
        at += size
    class_sum = summed[at : at + NCLASS]
    n_qkv_cols = 3 * width
    return (
        pooled[None],
        input_grad.reshape(embeddings.shape),
        last_out[:, :n_qkv_cols],
        outs[0], outs[1],
        last_out[:, n_qkv_cols:],
        outs[2], outs[3], outs[4],
        up_out,
        outs[5],
        down_out,
        outs[6], outs[7], outs[8],
        outs[9].reshape(-1, NCLASS),
        class_sum,
    )


def solution(mesh):
    rows, vec = P("dp", None), P("dp")
    out_rows, out_vec = P(("tower", "dp"), None), P(("tower", "dp"))
    return jax.shard_map(
        body,
        mesh=mesh,
        in_specs=(
            P("tower", "dp", None, None), P("tower", "dp"), vec,
            rows, vec, vec, rows, vec, vec, vec, rows, vec, rows, vec, vec, vec, rows, P(),
        ),
        out_specs=(
            P("tower", "dp", None), P("tower", "dp", None, None),
            out_rows, out_vec, out_vec, out_rows, out_vec, out_vec, out_vec, out_rows, out_vec, out_rows, out_vec,
            out_vec, out_vec, out_rows, P(),
        ),
        check_vma=False,
    )
```

```python
from functools import partial
import math

import jax
import jax.numpy as jnp
from jax import lax
from jax.experimental import pallas as pl
from jax.experimental.pallas import tpu as pltpu
from jax.sharding import PartitionSpec as P

HEADS = 12
HEAD_DIM = 64
NCLASS = 3
CHUNK = 384
FAR = 4

eps_norm = 1e-12
gap_soft = 0.01
f32 = jnp.float32
b16 = jnp.bfloat16


def swap(x, axis, k):
    return lax.ppermute(x, axis, [(i, i ^ k) for i in range(lax.axis_size(axis))])


def places():
    low = lax.axis_size("dp") // FAR
    me = lax.axis_index("dp")
    return low, me // low, me % low


def in_order(pieces, me, axis):
    stack = jnp.stack(pieces, axis)
    return jnp.concatenate(
        [lax.dynamic_index_in_dim(stack, me ^ j, axis) for j in range(len(pieces))], axis
    )


def far_pieces(part):
    low, _, _ = places()
    return [part] + [swap(part, "dp", j * low) for j in range(1, FAR)]


def after(x, *deps):
    return lax.optimization_barrier((x, *deps))[0]


def gather_near(block, *ready):
    half = FAR // 2
    by_one, by_two = after((swap(block, "dp", 1), swap(block, "dp", 2)), *ready)
    return [block, by_one, by_two, swap(by_one[:half], "dp", 2), swap(by_two[half:], "dp", 1)]


def gather_any(block):
    low, _, near = places()
    pieces, bit = [block], 1
    while bit < low:
        pieces = pieces + [swap(p, "dp", bit) for p in pieces]
        bit *= 2
    return in_order(pieces, near, 1)


def to_chunks(shard):
    rows, cols = shard.shape
    half = cols // 2
    mine = lax.dynamic_slice_in_dim(shard, lax.axis_index("tower") * half, half, 1)
    return mine.reshape(rows, half // CHUNK, CHUNK).transpose(1, 0, 2).reshape(-1, CHUNK)


def from_chunks(mine, rows):
    other = swap(mine, "tower", 1)
    low_half = lax.axis_index("tower") == 0
    both = jnp.stack([jnp.where(low_half, mine, other), jnp.where(low_half, other, mine)])
    far, low, total = mine.shape[:3]
    n = total // rows
    both = both.reshape(2, far, low, n, rows, CHUNK).transpose(1, 2, 4, 0, 3, 5)
    return both.reshape(far, low * rows, 2 * n * CHUNK)


def add_low(a, b):
    return (a.astype(f32) + b.astype(f32)).astype(b16)


class Scatter:
    def __init__(self, parts):
        self.mine, *others = parts
        self.first = swap(others[0], "tower", 1)
        self.rest = swap(after(others[1], self.first), "tower", 1)
        self.corner = self.side = self.far = None

    def both(self, k, part=slice(None)):
        got = self.first[part] if k == 3 else self.rest[k, part]
        return self.mine[k, part].astype(f32) + got.astype(f32)

    def corners(self):
        if self.corner is None:
            half = FAR // 2
            self.corner = (
                swap(self.both(3, slice(0, half)).astype(b16), "dp", 1),
                swap(self.both(3, slice(half, FAR)).astype(b16), "dp", 2),
            )
        return self.corner

    def sides(self):
        if self.side is None:
            half = FAR // 2
            first, second = slice(0, half), slice(half, FAR)
            for_one, for_two = self.corners()
            one = [self.both(1, first).astype(b16), (self.both(1, second) + for_two.astype(f32)).astype(b16)]
            two = [(self.both(2, first) + for_one.astype(f32)).astype(b16), self.both(2, second).astype(b16)]
            self.sent = jnp.concatenate(one, 0), jnp.concatenate(two, 0)
            self.side = swap(self.sent[0], "dp", 1), swap(self.sent[1], "dp", 2)
        return self.side

    def fars(self):
        if self.far is None:
            low = lax.axis_size("dp") // FAR
            one, two = self.sides()
            self.own = self.both(0) + one.astype(f32) + two.astype(f32)
            self.far = [swap(self.own[j].astype(b16), "dp", j * low) for j in range(1, FAR)]
        return self.far

    def sum(self):
        far = self.fars()
        return self.own[0] + far[0].astype(f32) + far[1].astype(f32) + far[2].astype(f32)


def scatter_any(grad):
    low, far, near = places()
    tower = lax.axis_index("tower")
    halves = grad.reshape((2, FAR, low, -1) + grad.shape[1:])
    got = swap(lax.dynamic_index_in_dim(halves, 1 - tower, 0, keepdims=False), "tower", 1)
    data = add_low(lax.dynamic_index_in_dim(halves, tower, 0, keepdims=False), got)
    blocks = [lax.dynamic_index_in_dim(data, near ^ k, 1, keepdims=False) for k in range(low)]
    bit = low // 2
    while bit:
        blocks = [add_low(blocks[k], swap(blocks[k + bit], "dp", bit)) for k in range(bit)]
        bit //= 2
    own = [lax.dynamic_index_in_dim(blocks[0], far ^ j, 0, keepdims=False) for j in range(FAR)]
    total = own[0].astype(f32)
    for j in range(1, FAR):
        total = total + swap(own[j], "dp", j * low).astype(f32)
    return total


def add_from(x, axis, k):
    return x + swap(x, axis, k)


TILE = 192
PACK = 16
PAIR = 2 * HEAD_DIM
GROUP = 3
Q_BIAS, V_BIAS, O_BIAS, GAIN_1, SHIFT_1, D_BIAS, GAIN_2, SHIFT_2 = range(8)


def dot(a, b):
    return jnp.dot(a, b, preferred_element_type=f32)


def dot_nt(a, b):
    return lax.dot_general(a, b, (((1,), (1,)), ((), ())), preferred_element_type=f32)


def dot_tn(a, b):
    return lax.dot_general(a, b, (((0,), (0,)), ((), ())), preferred_element_type=f32)


def tile_at(t):
    return pl.ds(pl.multiple_of(t * TILE, TILE), TILE)


def sentence_rows(offs, b, seq):
    return pl.ds(pl.multiple_of(offs[b], PACK), seq)


def split_heads(x):
    left = lax.broadcasted_iota(jnp.int32, x.shape, 1) < HEAD_DIM
    zero = jnp.zeros_like(x)
    return jnp.concatenate([jnp.where(left, x, zero), jnp.where(left, zero, x)], 0)


def join_heads(x):
    seq = x.shape[0] // 2
    left = lax.broadcasted_iota(jnp.int32, (seq, PAIR), 1) < HEAD_DIM
    return jnp.where(left, x[:seq], x[seq:])


def by_head(fn, x):
    half = x.shape[0] // 2
    return jnp.concatenate([fn(x[:half]), fn(x[half:])], 0)


def by_length(lens, count, seq, step):
    def one(b, _):
        @pl.when(lens[b] > seq // 2)
        def _():
            step(b, seq)

        @pl.when(lens[b] <= seq // 2)
        def _():
            step(b, seq // 2)

        return 0

    lax.fori_loop(0, count, one, 0)


def norm_rows(hidden):
    center = hidden - jnp.mean(hidden, axis=-1, keepdims=True)
    inverse = lax.rsqrt(jnp.mean(center * center, axis=-1, keepdims=True) + eps_norm)
    return center * inverse, inverse


def norm_back(upstream, normal, inverse, gain):
    scaled = upstream * gain
    inner = scaled - jnp.mean(scaled, axis=-1, keepdims=True)
    return inverse * (inner - normal * jnp.mean(scaled * normal, axis=-1, keepdims=True))


def row_of(vec, i):
    return vec[i : i + 1, :].astype(f32)


def add_row(sums, i, x):
    sums[i : i + 1, :] += jnp.sum(x, axis=0, keepdims=True)


def parts_kernel(place, wqkv, wout, wup, wdown, packed, first, second, third):
    def put(src, dst, at):
        rows, half = src.shape[0], src.shape[1] // 2
        for c in range(half // CHUNK):
            dst[at : at + rows, :] = src[:, pl.ds(pl.multiple_of(place[0] * half + c * CHUNK, 128), CHUNK)]
            at += rows
        return at

    at = put(wout, first, put(wqkv, first, 0))
    first[at:, :] = packed[...]
    put(wup, second, 0)
    put(wdown, third, 0)


def fetch(place, pieces, targets, sems):
    copies = []
    for side in range(2):
        tower = place[0] if side == 0 else 1 - place[0]
        block, by_one, by_two, low, high = pieces[5 * side : 5 * side + 5]
        half = FAR // 2
        spots = ((block, 0, 0, FAR), (by_one, 1, 0, FAR), (by_two, 2, 0, FAR), (low, 3, 0, half), (high, 3, half, half))
        for piece, k, far, size in spots:
            at = 0
            for weight, rows in targets:
                cols = weight.shape[2] // 2
                for c in range(cols // CHUNK):
                    row = pl.multiple_of((place[1] ^ k) * rows, PACK)
                    col = pl.multiple_of(tower * cols + c * CHUNK, 128)
                    copies.append(
                        pltpu.make_async_copy(
                            piece.at[:, pl.ds(at, rows), :],
                            weight.at[pl.ds(far, size), pl.ds(row, rows), pl.ds(col, CHUNK)],
                            sems.at[len(copies)],
                        )
                    )
                    at += rows
    for copy in copies:
        copy.start()
    return copies


def deal(place, acc, outs, base=0):
    cols = acc.shape[1]
    if len(outs) == 1:
        outs[0][:, base : base + cols] = acc[...].astype(b16)
        return
    mine, first, rest = outs
    rows = first.shape[1]
    for own in (False, True):
        side = place[0] if own else 1 - place[0]
        for k in range(4):
            target = mine.at[k] if own else first if k == 3 else rest.at[k]
            for j in range(FAR):
                at = (side * 4 * FAR + (place[2] ^ j) * 4 + (place[1] ^ k)) * rows
                target[j, :, base : base + cols] = acc[pl.ds(pl.multiple_of(at, 8), rows), :].astype(b16)


def flat_of(weight, cols=slice(None)):
    block = weight[:, :, cols]
    return block.reshape(block.shape[0] * block.shape[1], block.shape[2])


def attend_kernel(n_pieces, lens, offs, tiles, place, x_ref, vec, *refs):
    pieces, refs = refs[:n_pieces], refs[n_pieces:]
    if n_pieces:
        sinks, refs = refs[:8], refs[8:]
        wqkv, wout, xs, qkv, probs, ctx, n1, inv1, got, sent = refs
        copies = fetch(place, pieces, ((wqkv, wqkv.shape[1] // 4), (wout, wout.shape[1] // 4)), got)
    else:
        wqkv, wout = refs[:2]
        sinks, refs = refs[2:8], refs[8:]
        xs, qkv, probs, ctx, n1, inv1, sent = refs
        copies = []
    held = (wqkv, wout, xs, qkv, probs, ctx, n1, inv1)[8 - len(sinks) :]
    count, seq, width = x_ref.shape
    leaving = []

    def leave(*which):
        for ref in which:
            for i, own in enumerate(held):
                if own is ref:
                    copy = pltpu.make_async_copy(ref, sinks[i], sent.at[i])
                    copy.start()
                    leaving.append(copy)

    xs[...] = jnp.zeros_like(xs)
    ctx[...] = jnp.zeros_like(ctx)

    def pack(b, _):
        def block(i, _):
            at = pl.multiple_of(offs[b] + i * PACK, PACK)
            xs[pl.ds(at, PACK), :] = x_ref[b, pl.ds(pl.multiple_of(i * PACK, PACK), PACK), :]
            return 0

        return lax.fori_loop(0, (lens[b] + PACK - 1) // PACK, block, 0)

    lax.fori_loop(0, count, pack, 0)
    for copy in copies:
        copy.wait()
    leave(wqkv, wout, xs)

    def project(t, _):
        x = xs[tile_at(t), :]
        for c in range(3):
            cols = slice(c * width, (c + 1) * width)
            joined = dot(x, flat_of(wqkv, cols))
            if c == 0:
                joined = (joined + row_of(vec, Q_BIAS)) * (HEAD_DIM ** -0.5)
            if c == 2:
                joined = joined + row_of(vec, V_BIAS)
            qkv[tile_at(t), cols] = joined.astype(b16)
        return 0

    lax.fori_loop(0, tiles[0], project, 0)
    qkv[pl.ds(pl.multiple_of(tiles[0] * TILE, TILE), seq), :] = jnp.zeros((seq, 3 * width), b16)
    leave(qkv)

    def attend(b, size):
        rows, key_rows = sentence_rows(offs, b, seq), sentence_rows(offs, b, size)
        valid = lax.broadcasted_iota(jnp.int32, (size, seq), 0) < lens[b]

        def softmax(s):
            s = jnp.where(valid, s, -1000000000.0)
            e = jnp.exp(s - jnp.max(s, axis=0, keepdims=True))
            return (e * (1.0 / jnp.sum(e, axis=0, keepdims=True))).astype(b16)

        for group in range(0, width // PAIR, GROUP):
            pairs = range(group, group + GROUP)
            cols = [slice(p * PAIR, (p + 1) * PAIR) for p in pairs]
            queries = [qkv[rows, c] for c in cols]
            keys = [split_heads(qkv[key_rows, width + c.start : width + c.stop]) for c in cols]
            vals = [split_heads(qkv[key_rows, 2 * width + c.start : 2 * width + c.stop]) for c in cols]
            scores = [dot_nt(k, q) for k, q in zip(keys, queries)]
            lows = [by_head(softmax, s) for s in scores]
            outs = [dot_tn(low, v).astype(b16) for low, v in zip(lows, vals)]
            for p, c, low, out in zip(pairs, cols, lows, outs):
                probs[b, p * 2 * size : (p + 1) * 2 * size, :] = low
                ctx[rows, c] = out

    by_length(lens, count, seq, attend)
    leave(probs, ctx)

    def out(t, _):
        rows = tile_at(t)
        attended = dot(ctx[rows, :], flat_of(wout)) + row_of(vec, O_BIAS)
        normal, inverse = norm_rows(xs[rows, :].astype(f32) + attended)
        n1[rows, :] = normal
        inv1[rows, :] = jnp.broadcast_to(inverse, (TILE, 128))
        return 0

    lax.fori_loop(0, tiles[0], out, 0)
    leave(n1, inv1)
    for copy in leaving:
        copy.wait()


def inside(offs, lens, b, t):
    row = t * TILE + lax.broadcasted_iota(jnp.int32, (TILE, 1), 0)
    return (row >= offs[b]) & (row < offs[b] + lens[b])


def take_weight(step, tiles, place, pieces, refs, rows_of):
    if not pieces:
        return refs[0], refs[1:], lambda: None
    sink, refs = refs[0], refs[1:]
    weight, got, sent, refs = refs[-3], refs[-2], refs[-1], refs[:-3]
    leave = pltpu.make_async_copy(weight, sink, sent.at[0])

    @pl.when(step == 0)
    def _():
        for copy in fetch(place, pieces, ((weight, rows_of),), got):
            copy.wait()
        leave.start()

    def finish():
        @pl.when(step == pl.num_programs(0) - 1)
        def _():
            leave.wait()

    return weight, refs, finish


def up_kernel(n_pieces, lens, offs, tiles, place, n1, vec, ups, *refs):
    t = pl.program_id(0)
    pieces, refs = refs[:n_pieces], refs[n_pieces:]
    rows_of = pieces[0].shape[1] * CHUNK * 2 // (ups.shape[0] * ups.shape[1]) if n_pieces else 0
    wup, (act, slope), finish = take_weight(t, tiles, place, pieces, refs, rows_of)
    width = n1.shape[1]

    @pl.when(t < tiles[0])
    def _():
        low = (n1[...] * row_of(vec, GAIN_1) + row_of(vec, SHIFT_1)).astype(b16)
        for c in range(ups.shape[0]):
            cols = slice(c * width, (c + 1) * width)
            pre = dot(low, flat_of(wup, cols)) + row_of(ups, c)
            half = 0.5 * (1.0 + lax.erf(pre * (0.5 ** 0.5)))
            act[:, cols] = (pre * half).astype(b16)
            slope[:, cols] = (half + pre * (jnp.exp(-0.5 * pre * pre) * 0.3989422804014327)).astype(b16)

    finish()


def down_kernel(n_pieces, lens, offs, tiles, place, n1, act, vec, *refs):
    t = pl.program_id(0)
    pieces, refs = refs[:n_pieces], refs[n_pieces:]
    rows_of = pieces[0].shape[1] if n_pieces else 0
    wdown, (n2, inv2, pooled), finish = take_weight(t, tiles, place, pieces, refs, rows_of)
    width = n1.shape[1]
    count = pooled.shape[0]

    @pl.when(t == 0)
    def _():
        pooled[...] = jnp.zeros_like(pooled)

    @pl.when(t < tiles[0])
    def _():
        total = n1[...] * row_of(vec, GAIN_1) + row_of(vec, SHIFT_1) + row_of(vec, D_BIAS)
        total = total + dot(act[...], flat_of(wdown))
        normal, inverse = norm_rows(total)
        n2[...] = normal
        inv2[...] = jnp.broadcast_to(inverse, (TILE, 128))
        for b in range(count):
            add_row(pooled, b, jnp.where(inside(offs, lens, b, t), normal, 0.0))

    @pl.when(t == pl.num_programs(0) - 1)
    def _():
        for b in range(count):
            size = jnp.full((1, width), lens[b], jnp.int32).astype(f32)
            pooled[b : b + 1, :] = pooled[b : b + 1, :] / size * row_of(vec, GAIN_2) + row_of(vec, SHIFT_2)

    finish()


def accumulate(t, acc, cols, left, right):
    @pl.when(t == 0)
    def _():
        acc[:, cols] = dot_tn(left, right)

    @pl.when(t > 0)
    def _():
        acc[:, cols] += dot_tn(left, right)


def pair_head(lens, place, labels, bias, pooled, partner, head, tops):
    count, width = pooled.shape
    mine, other = pooled[...], partner[...]
    first = place[0] == 0
    left, right = jnp.where(first, mine, other), jnp.where(first, other, mine)
    gap = left - right
    soft = jnp.sqrt(gap * gap + gap_soft)
    feats = (left, right, soft)
    row = lax.broadcasted_iota(jnp.int32, (count, 1), 0)
    label = jnp.zeros((count, 1), jnp.int32)
    size = jnp.zeros((count, 1), jnp.int32)
    for b in range(count):
        label = jnp.where(row == b, labels[b], label)
        size = jnp.where(row == b, lens[b], size)
    logits = []
    for c in range(NCLASS):
        terms = [
            jnp.sum(feats[i] * head[c : c + 1, i * width : (i + 1) * width], axis=-1, keepdims=True) for i in range(3)
        ]
        logits.append(terms[0] + terms[1] + terms[2] + bias[c])
    top = jnp.maximum(jnp.maximum(logits[0], logits[1]), logits[2])
    exps = [jnp.exp(x - top) for x in logits]
    norm = exps[0] + exps[1] + exps[2]
    grads = [exps[c] / norm - jnp.where(label == c, 1.0, 0.0) for c in range(NCLASS)]
    back = []
    tops[...] = jnp.zeros_like(tops)
    for i in range(3):
        cols = slice(i * width, (i + 1) * width)
        back.append(sum(grads[c] * head[c : c + 1, cols] for c in range(NCLASS)))
        for c in range(NCLASS):
            tops[c : c + 1, cols] = 0.5 * jnp.sum(grads[c] * feats[i], axis=0, keepdims=True)
    for c in range(NCLASS):
        tops[NCLASS + c : NCLASS + c + 1, 0:128] = jnp.broadcast_to(0.5 * jnp.sum(grads[c], axis=0, keepdims=True), (1, 128))
    slope = gap / soft
    pooled_grad = jnp.where(first, back[0] + slope * back[2], back[1] - slope * back[2])
    return pooled_grad / size.astype(f32)


def down_back_kernel(
    lens, offs, tiles, place, labels, bias, pooled, partner, head, act, n2, inv2, vec, sum_grad, *refs
):
    *outs, sums, tops, acc, per_row = refs
    t = pl.program_id(0)
    count, width = pooled.shape

    @pl.when(t == 0)
    def _():
        per_row[...] = pair_head(lens, place, labels, bias, pooled, partner, head, tops)
        sums[...] = jnp.zeros_like(sums)

    @pl.when(t < tiles[0])
    def _():
        up = jnp.zeros((TILE, width), f32)
        for b in range(count):
            up = jnp.where(inside(offs, lens, b, t), per_row[b : b + 1, :], up)
        normal = n2[...]
        grad = norm_back(up, normal, inv2[:, 0:1], row_of(vec, GAIN_2))
        sum_grad[...] = grad
        add_row(sums, 0, up * normal)
        add_row(sums, 1, up)
        add_row(sums, 2, grad)
        low = grad.astype(b16)

        accumulate(t, acc, slice(None), act[...], low)

    @pl.when(t == pl.num_programs(0) - 1)
    def _():
        deal(place, acc, outs)


def pre_back_kernel(lens, offs, tiles, place, sum_grad, slope, wdown, pre_low, sums):
    t = pl.program_id(0)
    width = sum_grad.shape[1]
    chunks = slope.shape[1] // width
    split = wdown.shape[0] // chunks

    @pl.when(t == 0)
    def _():
        sums[...] = jnp.zeros_like(sums)

    @pl.when(t < tiles[0])
    def _():
        low = sum_grad[...].astype(b16)
        for c in range(chunks):
            cols = slice(c * width, (c + 1) * width)
            pre = dot_nt(low, flat_of(wdown[c * split : (c + 1) * split])) * slope[:, cols].astype(f32)
            add_row(sums, c, pre)
            pre_low[:, cols] = pre.astype(b16)


def mid_back_kernel(
    lens, offs, tiles, place, sum_grad, pre_low, n1, inv1, ctx, wup, wout, vec, mid, ctx_grad, *refs
):
    *outs, sums, acc = refs
    t = pl.program_id(0)
    hidden = pre_low.shape[1]

    @pl.when(t == 0)
    def _():
        sums[...] = jnp.zeros_like(sums)

    @pl.when(t < tiles[0])
    def _():
        pre = pre_low[...]
        grad = sum_grad[...] + dot_nt(pre, flat_of(wup))
        normal = n1[...]
        add_row(sums, 0, grad * normal)
        add_row(sums, 1, grad)
        middle = norm_back(grad, normal, inv1[:, 0:1], row_of(vec, GAIN_1))
        add_row(sums, 2, middle)
        mid[...] = middle
        low = middle.astype(b16)
        ctx_grad[...] = dot_nt(low, flat_of(wout)).astype(b16)
        first_low = (normal * row_of(vec, GAIN_1) + row_of(vec, SHIFT_1)).astype(b16)
        accumulate(t, acc, slice(0, hidden), first_low, pre)
        accumulate(t, acc, slice(hidden, None), ctx[...], low)

    @pl.when(t == pl.num_programs(0) - 1)
    def _():
        deal(place, acc, outs)


def attend_back_kernel(lens, offs, tiles, place, qkv_h, probs_h, ctx_grad_h, grad, sums, qkv, probs, ctx_grad, sems):
    width = ctx_grad.shape[1]
    count, seq = probs.shape[0], probs.shape[2]
    pairs = ((qkv_h, qkv), (probs_h, probs), (ctx_grad_h, ctx_grad))
    copies = [pltpu.make_async_copy(a, b, sems.at[i]) for i, (a, b) in enumerate(pairs)]
    for copy in copies:
        copy.start()
    grad[...] = jnp.zeros_like(grad)
    sums[...] = jnp.zeros_like(sums)
    for copy in copies:
        copy.wait()

    def attend(b, size):
        rows, key_rows = sentence_rows(offs, b, seq), sentence_rows(offs, b, size)
        real = lax.broadcasted_iota(jnp.int32, (seq, 1), 0) < lens[b]
        def spread(x):
            return jnp.broadcast_to(jnp.sum(x, axis=0, keepdims=True), x.shape)

        for group in range(0, width // PAIR, GROUP):
            pairs = range(group, group + GROUP)
            cols = [slice(p * PAIR, (p + 1) * PAIR) for p in pairs]
            ups = [jnp.where(real, ctx_grad[rows, c], jnp.zeros((), b16)) for c in cols]
            queries = [qkv[rows, c] for c in cols]
            keys = [split_heads(qkv[key_rows, width + c.start : width + c.stop]) for c in cols]
            vals = [split_heads(qkv[key_rows, 2 * width + c.start : 2 * width + c.stop]) for c in cols]
            lows = [probs[b, p * 2 * size : (p + 1) * 2 * size, :] for p in pairs]
            prob_grads = [dot_nt(v, up) for v, up in zip(vals, ups)]
            val_grads = [join_heads(dot(low, up)).astype(b16) for low, up in zip(lows, ups)]
            scores = []
            for low, pg in zip(lows, prob_grads):
                pr = low.astype(f32)
                scores.append((pr * (pg - by_head(spread, pg * pr))).astype(b16))
            query_grads = [(dot_tn(s, k) * (HEAD_DIM ** -0.5)).astype(b16) for s, k in zip(scores, keys)]
            key_grads = [join_heads(dot(s, q)).astype(b16) for s, q in zip(scores, queries)]
            for i, c in enumerate(cols):
                grad[rows, c] = query_grads[i]
                grad[key_rows, width + c.start : width + c.stop] = key_grads[i]
                grad[key_rows, 2 * width + c.start : 2 * width + c.stop] = val_grads[i]

    by_length(lens, count, seq, attend)

    def total(t, _):
        for c in (0, 2):
            add_row(sums, c // 2, grad[tile_at(t), c * width : (c + 1) * width].astype(f32))
        return 0

    lax.fori_loop(0, tiles[0], total, 0)

def qkv_back_kernel(lens, offs, tiles, place, xs, grad, *refs):
    *outs, acc = refs
    t = pl.program_id(0)

    @pl.when(t < tiles[0])
    def _():
        accumulate(t, acc, slice(None), xs[...], grad[...])

    @pl.when(t == pl.num_programs(0) - 1)
    def _():
        deal(place, acc, outs)


def input_kernel(lens, offs, tiles, place, grad, mid, wqkv, gx, buf):
    count, seq, width = gx.shape
    t = pl.program_id(0)

    @pl.when(t == 0)
    def _():
        gx[...] = jnp.zeros_like(gx)

    @pl.when(t < tiles[0])
    def _():
        buf[tile_at(t), :] = dot_nt(grad[...], flat_of(wqkv)) + mid[...]

    @pl.when(t == pl.num_programs(0) - 1)
    def _():
        def unpack(b, _):
            def block(i, _):
                at = pl.multiple_of(offs[b] + i * PACK, PACK)
                gx[b, pl.ds(pl.multiple_of(i * PACK, PACK), PACK), :] = buf[pl.ds(at, PACK), :]
                return 0

            return lax.fori_loop(0, (lens[b] + PACK - 1) // PACK, block, 0)

        lax.fori_loop(0, count, unpack, 0)


def small_kernel(spot, sums, *outs):
    width = sums.shape[1] // 4
    *plain, ups, head, classes = outs
    mine = plain[0].shape[1]

    def share(x, size):
        return pltpu.roll(x, lax.rem(x.shape[1] - spot[0] * size, x.shape[1]), axis=1)[:, 0:size]

    blocks = [share(sums[0:8, p * width : (p + 1) * width], mine) for p in (0, 2, 3)]
    for out, (block, row) in zip(plain, ((2, 0), (2, 1), (1, 2), (1, 0), (1, 1), (0, 2), (0, 0), (0, 1))):
        out[...] = blocks[block][row : row + 1]
    flat = jnp.concatenate([sums[r : r + 1, width : 2 * width] for r in range(4)], 1)
    ups[...] = share(jnp.broadcast_to(flat, (8, 4 * width)), 4 * mine)[0:1]
    head[...] = jnp.transpose(share(sums[8:16, 0 : 3 * width], 3 * mine))[:, 0:NCLASS]
    classes[...] = jnp.transpose(sums[8:16, 0:128])[0:1, NCLASS : 2 * NCLASS]


class Tiled:
    def __init__(self, array):
        self.array = array


class Flat:
    def __init__(self, array):
        self.array = array


class Scalars:
    def __init__(self, array):
        self.array = array


def spec_of(x):
    if isinstance(x, Scalars):
        return pl.BlockSpec(memory_space=pltpu.SMEM)
    if isinstance(x, Flat):
        return pl.BlockSpec(memory_space=pl.ANY)
    if isinstance(x, Tiled):
        return pl.BlockSpec((TILE, x.array.shape[1]), lambda i, lens, offs, tiles, place: (jnp.minimum(i, tiles[0] - 1), 0))
    return pl.BlockSpec(x.shape, lambda *_: (0,) * len(x.shape), pipeline_mode=pl.Buffered(1))


def bare(x):
    return x.array if isinstance(x, (Tiled, Flat, Scalars)) else x


def shape(dtype, *dims):
    return jax.ShapeDtypeStruct(dims, dtype)


def call(kernel, meta, args, outs, scratch=(), steps=1, micros=0):
    moved = sum(bare(a).size * bare(a).dtype.itemsize for a in (*args, *outs))
    return pl.pallas_call(
        kernel,
        out_shape=[bare(o) for o in outs],
        grid_spec=pltpu.PrefetchScalarGridSpec(
            num_scalar_prefetch=len(meta),
            grid=(steps,),
            in_specs=[spec_of(a) for a in args],
            out_specs=[spec_of(o) for o in outs],
            scratch_shapes=list(scratch),
        ),
        cost_estimate=pl.CostEstimate(flops=int(micros * 1.15e9), transcendentals=0, bytes_accessed=moved),
        compiler_params=pltpu.CompilerParams(vmem_limit_bytes=58 << 20),
    )(*meta, *[bare(a) for a in args])


def pack_small(vectors):
    total = sum(v.shape[0] for v in vectors)
    rows = -(-total // (8 * CHUNK)) * 8
    at, flat = 0, 0.0
    for v in vectors:
        flat = flat + jnp.pad(v.astype(f32), (at, rows * CHUNK - at - v.shape[0]))
        at += v.shape[0]
    return flat.astype(b16).reshape(rows, CHUNK)


def body(
    embeddings, lengths, labels, qkv_weight, query_bias, value_bias, out_weight, out_bias, attn_gain,
    attn_shift, up_weight, up_bias, down_weight, down_bias, ffn_gain, ffn_shift, head_weight, head_bias,
):
    width = embeddings.shape[-1]
    seq_len = embeddings.shape[2]
    count = embeddings.shape[1]
    rows = -(-count * seq_len // TILE) * TILE
    hidden = up_weight.shape[1]
    groups = lax.axis_size("dp")
    low, far, near = places()
    tower = lax.axis_index("tower")
    shard_rows = qkv_weight.shape[0]
    quick = low == 4 and shard_rows % PACK == 0

    sent_len = lengths[0]
    taken = (sent_len + PACK - 1) // PACK * PACK
    before = jnp.arange(count)[None, :] < jnp.arange(count)[:, None]
    offs = jnp.sum(jnp.where(before, taken[None, :], 0), axis=1)
    tiles = (jnp.sum(taken)[None] + TILE - 1) // TILE
    place = jnp.stack([tower, near, far]).astype(jnp.int32)
    meta = (sent_len, offs, tiles, place)
    steps = rows // TILE

    packed = pack_small((
        query_bias, value_bias, out_bias, attn_gain, attn_shift, down_bias, ffn_gain, ffn_shift, up_bias,
        head_weight.reshape(-1),
    ))
    weights = (qkv_weight, out_weight, up_weight, down_weight)
    if quick:
        sizes = [w.size // 2 // CHUNK for w in weights]
        first_part, up_part, down_part = call(
            parts_kernel, (place,), (*weights, packed),
            (
                shape(b16, sizes[0] + sizes[1] + packed.shape[0], CHUNK), shape(b16, sizes[2], CHUNK),
                shape(b16, sizes[3], CHUNK),
            ),
        )
    else:
        first_part = jnp.concatenate([to_chunks(qkv_weight), to_chunks(out_weight), packed], 0)
        up_part, down_part = to_chunks(up_weight), to_chunks(down_weight)
    cut = first_part.shape[0] - packed.shape[0]
    low_far = far_pieces(first_part)
    block_first = in_order(low_far, far, 0)
    far_up = far_pieces(after(up_part, *low_far))
    full = [(FAR, w.shape[0] * low, w.shape[1]) for w in weights]
    if quick:
        near_first = gather_near(block_first)
        far_up = after(far_up, *near_first[3:])
        block_up = in_order(far_up, far, 0)
        far_down = far_pieces(after(down_part, *far_up))
        pieces_first = near_first + [swap(p, "tower", 1) for p in near_first]
        tails = [p[:, cut:] for p in near_first]
        packs = in_order(tails[:3] + [jnp.concatenate(tails[3:], 0)], near, 1)
    else:
        block_up = in_order(far_up, far, 0)
        far_down = far_pieces(down_part)
        whole_first = gather_any(block_first)
        n_qkv = qkv_weight.shape[1] // 2 // CHUNK * shard_rows
        pieces_first = [
            from_chunks(whole_first[:, :, :n_qkv], shard_rows), from_chunks(whole_first[:, :, n_qkv:cut], shard_rows)
        ]
        packs = whole_first[:, :, cut:]
    packs = packs.reshape(groups, -1).astype(f32)
    cuts = [8 * shard_rows, 8 * shard_rows + up_bias.shape[0]]
    cuts.append(cuts[1] + head_weight.size)
    vec = packs[:, : cuts[0]].reshape(groups, 8, shard_rows).transpose(1, 0, 2).reshape(8, width)
    ups = packs[:, cuts[0] : cuts[1]].reshape(-1, width)
    head_rows = packs[:, cuts[1] : cuts[2]].reshape(-1, NCLASS).T

    ext = rows + seq_len
    dense = 2 * rows * width
    sinks = [
        Flat(shape(b16, ext, width)), Flat(shape(b16, ext, 3 * width)),
        Flat(shape(b16, count, HEADS * seq_len, seq_len)), Flat(shape(b16, ext, width)), Flat(shape(f32, rows, width)),
        Flat(shape(f32, rows, 128)),
    ]
    both = [Flat(shape(b16, *full[0])), Flat(shape(b16, *full[1]))]
    if quick:
        pieces_first = after(pieces_first, block_up)
        proj_qkv, proj_out, xs, qkv, probs, ctx, n1, inv1 = call(
            partial(attend_kernel, 10), meta, (embeddings[0], vec, *map(Flat, pieces_first)), both + sinks,
            [pltpu.VMEM(o.array.shape, o.array.dtype) for o in both + sinks]
            + [pltpu.SemaphoreType.DMA((40,)), pltpu.SemaphoreType.DMA((8,))],
            micros=20,
        )
    else:
        proj_qkv, proj_out = pieces_first
        xs, qkv, probs, ctx, n1, inv1 = call(
            partial(attend_kernel, 0), meta, (embeddings[0], vec, proj_qkv, proj_out), sinks,
            [pltpu.VMEM(o.array.shape, o.array.dtype) for o in sinks] + [pltpu.SemaphoreType.DMA((8,))],
            micros=20,
        )

    wide, slim = shape(b16, rows, hidden), shape(f32, rows, width)
    if quick:
        near_up = gather_near(block_up, n1)
        pieces_up = near_up + [swap(p, "tower", 1) for p in near_up]
        proj_up, act, slope = call(
            partial(up_kernel, 10), meta, (Tiled(n1), vec, ups, *map(Flat, pieces_up)),
            [Flat(shape(b16, *full[2])), Tiled(wide), Tiled(wide)],
            [pltpu.VMEM(full[2], b16), pltpu.SemaphoreType.DMA((40,)), pltpu.SemaphoreType.DMA((1,))],
            steps=steps, micros=12,
        )
    else:
        proj_up = from_chunks(gather_any(block_up), shard_rows)
        act, slope = call(
            partial(up_kernel, 0), meta, (Tiled(n1), vec, ups, proj_up), [Tiled(wide), Tiled(wide)], steps=steps,
            micros=12,
        )
    outs = [Tiled(slim), Tiled(shape(f32, rows, 128)), shape(f32, count, width)]
    if quick:
        block_down = in_order(after(far_down, n1), far, 0)
        near_down = gather_near(block_down, act)
        pieces_down = near_down + [swap(p, "tower", 1) for p in near_down]
        proj_down, n2, inv2, pooled = call(
            partial(down_kernel, 10), meta, (Tiled(n1), Tiled(act), vec, *map(Flat, pieces_down)),
            [Flat(shape(b16, *full[3]))] + outs,
            [pltpu.VMEM(full[3], b16), pltpu.SemaphoreType.DMA((10,)), pltpu.SemaphoreType.DMA((1,))],
            steps=steps, micros=10,
        )
    else:
        proj_down = from_chunks(gather_any(in_order(far_down, far, 0)), down_weight.shape[0])
        n2, inv2, pooled = call(
            partial(down_kernel, 0), meta, (Tiled(n1), Tiled(act), vec, proj_down), outs, steps=steps, micros=10,
        )

    def dealt(full_rows, cols):
        if quick:
            block = FAR, full_rows // (8 * FAR), cols
            return [shape(b16, 4, *block), shape(b16, *block), shape(b16, 3, *block)]
        return [shape(b16, full_rows, cols)]

    partner = swap(pooled, "tower", 1)
    sums_of = shape(f32, 8, width)
    sum_grad, *down_parts, sums_two, tops = call(
        down_back_kernel, meta,
        (
            Scalars(labels), Scalars(head_bias.astype(f32)), pooled, partner, head_rows, Tiled(act), Tiled(n2),
            Tiled(inv2), vec,
        ),
        [Tiled(slim)] + dealt(hidden, width) + [sums_of, shape(f32, 8, hidden)],
        [pltpu.VMEM((hidden, width), f32), pltpu.VMEM((count, width), f32)], steps=steps, micros=11,
    )
    if quick:
        down = Scatter(down_parts)
        sum_grad = after(sum_grad, down.first)
    pre_low, sums_up = call(
        pre_back_kernel, meta, (Tiled(sum_grad), Tiled(slope), proj_down), [Tiled(wide), sums_of], steps=steps,
        micros=8,
    )
    if quick:
        pre_low = after(pre_low, down.corners(), down.rest)
    mid, ctx_grad, *up_parts, sums_one = call(
        mid_back_kernel, meta,
        (Tiled(sum_grad), Tiled(pre_low), Tiled(n1), Tiled(inv1), Tiled(ctx), proj_up, proj_out, vec),
        [Tiled(slim), Tiled(shape(b16, ext, width))] + dealt(width, hidden + width) + [sums_of],
        [pltpu.VMEM((width, hidden + width), f32)], steps=steps, micros=20,
    )
    if quick:
        up = Scatter(after(up_parts, down.sides()))
        ctx_grad = after(ctx_grad, up.first, up.rest)
    qkv_grad, sums_in = call(
        attend_back_kernel, meta, (Flat(qkv), Flat(probs), Flat(ctx_grad)), [shape(b16, ext, 3 * width), sums_of],
        [
            pltpu.VMEM(qkv.shape, b16), pltpu.VMEM(probs.shape, b16), pltpu.VMEM(ctx_grad.shape, b16),
            pltpu.SemaphoreType.DMA((3,)),
        ],
        micros=14,
    )
    if quick:
        up.sides()
        down.far = after(down.fars(), qkv_grad)
        xs = after(xs, qkv_grad, *up.corner, *up.sent, *down.far)
    last_parts = call(
        qkv_back_kernel, meta, (Tiled(xs), Tiled(qkv_grad)), dealt(width, 3 * width),
        [pltpu.VMEM((width, 3 * width), f32)], steps=steps, micros=8,
    )
    summed = jnp.concatenate([jnp.concatenate([sums_two, sums_up, sums_one, sums_in], 1), tops], 0)
    summed = add_from(after(summed, *last_parts), "tower", 1)
    if quick:
        last = Scatter(last_parts)
        mid = after(mid, last.first, summed)
    came = swap(summed, "dp", low)
    (grad_in,) = call(
        input_kernel, meta, (Tiled(qkv_grad), Tiled(mid), proj_qkv), [shape(f32, count, seq_len, width)],
        [pltpu.VMEM((rows, width), f32)], steps=steps, micros=8,
    )
    if quick:
        last.corner = after(last.corners(), grad_in)
        last.sides()
        up.side = after(up.sides(), grad_in, *last.sent)
        came = after(came, grad_in, *last.sent)
        down_out, up_out, last_out = down.sum(), up.sum(), last.sum()
    else:
        down_out, up_out, last_out = (scatter_any(*p) for p in (down_parts, up_parts, last_parts))

    summed, bit = add_from(summed + came, "dp", 2 * low), 1
    while bit < low:
        summed = add_from(summed, "dp", bit)
        bit *= 2
    spot = (tower * groups + lax.axis_index("dp")).astype(jnp.int32)[None]
    mine = width // (2 * groups)
    *plain, up_bias_sum, head_sum, class_sum = pl.pallas_call(
        small_kernel,
        out_shape=[shape(f32, 1, mine)] * 8
        + [shape(f32, 1, 4 * mine), shape(f32, 3 * mine, NCLASS), shape(f32, 1, NCLASS)],
        in_specs=[pl.BlockSpec(memory_space=pltpu.SMEM), pl.BlockSpec(memory_space=pltpu.VMEM)],
        out_specs=[pl.BlockSpec(memory_space=pltpu.VMEM)] * 11,
    )(spot, summed)
    q_sum, v_sum, o_sum, gain_one, shift_one, d_sum, gain_two, shift_two = [x.reshape(-1) for x in plain]
    return (
        pooled[None],
        grad_in[None],
        last_out,
        q_sum, v_sum,
        up_out[:, hidden:],
        o_sum, gain_one, shift_one,
        up_out[:, :hidden],
        up_bias_sum.reshape(-1),
        down_out,
        d_sum, gain_two, shift_two,
        head_sum,
        class_sum.reshape(-1),
    )


def solution(mesh):
    rows, vec = P("dp", None), P("dp")
    out_rows, out_vec = P(("tower", "dp"), None), P(("tower", "dp"))
    return jax.shard_map(
        body,
        mesh=mesh,
        in_specs=(
            P("tower", "dp", None, None), P("tower", "dp"), vec,
            rows, vec, vec, rows, vec, vec, vec, rows, vec, rows, vec, vec, vec, rows, P(),
        ),
        out_specs=(
            P("tower", "dp", None), P("tower", "dp", None, None),
            out_rows, out_vec, out_vec, out_rows, out_vec, out_vec, out_vec, out_rows, out_vec, out_rows, out_vec,
            out_vec, out_vec, out_rows, P(),
        ),
        check_vma=False,
    )
```

```python
from functools import partial
import math

import jax
import jax.numpy as jnp
from jax import lax
from jax.experimental import pallas as pl
from jax.experimental.pallas import tpu as pltpu
from jax.sharding import PartitionSpec as P

HEADS = 12
HEAD_DIM = 64
NCLASS = 3
CHUNK = 384
FAR = 4

eps_norm = 1e-12
gap_soft = 0.01
f32 = jnp.float32
b16 = jnp.bfloat16


def swap(x, axis, k):
    return lax.ppermute(x, axis, [(i, i ^ k) for i in range(lax.axis_size(axis))])


def places():
    low = lax.axis_size("dp") // FAR
    me = lax.axis_index("dp")
    return low, me // low, me % low


def in_order(pieces, me, axis):
    stack = jnp.stack(pieces, axis)
    return jnp.concatenate(
        [lax.dynamic_index_in_dim(stack, me ^ j, axis) for j in range(len(pieces))], axis
    )


def far_pieces(part):
    low, _, _ = places()
    return [part] + [swap(part, "dp", j * low) for j in range(1, FAR)]


def after(x, *deps):
    return lax.optimization_barrier((x, *deps))[0]


def gather_near(block, *ready):
    half = FAR // 2
    by_one, by_two = after((swap(block, "dp", 1), swap(block, "dp", 2)), *ready)
    return [block, by_one, by_two, swap(by_one[:half], "dp", 2), swap(by_two[half:], "dp", 1)]


def gather_any(block):
    low, _, near = places()
    pieces, bit = [block], 1
    while bit < low:
        pieces = pieces + [swap(p, "dp", bit) for p in pieces]
        bit *= 2
    return in_order(pieces, near, 1)


def to_chunks(shard):
    rows, cols = shard.shape
    half = cols // 2
    mine = lax.dynamic_slice_in_dim(shard, lax.axis_index("tower") * half, half, 1)
    return mine.reshape(rows, half // CHUNK, CHUNK).transpose(1, 0, 2).reshape(-1, CHUNK)


def from_chunks(mine, rows):
    other = swap(mine, "tower", 1)
    low_half = lax.axis_index("tower") == 0
    both = jnp.stack([jnp.where(low_half, mine, other), jnp.where(low_half, other, mine)])
    far, low, total = mine.shape[:3]
    n = total // rows
    both = both.reshape(2, far, low, n, rows, CHUNK).transpose(1, 2, 4, 0, 3, 5)
    return both.reshape(far, low * rows, 2 * n * CHUNK)


def add_low(a, b):
    return (a.astype(f32) + b.astype(f32)).astype(b16)


class Scatter:
    def __init__(self, parts):
        self.mine, *others = parts
        self.first = swap(others[0], "tower", 1)
        self.rest = swap(after(others[1], self.first), "tower", 1)
        self.corner = self.side = self.far = None

    def both(self, k, part=slice(None)):
        got = self.first[part] if k == 3 else self.rest[k, part]
        return self.mine[k, part].astype(f32) + got.astype(f32)

    def corners(self):
        if self.corner is None:
            half = FAR // 2
            self.corner = (
                swap(self.both(3, slice(0, half)).astype(b16), "dp", 1),
                swap(self.both(3, slice(half, FAR)).astype(b16), "dp", 2),
            )
        return self.corner

    def sides(self):
        if self.side is None:
            half = FAR // 2
            for_one, for_two = (x.astype(f32) for x in self.corners())
            none = ((0, 0), (0, 0))
            one = self.both(1) + jnp.pad(for_two, ((half, 0), *none))
            two = self.both(2) + jnp.pad(for_one, ((0, half), *none))
            self.sent = one.astype(b16), two.astype(b16)
            self.side = swap(self.sent[0], "dp", 1), swap(self.sent[1], "dp", 2)
        return self.side

    def fars(self):
        if self.far is None:
            low = lax.axis_size("dp") // FAR
            one, two = self.sides()
            self.own = [self.both(0, j) + one[j].astype(f32) + two[j].astype(f32) for j in range(FAR)]
            self.far = [swap(self.own[j].astype(b16), "dp", j * low) for j in range(1, FAR)]
        return self.far

    def sum(self):
        far = self.fars()
        return self.own[0] + far[0].astype(f32) + far[1].astype(f32) + far[2].astype(f32)


def scatter_any(grad):
    low, far, near = places()
    tower = lax.axis_index("tower")
    halves = grad.reshape((2, FAR, low, -1) + grad.shape[1:])
    got = swap(lax.dynamic_index_in_dim(halves, 1 - tower, 0, keepdims=False), "tower", 1)
    data = add_low(lax.dynamic_index_in_dim(halves, tower, 0, keepdims=False), got)
    blocks = [lax.dynamic_index_in_dim(data, near ^ k, 1, keepdims=False) for k in range(low)]
    bit = low // 2
    while bit:
        blocks = [add_low(blocks[k], swap(blocks[k + bit], "dp", bit)) for k in range(bit)]
        bit //= 2
    own = [lax.dynamic_index_in_dim(blocks[0], far ^ j, 0, keepdims=False) for j in range(FAR)]
    total = own[0].astype(f32)
    for j in range(1, FAR):
        total = total + swap(own[j], "dp", j * low).astype(f32)
    return total


def add_from(x, axis, k):
    return x + swap(x, axis, k)


TILE = 256
PACK = 16
PAIR = 2 * HEAD_DIM
GROUP = 3
Q_BIAS, V_BIAS, O_BIAS, GAIN_1, SHIFT_1, D_BIAS, GAIN_2, SHIFT_2 = range(8)


def dot(a, b):
    return jnp.dot(a, b, preferred_element_type=f32)


def dot_nt(a, b):
    return lax.dot_general(a, b, (((1,), (1,)), ((), ())), preferred_element_type=f32)


def dot_tn(a, b):
    return lax.dot_general(a, b, (((0,), (0,)), ((), ())), preferred_element_type=f32)


def tile_at(t):
    return pl.ds(pl.multiple_of(t * TILE, TILE), TILE)


def sentence_rows(offs, b, seq):
    return pl.ds(pl.multiple_of(offs[b], PACK), seq)


def split_heads(x):
    left = lax.broadcasted_iota(jnp.int32, x.shape, 1) < HEAD_DIM
    zero = jnp.zeros_like(x)
    return jnp.concatenate([jnp.where(left, x, zero), jnp.where(left, zero, x)], 0)


def join_heads(x):
    seq = x.shape[0] // 2
    left = lax.broadcasted_iota(jnp.int32, (seq, PAIR), 1) < HEAD_DIM
    return jnp.where(left, x[:seq], x[seq:])


def by_head(fn, x):
    half = x.shape[0] // 2
    return jnp.concatenate([fn(x[:half]), fn(x[half:])], 0)


def by_length(lens, count, seq, step):
    def one(b, _):
        @pl.when(lens[b] > seq // 2)
        def _():
            step(b, seq)

        @pl.when(lens[b] <= seq // 2)
        def _():
            step(b, seq // 2)

        return 0

    lax.fori_loop(0, count, one, 0)


def norm_rows(hidden):
    center = hidden - jnp.mean(hidden, axis=-1, keepdims=True)
    inverse = lax.rsqrt(jnp.mean(center * center, axis=-1, keepdims=True) + eps_norm)
    return center * inverse, inverse


def norm_back(upstream, normal, inverse, gain):
    scaled = upstream * gain
    inner = scaled - jnp.mean(scaled, axis=-1, keepdims=True)
    return inverse * (inner - normal * jnp.mean(scaled * normal, axis=-1, keepdims=True))


def row_of(vec, i):
    return vec[i : i + 1, :].astype(f32)


def add_row(sums, i, x):
    sums[i : i + 1, :] += jnp.sum(x, axis=0, keepdims=True)


def parts_kernel(place, wqkv, wout, wup, wdown, packed, first, second, third):
    def put(src, dst, at):
        rows, half = src.shape[0], src.shape[1] // 2
        for c in range(half // CHUNK):
            dst[at : at + rows, :] = src[:, pl.ds(pl.multiple_of(place[0] * half + c * CHUNK, 128), CHUNK)]
            at += rows
        return at

    first[put(wqkv, first, 0) :, :] = packed[...]
    put(wup, second, put(wout, second, 0))
    put(wdown, third, 0)


def fetch(place, pieces, targets, sems):
    copies = []
    for side in range(2):
        tower = place[0] if side == 0 else 1 - place[0]
        block, by_one, by_two, low, high = pieces[5 * side : 5 * side + 5]
        half = FAR // 2
        spots = ((block, 0, 0, FAR), (by_one, 1, 0, FAR), (by_two, 2, 0, FAR), (low, 3, 0, half), (high, 3, half, half))
        for piece, k, far, size in spots:
            at = 0
            for weight, rows in targets:
                cols = weight.shape[2] // 2
                for c in range(cols // CHUNK):
                    row = pl.multiple_of((place[1] ^ k) * rows, PACK)
                    col = pl.multiple_of(tower * cols + c * CHUNK, 128)
                    copies.append(
                        pltpu.make_async_copy(
                            piece.at[:, pl.ds(at, rows), :],
                            weight.at[pl.ds(far, size), pl.ds(row, rows), pl.ds(col, CHUNK)],
                            sems.at[len(copies)],
                        )
                    )
                    at += rows
    for copy in copies:
        copy.start()
    return copies


def deal(place, acc, outs, base=0):
    cols = acc.shape[1]
    if len(outs) == 1:
        outs[0][:, base : base + cols] = acc[...].astype(b16)
        return
    mine, first, rest = outs
    rows = first.shape[1]
    for own in (False, True):
        side = place[0] if own else 1 - place[0]
        for k in range(4):
            target = mine.at[k] if own else first if k == 3 else rest.at[k]
            for j in range(FAR):
                at = (side * 4 * FAR + (place[2] ^ j) * 4 + (place[1] ^ k)) * rows
                target[j, :, base : base + cols] = acc[pl.ds(pl.multiple_of(at, 8), rows), :].astype(b16)


def flat_of(weight, cols=slice(None)):
    block = weight[:, :, cols]
    return block.reshape(block.shape[0] * block.shape[1], block.shape[2])


def attend_kernel(n_pieces, lens, offs, tiles, place, homes, x_ref, y_ref, vec, *refs):
    pieces, refs = refs[:n_pieces], refs[n_pieces:]
    if n_pieces:
        sinks, refs = refs[:5], refs[5:]
        wqkv, xs, qkv, probs, ctx, got, sent = refs
        copies = fetch(place, pieces, ((wqkv, wqkv.shape[1] // 4),), got)
    else:
        wqkv = refs[0]
        sinks, refs = refs[1:5], refs[5:]
        xs, qkv, probs, ctx, sent = refs
        copies = []
    held = (wqkv, xs, qkv, probs, ctx)[5 - len(sinks) :]
    count, seq, width = x_ref.shape
    leaving = []

    def leave(*which):
        for ref in which:
            for i, own in enumerate(held):
                if own is ref:
                    copy = pltpu.make_async_copy(ref, sinks[i], sent.at[i])
                    copy.start()
                    leaving.append(copy)

    xs[...] = jnp.zeros_like(xs)
    ctx[...] = jnp.zeros_like(ctx)

    def pack(b, _):
        blocks = (lens[b] + PACK - 1) // PACK
        for side, source in enumerate((x_ref, y_ref)):

            def block(i, _):
                at = pl.multiple_of(offs[b] + i * PACK, PACK)
                xs[pl.ds(at, PACK), :] = source[homes[count + b], pl.ds(pl.multiple_of(i * PACK, PACK), PACK), :]
                return 0

            lax.fori_loop(0, jnp.where(homes[b] == side, blocks, 0), block, 0)
        return 0

    lax.fori_loop(0, count, pack, 0)
    for copy in copies:
        copy.wait()
    leave(wqkv, xs)

    def project(t, _):
        x = xs[tile_at(t), :]
        for c in range(3):
            cols = slice(c * width, (c + 1) * width)
            joined = dot(x, flat_of(wqkv, cols))
            if c == 0:
                joined = (joined + row_of(vec, Q_BIAS)) * (HEAD_DIM ** -0.5)
            if c == 2:
                joined = joined + row_of(vec, V_BIAS)
            qkv[tile_at(t), cols] = joined.astype(b16)
        return 0

    lax.fori_loop(0, tiles[0], project, 0)
    qkv[pl.ds(pl.multiple_of(tiles[0] * TILE, TILE), seq), :] = jnp.zeros((seq, 3 * width), b16)
    leave(qkv)

    def attend(b, size):
        rows, key_rows = sentence_rows(offs, b, seq), sentence_rows(offs, b, size)
        valid = lax.broadcasted_iota(jnp.int32, (size, seq), 0) < lens[b]

        def softmax(s):
            s = jnp.where(valid, s, -1000000000.0)
            e = jnp.exp(s - jnp.max(s, axis=0, keepdims=True))
            return (e * (1.0 / jnp.sum(e, axis=0, keepdims=True))).astype(b16)

        for group in range(0, width // PAIR, GROUP):
            pairs = range(group, group + GROUP)
            cols = [slice(p * PAIR, (p + 1) * PAIR) for p in pairs]
            queries = [qkv[rows, c] for c in cols]
            keys = [split_heads(qkv[key_rows, width + c.start : width + c.stop]) for c in cols]
            vals = [split_heads(qkv[key_rows, 2 * width + c.start : 2 * width + c.stop]) for c in cols]
            scores = [dot_nt(k, q) for k, q in zip(keys, queries)]
            lows = [by_head(softmax, s) for s in scores]
            outs = [dot_tn(low, v).astype(b16) for low, v in zip(lows, vals)]
            for p, c, low, out in zip(pairs, cols, lows, outs):
                probs[b, p * 2 * size : (p + 1) * 2 * size, :] = low
                ctx[rows, c] = out

    by_length(lens, count, seq, attend)
    leave(probs, ctx)

    for copy in leaving:
        copy.wait()


def inside(offs, lens, b, t):
    row = t * TILE + lax.broadcasted_iota(jnp.int32, (TILE, 1), 0)
    return (row >= offs[b]) & (row < offs[b] + lens[b])


def take_weights(step, place, pieces, refs, count, rows):
    if not pieces:
        return refs[:count], refs[count:], lambda: None
    sinks, refs = refs[:count], refs[count:]
    held, got, sent, refs = refs[-count - 2 : -2], refs[-2], refs[-1], refs[: -count - 2]
    leave = [pltpu.make_async_copy(a, b, sent.at[i]) for i, (a, b) in enumerate(zip(held, sinks))]

    @pl.when(step == 0)
    def _():
        for copy in fetch(place, pieces, [(weight, rows) for weight in held], got):
            copy.wait()
        for copy in leave:
            copy.start()

    def finish():
        @pl.when(step == pl.num_programs(0) - 1)
        def _():
            for copy in leave:
                copy.wait()

    return held, refs, finish


def up_kernel(n_pieces, rows, lens, offs, tiles, place, ctx, xs, vec, ups, *refs):
    t = pl.program_id(0)
    pieces, refs = refs[:n_pieces], refs[n_pieces:]
    (wout, wup), (act, slope, n1, inv1), finish = take_weights(t, place, pieces, refs, 2, rows)
    width = n1.shape[1]

    @pl.when(t < tiles[0])
    def _():
        attended = dot(ctx[...], flat_of(wout)) + row_of(vec, O_BIAS)
        normal, inverse = norm_rows(xs[...].astype(f32) + attended)
        n1[...] = normal
        inv1[...] = jnp.broadcast_to(inverse, (TILE, 128))
        low = (normal * row_of(vec, GAIN_1) + row_of(vec, SHIFT_1)).astype(b16)
        for c in range(ups.shape[0]):
            cols = slice(c * width, (c + 1) * width)
            pre = dot(low, flat_of(wup, cols)) + row_of(ups, c)
            half = 0.5 * (1.0 + lax.erf(pre * (0.5 ** 0.5)))
            act[:, cols] = (pre * half).astype(b16)
            slope[:, cols] = (half + pre * (jnp.exp(-0.5 * pre * pre) * 0.3989422804014327)).astype(b16)

    finish()


def down_kernel(n_pieces, rows, lens, offs, tiles, place, n1, act, vec, *refs):
    t = pl.program_id(0)
    pieces, refs = refs[:n_pieces], refs[n_pieces:]
    (wdown,), (n2, inv2, pooled), finish = take_weights(t, place, pieces, refs, 1, rows)
    width = n1.shape[1]
    count = pooled.shape[0]

    @pl.when(t == 0)
    def _():
        pooled[...] = jnp.zeros_like(pooled)

    @pl.when(t < tiles[0])
    def _():
        total = n1[...] * row_of(vec, GAIN_1) + row_of(vec, SHIFT_1) + row_of(vec, D_BIAS)
        total = total + dot(act[...], flat_of(wdown))
        normal, inverse = norm_rows(total)
        n2[...] = normal
        inv2[...] = jnp.broadcast_to(inverse, (TILE, 128))
        for b in range(count):
            add_row(pooled, b, jnp.where(inside(offs, lens, b, t), normal, 0.0))

    @pl.when(t == pl.num_programs(0) - 1)
    def _():
        for b in range(count):
            size = jnp.full((1, width), lens[b], jnp.int32).astype(f32)
            pooled[b : b + 1, :] = pooled[b : b + 1, :] / size * row_of(vec, GAIN_2) + row_of(vec, SHIFT_2)

    finish()


def accumulate(t, acc, cols, left, right):
    @pl.when(t == 0)
    def _():
        acc[:, cols] = dot_tn(left, right)

    @pl.when(t > 0)
    def _():
        acc[:, cols] += dot_tn(left, right)


def pair_head(lens, place, homes, labels, bias, pooled, partner, head, tops, own, ends):
    count, width = pooled.shape

    for side in range(2):
        for i in range(count):
            at = side * count + i
            away, slot = homes[2 * count + at], homes[4 * count + at]
            row = jnp.where(away == 0, pooled[pl.ds(slot, 1), :], partner[pl.ds(slot, 1), :])
            ends[side, i : i + 1, :] = row
    left, right = ends[0], ends[1]
    own[...] = jnp.where(place[0] == 0, left, right)
    gap = left - right
    soft = jnp.sqrt(gap * gap + gap_soft)
    feats = (left, right, soft)
    row = lax.broadcasted_iota(jnp.int32, (count, 1), 0)
    label = jnp.zeros((count, 1), jnp.int32)
    for b in range(count):
        label = jnp.where(row == b, labels[b], label)
    logits = []
    for c in range(NCLASS):
        terms = [
            jnp.sum(feats[i] * head[c : c + 1, i * width : (i + 1) * width], axis=-1, keepdims=True) for i in range(3)
        ]
        logits.append(terms[0] + terms[1] + terms[2] + bias[c])
    top = jnp.maximum(jnp.maximum(logits[0], logits[1]), logits[2])
    exps = [jnp.exp(x - top) for x in logits]
    norm = exps[0] + exps[1] + exps[2]
    grads = [exps[c] / norm - jnp.where(label == c, 1.0, 0.0) for c in range(NCLASS)]
    back = []
    tops[...] = jnp.zeros_like(tops)
    for i in range(3):
        cols = slice(i * width, (i + 1) * width)
        back.append(sum(grads[c] * head[c : c + 1, cols] for c in range(NCLASS)))
        for c in range(NCLASS):
            tops[c : c + 1, cols] = 0.5 * jnp.sum(grads[c] * feats[i], axis=0, keepdims=True)
    for c in range(NCLASS):
        tops[NCLASS + c : NCLASS + c + 1, 0:128] = jnp.broadcast_to(0.5 * jnp.sum(grads[c], axis=0, keepdims=True), (1, 128))
    slope = gap / soft
    ends[0] = back[0] + slope * back[2]
    ends[1] = back[1] - slope * back[2]
    for b in range(count):
        side = jnp.where(homes[b] == 0, place[0], 1 - place[0])
        row = ends[side, pl.ds(homes[count + b], 1), :]
        size = jnp.full((1, width), lens[b], jnp.int32).astype(f32)
        ends[2, b : b + 1, :] = row / size


def down_back_kernel(
    lens, offs, tiles, place, homes, labels, bias, pooled, partner, head, act, n2, inv2, vec, sum_grad, *refs
):
    *outs, sums, tops, own, acc, ends = refs
    t = pl.program_id(0)
    count, width = pooled.shape

    @pl.when(t == 0)
    def _():
        pair_head(lens, place, homes, labels, bias, pooled, partner, head, tops, own, ends)
        sums[...] = jnp.zeros_like(sums)

    @pl.when(t < tiles[0])
    def _():
        up = jnp.zeros((TILE, width), f32)
        for b in range(count):
            up = jnp.where(inside(offs, lens, b, t), ends[2, b : b + 1, :], up)
        normal = n2[...]
        grad = norm_back(up, normal, inv2[:, 0:1], row_of(vec, GAIN_2))
        sum_grad[...] = grad
        add_row(sums, 0, up * normal)
        add_row(sums, 1, up)
        add_row(sums, 2, grad)
        low = grad.astype(b16)

        accumulate(t, acc, slice(None), act[...], low)

    @pl.when(t == pl.num_programs(0) - 1)
    def _():
        deal(place, acc, outs)


def early(t, copies):
    @pl.when(t == 0)
    def _():
        for copy in copies:
            copy.start()

    def ready(i):
        @pl.when(t == 0)
        def _():
            copies[i].wait()

    return ready


def pre_back_kernel(lens, offs, tiles, place, sum_grad, slope, wdown, pre_low, sums):
    t = pl.program_id(0)
    width = sum_grad.shape[1]
    chunks = slope.shape[1] // width
    split = wdown.shape[0] // chunks

    @pl.when(t == 0)
    def _():
        sums[...] = jnp.zeros_like(sums)

    @pl.when(t < tiles[0])
    def _():
        low = sum_grad[...].astype(b16)
        for c in range(chunks):
            cols = slice(c * width, (c + 1) * width)
            pre = dot_nt(low, flat_of(wdown[c * split : (c + 1) * split])) * slope[:, cols].astype(f32)
            add_row(sums, c, pre)
            pre_low[:, cols] = pre.astype(b16)


def mid_back_kernel(
    lens, offs, tiles, place, sum_grad, pre_low, n1, inv1, ctx, wup, wout, vec, mid, ctx_grad, *refs
):
    *outs, sums, acc = refs
    t = pl.program_id(0)
    hidden = pre_low.shape[1]

    @pl.when(t == 0)
    def _():
        sums[...] = jnp.zeros_like(sums)

    @pl.when(t < tiles[0])
    def _():
        pre = pre_low[...]
        grad = sum_grad[...] + dot_nt(pre, flat_of(wup))
        normal = n1[...]
        add_row(sums, 0, grad * normal)
        add_row(sums, 1, grad)
        middle = norm_back(grad, normal, inv1[:, 0:1], row_of(vec, GAIN_1))
        add_row(sums, 2, middle)
        mid[...] = middle
        low = middle.astype(b16)
        ctx_grad[...] = dot_nt(low, flat_of(wout)).astype(b16)
        first_low = (normal * row_of(vec, GAIN_1) + row_of(vec, SHIFT_1)).astype(b16)
        accumulate(t, acc, slice(0, hidden), first_low, pre)
        accumulate(t, acc, slice(hidden, None), ctx[...], low)

    @pl.when(t == pl.num_programs(0) - 1)
    def _():
        deal(place, acc, outs)


def attend_back_kernel(lens, offs, tiles, place, qkv_h, probs_h, ctx_grad_h, grad, sums, qkv, probs, ctx_grad, sems):
    width = ctx_grad.shape[1]
    count, seq = probs.shape[0], probs.shape[2]
    blocks = qkv.shape[0] // seq

    def rows_in_use(do):
        for i in range(blocks):

            @pl.when(i * seq < tiles[0] * TILE + seq)
            def _():
                at = pl.ds(i * seq, seq)
                do(pltpu.make_async_copy(qkv_h.at[at], qkv.at[at], sems.at[i]))
                do(pltpu.make_async_copy(ctx_grad_h.at[at], ctx_grad.at[at], sems.at[blocks + i]))

    def probs_of(b, size):
        at = pl.ds(0, HEADS * size)
        return pltpu.make_async_copy(probs_h.at[b, at], probs.at[b, at], sems.at[2 * blocks + b])

    rows_in_use(lambda copy: copy.start())
    by_length(lens, count, seq, lambda b, size: probs_of(b, size).start())
    grad[...] = jnp.zeros_like(grad)
    sums[...] = jnp.zeros_like(sums)
    rows_in_use(lambda copy: copy.wait())

    def attend(b, size):
        rows, key_rows = sentence_rows(offs, b, seq), sentence_rows(offs, b, size)
        real = lax.broadcasted_iota(jnp.int32, (seq, 1), 0) < lens[b]
        probs_of(b, size).wait()

        def spread(x):
            return jnp.broadcast_to(jnp.sum(x, axis=0, keepdims=True), x.shape)

        for group in range(0, width // PAIR, GROUP):
            pairs = range(group, group + GROUP)
            cols = [slice(p * PAIR, (p + 1) * PAIR) for p in pairs]
            ups = [jnp.where(real, ctx_grad[rows, c], jnp.zeros((), b16)) for c in cols]
            queries = [qkv[rows, c] for c in cols]
            keys = [split_heads(qkv[key_rows, width + c.start : width + c.stop]) for c in cols]
            vals = [split_heads(qkv[key_rows, 2 * width + c.start : 2 * width + c.stop]) for c in cols]
            lows = [probs[b, p * 2 * size : (p + 1) * 2 * size, :] for p in pairs]
            prob_grads = [dot_nt(v, up) for v, up in zip(vals, ups)]
            val_grads = [join_heads(dot(low, up)).astype(b16) for low, up in zip(lows, ups)]
            scores = []
            for low, pg in zip(lows, prob_grads):
                pr = low.astype(f32)
                scores.append((pr * (pg - by_head(spread, pg * pr))).astype(b16))
            query_grads = [(dot_tn(s, k) * (HEAD_DIM ** -0.5)).astype(b16) for s, k in zip(scores, keys)]
            key_grads = [join_heads(dot(s, q)).astype(b16) for s, q in zip(scores, queries)]
            for i, c in enumerate(cols):
                grad[rows, c] = query_grads[i]
                grad[key_rows, width + c.start : width + c.stop] = key_grads[i]
                grad[key_rows, 2 * width + c.start : 2 * width + c.stop] = val_grads[i]

    by_length(lens, count, seq, attend)

    def total(t, _):
        for c in (0, 2):
            add_row(sums, c // 2, grad[tile_at(t), c * width : (c + 1) * width].astype(f32))
        return 0

    lax.fori_loop(0, tiles[0], total, 0)

def input_kernel(lens, offs, tiles, place, homes, grad, mid, xs, biases, wqkv_h, gx, gy, *refs):
    *outs, buf, acc, tail, wqkv, sems = refs
    count, seq, width = gx.shape
    t = pl.program_id(0)
    ready = early(t, [pltpu.make_async_copy(wqkv_h, wqkv, sems.at[0])])

    @pl.when(t == 0)
    def _():
        gx[...] = jnp.zeros_like(gx)
        gy[...] = jnp.zeros_like(gy)

    @pl.when(t < tiles[0])
    def _():
        accumulate(t, acc, slice(None), xs[...], grad[...])
        ready(0)
        buf[tile_at(t), :] = dot_nt(grad[...], flat_of(wqkv)) + mid[...]

    @pl.when(t == pl.num_programs(0) - 1)
    def _():
        def unpack(b, _):
            blocks = (lens[b] + PACK - 1) // PACK
            for side, target in enumerate((gx, gy)):

                def block(i, _):
                    at = pl.multiple_of(offs[b] + i * PACK, PACK)
                    rows = pl.ds(pl.multiple_of(i * PACK, PACK), PACK)
                    target[homes[count + b], rows, :] = buf[pl.ds(at, PACK), :].astype(target.dtype)
                    return 0

                lax.fori_loop(0, jnp.where(homes[b] == side, blocks, 0), block, 0)
            return 0

        lax.fori_loop(0, count, unpack, 0)
        deal(place, acc, outs)
        if len(outs) > 1:
            cols, lanes = acc.shape[1], tail.shape[1]
            each = biases.shape[1] // lanes
            tail[...] = jnp.zeros_like(tail)
            for r in range(2 * each):
                tail[r : r + 1, :] = biases[r // each : r // each + 1, r % each * lanes : (r % each + 1) * lanes]
            block = tail[...].astype(b16)
            mine, first, rest = outs
            for target in [mine.at[k] for k in range(4)] + [first] + [rest.at[k] for k in range(3)]:
                for spot in range(FAR):
                    target[spot, :, cols : cols + lanes] = block


def small_kernel(spot, sums, tail, *outs):
    width = sums.shape[1] // 3
    *plain, ups, head, classes = outs
    mine = plain[0].shape[1]

    def share(x, size):
        x = jnp.broadcast_to(x, (8, x.shape[1])) if x.shape[0] == 1 else x
        return pltpu.roll(x, lax.rem(x.shape[1] - spot[0] * size, x.shape[1]), axis=1)[:, 0:size]

    count = width // tail.shape[1]
    for p in range(2):
        row = jnp.concatenate([tail[p * count + r : p * count + r + 1, :] for r in range(count)], 1)
        plain[p][...] = share(row, mine)[0:1]
    blocks = [share(sums[0:8, p * width : (p + 1) * width], mine) for p in (0, 2)]
    for out, (block, row) in zip(plain[2:], ((1, 2), (1, 0), (1, 1), (0, 2), (0, 0), (0, 1))):
        out[...] = blocks[block][row : row + 1]
    ups[...] = share(jnp.concatenate([sums[r : r + 1, width : 2 * width] for r in range(4)], 1), 4 * mine)[0:1]
    head[...] = share(sums[8:16, :], 3 * mine)[0:NCLASS]
    classes[...] = jnp.transpose(sums[8:16, 0:128])[0:1, NCLASS : 2 * NCLASS]


class Tiled:
    def __init__(self, array):
        self.array = array


class Flat:
    def __init__(self, array):
        self.array = array


class Scalars:
    def __init__(self, array):
        self.array = array


def spec_of(x):
    if isinstance(x, Scalars):
        return pl.BlockSpec(memory_space=pltpu.SMEM)
    if isinstance(x, Flat):
        return pl.BlockSpec(memory_space=pl.ANY)
    if isinstance(x, Tiled):
        return pl.BlockSpec((TILE, x.array.shape[1]), lambda i, lens, offs, tiles, place: (jnp.minimum(i, tiles[0] - 1), 0))
    return pl.BlockSpec(x.shape, lambda *_: (0,) * len(x.shape), pipeline_mode=pl.Buffered(1))


def bare(x):
    return x.array if isinstance(x, (Tiled, Flat, Scalars)) else x


def shape(dtype, *dims):
    return jax.ShapeDtypeStruct(dims, dtype)


def call(kernel, meta, args, outs, scratch=(), steps=1, micros=0):
    moved = sum(bare(a).size * bare(a).dtype.itemsize for a in (*args, *outs))
    return pl.pallas_call(
        kernel,
        out_shape=[bare(o) for o in outs],
        grid_spec=pltpu.PrefetchScalarGridSpec(
            num_scalar_prefetch=len(meta),
            grid=(steps,),
            in_specs=[spec_of(a) for a in args],
            out_specs=[spec_of(o) for o in outs],
            scratch_shapes=list(scratch),
        ),
        cost_estimate=pl.CostEstimate(flops=int(micros * 1.15e9), transcendentals=0, bytes_accessed=moved),
        compiler_params=pltpu.CompilerParams(vmem_limit_bytes=58 << 20),
    )(*meta, *[bare(a) for a in args])


def pack_small(vectors):
    total = sum(v.shape[0] for v in vectors)
    rows = -(-total // (8 * CHUNK)) * 8
    at, flat = 0, 0.0
    for v in vectors:
        flat = flat + jnp.pad(v.astype(f32), (at, rows * CHUNK - at - v.shape[0]))
        at += v.shape[0]
    return flat.astype(b16).reshape(rows, CHUNK)


def body(
    embeddings, lengths, labels, qkv_weight, query_bias, value_bias, out_weight, out_bias, attn_gain,
    attn_shift, up_weight, up_bias, down_weight, down_bias, ffn_gain, ffn_shift, head_weight, head_bias,
):
    width = embeddings.shape[-1]
    seq_len = embeddings.shape[2]
    count = embeddings.shape[1]
    rows = -(-count * seq_len // TILE) * TILE
    hidden = up_weight.shape[1]
    groups = lax.axis_size("dp")
    low, far, near = places()
    tower = lax.axis_index("tower")
    shard_rows = qkv_weight.shape[0]
    quick = low == 4 and shard_rows % PACK == 0

    other_len = swap(lengths[0].astype(f32), "tower", 1).astype(jnp.int32)
    first_here = tower == 0
    all_len = jnp.where(
        first_here, jnp.concatenate([lengths[0], other_len]), jnp.concatenate([other_len, lengths[0]])
    )
    ids = jnp.arange(2 * count)
    ahead = (all_len[None, :] > all_len[:, None]) | (
        (all_len[None, :] == all_len[:, None]) & (ids[None, :] < ids[:, None])
    )
    rank = jnp.sum(ahead.astype(jnp.int32), axis=1)
    away = (((rank + 1) // 2) % 2 != tower).astype(jnp.int32)
    picked = (away[None, :] == 0) & (rank[None, :] // 2 == jnp.arange(count)[:, None])
    source = jnp.sum(jnp.where(picked, ids[None, :], 0), axis=1)
    sent_len = jnp.sum(jnp.where(picked, all_len[None, :], 0), axis=1)
    homes = jnp.concatenate([(source // count != tower).astype(jnp.int32), source % count, away, rank // 2])
    homes = homes.astype(jnp.int32)

    taken = (sent_len + PACK - 1) // PACK * PACK
    before = jnp.arange(count)[None, :] < jnp.arange(count)[:, None]
    offs = jnp.sum(jnp.where(before, taken[None, :], 0), axis=1)
    tiles = (jnp.sum(taken)[None] + TILE - 1) // TILE
    place = jnp.stack([tower, near, far]).astype(jnp.int32)
    meta = (sent_len, offs, tiles, place)
    steps = rows // TILE

    packed = pack_small((
        query_bias, value_bias, out_bias, attn_gain, attn_shift, down_bias, ffn_gain, ffn_shift, up_bias,
        head_weight.reshape(-1),
    ))
    weights = (qkv_weight, out_weight, up_weight, down_weight)
    if quick:
        sizes = [w.size // 2 // CHUNK for w in weights]
        first_part, up_part, down_part = call(
            parts_kernel, (place,), (*weights, packed),
            (
                shape(b16, sizes[0] + packed.shape[0], CHUNK), shape(b16, sizes[1] + sizes[2], CHUNK),
                shape(b16, sizes[3], CHUNK),
            ),
        )
    else:
        first_part = jnp.concatenate([to_chunks(qkv_weight), packed], 0)
        up_part, down_part = jnp.concatenate([to_chunks(out_weight), to_chunks(up_weight)], 0), to_chunks(down_weight)
    cut = first_part.shape[0] - packed.shape[0]
    low_far = far_pieces(first_part)
    other_tokens = swap(embeddings[0], "tower", 1)
    low_far = after(low_far, other_tokens, homes)
    block_first = in_order(low_far, far, 0)
    far_up = far_pieces(after(up_part, *low_far))
    full = [(FAR, w.shape[0] * low, w.shape[1]) for w in weights]
    if quick:
        near_first = gather_near(block_first)
        far_up = after(far_up, *near_first[3:])
        block_up = in_order(far_up, far, 0)
        far_down = far_pieces(after(down_part, *far_up))
        pieces_first = near_first + [swap(p, "tower", 1) for p in near_first]
        tails = [p[:, cut:] for p in near_first]
        packs = in_order(tails[:3] + [jnp.concatenate(tails[3:], 0)], near, 1)
    else:
        block_up = in_order(far_up, far, 0)
        far_down = far_pieces(down_part)
        whole_first = gather_any(block_first)
        pieces_first = [from_chunks(whole_first[:, :, :cut], shard_rows)]
        packs = whole_first[:, :, cut:]
    packs = packs.reshape(groups, -1).astype(f32)
    cuts = [8 * shard_rows, 8 * shard_rows + up_bias.shape[0]]
    cuts.append(cuts[1] + head_weight.size)
    vec = packs[:, : cuts[0]].reshape(groups, 8, shard_rows).transpose(1, 0, 2).reshape(8, width)
    ups = packs[:, cuts[0] : cuts[1]].reshape(-1, width)
    head_rows = packs[:, cuts[1] : cuts[2]].reshape(-1, NCLASS).T

    ext = rows + seq_len
    dense = 2 * rows * width
    sinks = [
        Flat(shape(b16, ext, width)), Flat(shape(b16, ext, 3 * width)),
        Flat(shape(b16, count, HEADS * seq_len, seq_len)), Flat(shape(b16, ext, width)),
    ]
    if quick:
        both = [Flat(shape(b16, *full[0]))] + sinks
        pieces_first = after(pieces_first, block_up)
        proj_qkv, xs, qkv, probs, ctx = call(
            partial(attend_kernel, 10), meta,
            (Scalars(homes), embeddings[0], other_tokens, vec, *map(Flat, pieces_first)), both,
            [pltpu.VMEM(o.array.shape, o.array.dtype) for o in both]
            + [pltpu.SemaphoreType.DMA((30,)), pltpu.SemaphoreType.DMA((5,))],
            micros=16,
        )
    else:
        (proj_qkv,) = pieces_first
        xs, qkv, probs, ctx = call(
            partial(attend_kernel, 0), meta, (Scalars(homes), embeddings[0], other_tokens, vec, proj_qkv), sinks,
            [pltpu.VMEM(o.array.shape, o.array.dtype) for o in sinks] + [pltpu.SemaphoreType.DMA((5,))],
            micros=16,
        )

    wide, slim, thin = shape(b16, rows, hidden), shape(f32, rows, width), shape(f32, rows, 128)
    outs = [Tiled(wide), Tiled(wide), Tiled(slim), Tiled(thin)]
    args = Tiled(ctx), Tiled(xs), vec, ups
    if quick:
        near_up = gather_near(block_up, ctx)
        block_down = in_order(after(far_down, ctx), far, 0)
        pieces_up = near_up + [swap(p, "tower", 1) for p in near_up]
        proj_out, proj_up, act, slope, n1, inv1 = call(
            partial(up_kernel, 10, shard_rows), meta, (*args, *map(Flat, pieces_up)),
            [Flat(shape(b16, *full[1])), Flat(shape(b16, *full[2]))] + outs,
            [
                pltpu.VMEM(full[1], b16), pltpu.VMEM(full[2], b16), pltpu.SemaphoreType.DMA((50,)),
                pltpu.SemaphoreType.DMA((2,)),
            ],
            steps=steps, micros=14,
        )
    else:
        whole_up = gather_any(block_up)
        cut = out_weight.size // 2 // CHUNK
        proj_out = from_chunks(whole_up[:, :, :cut], shard_rows)
        proj_up = from_chunks(whole_up[:, :, cut:], shard_rows)
        act, slope, n1, inv1 = call(
            partial(up_kernel, 0, 0), meta, (*args, proj_out, proj_up), outs, steps=steps, micros=14,
        )
    outs = [Tiled(slim), Tiled(thin), shape(f32, count, width)]
    if quick:
        near_down = gather_near(block_down, act)
        pieces_down = near_down + [swap(p, "tower", 1) for p in near_down]
        proj_down, n2, inv2, pooled = call(
            partial(down_kernel, 10, down_weight.shape[0]), meta, (Tiled(n1), Tiled(act), vec, *map(Flat, pieces_down)),
            [Flat(shape(b16, *full[3]))] + outs,
            [pltpu.VMEM(full[3], b16), pltpu.SemaphoreType.DMA((10,)), pltpu.SemaphoreType.DMA((1,))],
            steps=steps, micros=10,
        )
    else:
        proj_down = from_chunks(gather_any(in_order(far_down, far, 0)), down_weight.shape[0])
        n2, inv2, pooled = call(
            partial(down_kernel, 0, 0), meta, (Tiled(n1), Tiled(act), vec, proj_down), outs, steps=steps, micros=10,
        )

    def dealt(full_rows, cols):
        if quick:
            block = FAR, full_rows // (8 * FAR), cols
            return [shape(b16, 4, *block), shape(b16, *block), shape(b16, 3, *block)]
        return [shape(b16, full_rows, cols)]

    partner = swap(pooled, "tower", 1)
    sums_of = shape(f32, 8, width)
    sum_grad, *down_parts, sums_two, tops, own_pooled = call(
        down_back_kernel, meta,
        (
            Scalars(homes), Scalars(labels), Scalars(head_bias.astype(f32)), pooled, partner, head_rows, Tiled(act), Tiled(n2),
            Tiled(inv2), vec,
        ),
        [Tiled(slim)] + dealt(hidden, width) + [sums_of, shape(f32, 8, 3 * width), shape(f32, count, width)],
        [pltpu.VMEM((hidden, width), f32), pltpu.VMEM((3, count, width), f32)], steps=steps, micros=11,
    )
    if quick:
        down = Scatter(down_parts)
        sum_grad = after(sum_grad, down.first)
    pre_low, sums_up = call(
        pre_back_kernel, meta, (Tiled(sum_grad), Tiled(slope), proj_down), [Tiled(wide), sums_of], steps=steps,
        micros=8,
    )
    if quick:
        pre_low = after(pre_low, down.corners(), down.rest)
    mid, ctx_grad, *up_parts, sums_one = call(
        mid_back_kernel, meta,
        (Tiled(sum_grad), Tiled(pre_low), Tiled(n1), Tiled(inv1), Tiled(ctx), proj_up, proj_out, vec),
        [Tiled(slim), Tiled(shape(b16, ext, width))] + dealt(width, hidden + width) + [sums_of],
        [pltpu.VMEM((width, hidden + width), f32)], steps=steps, micros=20,
    )
    summed = jnp.concatenate([jnp.concatenate([sums_two, sums_up, sums_one], 1), tops], 0)
    came = swap(summed, "tower", 1)
    if quick:
        up = Scatter(after(up_parts, down.sides()))
        up.sides()
        ctx_grad = after(ctx_grad, came, *up.corner, *up.sent)
    qkv_grad, sums_in = call(
        attend_back_kernel, meta, (Flat(qkv), Flat(probs), Flat(ctx_grad)), [shape(b16, ext, 3 * width), sums_of],
        [
            pltpu.VMEM(qkv.shape, b16), pltpu.VMEM(probs.shape, b16), pltpu.VMEM(ctx_grad.shape, b16),
            pltpu.SemaphoreType.DMA((2 * (ext // seq_len) + count,)),
        ],
        micros=14,
    )
    summed = after(summed + came, qkv_grad)
    came = swap(summed, "dp", low)
    if quick:
        mid = after(mid, qkv_grad, *up.side, *down.fars())
        up.fars()
    lanes = 128
    last_cols = 3 * width + (lanes if quick else 0)
    grad_in, grad_away, *last_parts = call(
        input_kernel, meta, (Scalars(homes), Tiled(qkv_grad), Tiled(mid), Tiled(xs), sums_in, Flat(proj_qkv)),
        [shape(f32, count, seq_len, width), shape(b16, count, seq_len, width)] + dealt(width, last_cols),
        [pltpu.VMEM((rows, width), f32), pltpu.VMEM((width, 3 * width), f32), pltpu.VMEM((24, lanes), f32),
         pltpu.VMEM(full[0], b16), pltpu.SemaphoreType.DMA((1,))],
        steps=steps, micros=16,
    )
    if quick:
        last_parts, up.far, came = after((last_parts, up.far, came))
    summed = summed + came
    came = swap(summed, "dp", 2 * low)
    if quick:
        last = Scatter(last_parts)
        last.sides()
        came = after(came, *last.sent)
        grad_in = grad_in + swap(after(grad_away, *last.corner), "tower", 1).astype(f32)
        last.far = after(last.fars(), grad_in)
        down_out, up_out, last_out = down.sum(), up.sum(), last.sum()
        tail, last_out = last_out[:, 3 * width :], last_out[:, : 3 * width]
    else:
        grad_in = grad_in + swap(grad_away, "tower", 1).astype(f32)
        down_out, up_out, last_out = (scatter_any(*p) for p in (down_parts, up_parts, last_parts))
        tail, bit = add_from(sums_in[0:2].reshape(-1, lanes), "tower", 1), 1
        while bit < groups:
            tail = add_from(tail, "dp", bit)
            bit *= 2
    summed, bit = summed + came, 1
    while bit < low:
        came = swap(summed, "dp", bit)
        if quick and bit == 1:
            came = after(came, *last.side)
        summed, bit = summed + came, 2 * bit
    spot = (tower * groups + lax.axis_index("dp")).astype(jnp.int32)[None]
    mine = width // (2 * groups)
    *plain, up_bias_sum, head_sum, class_sum = pl.pallas_call(
        small_kernel,
        out_shape=[shape(f32, 1, mine)] * 8
        + [shape(f32, 1, 4 * mine), shape(f32, NCLASS, 3 * mine), shape(f32, 1, NCLASS)],
        in_specs=[pl.BlockSpec(memory_space=pltpu.SMEM)] + [pl.BlockSpec(memory_space=pltpu.VMEM)] * 2,
        out_specs=[pl.BlockSpec(memory_space=pltpu.VMEM)] * 11,
    )(spot, summed, tail)
    q_sum, v_sum, o_sum, gain_one, shift_one, d_sum, gain_two, shift_two = [x.reshape(-1) for x in plain]
    return (
        own_pooled[None],
        grad_in[None],
        last_out,
        q_sum, v_sum,
        up_out[:, hidden:],
        o_sum, gain_one, shift_one,
        up_out[:, :hidden],
        up_bias_sum.reshape(-1),
        down_out,
        d_sum, gain_two, shift_two,
        head_sum.T,
        class_sum.reshape(-1),
    )


def solution(mesh):
    rows, vec = P("dp", None), P("dp")
    out_rows, out_vec = P(("tower", "dp"), None), P(("tower", "dp"))
    return jax.shard_map(
        body,
        mesh=mesh,
        in_specs=(
            P("tower", "dp", None, None), P("tower", "dp"), vec,
            rows, vec, vec, rows, vec, vec, vec, rows, vec, rows, vec, vec, vec, rows, P(),
        ),
        out_specs=(
            P("tower", "dp", None), P("tower", "dp", None, None),
            out_rows, out_vec, out_vec, out_rows, out_vec, out_vec, out_vec, out_rows, out_vec, out_rows, out_vec,
            out_vec, out_vec, out_rows, P(),
        ),
        check_vma=False,
    )
```

```python
from functools import partial
import math

import jax
import jax.numpy as jnp
from jax import lax
from jax.experimental import pallas as pl
from jax.experimental.pallas import tpu as pltpu
from jax.sharding import PartitionSpec as P

HEADS = 12
HEAD_DIM = 64
NCLASS = 3
CHUNK = 384
FAR = 4

eps_norm = 1e-12
gap_soft = 0.01
f32 = jnp.float32
b16 = jnp.bfloat16


def swap(x, axis, k):
    return lax.ppermute(x, axis, [(i, i ^ k) for i in range(lax.axis_size(axis))])


def places():
    low = lax.axis_size("dp") // FAR
    me = lax.axis_index("dp")
    return low, me // low, me % low


def in_order(pieces, me, axis):
    stack = jnp.stack(pieces, axis)
    return jnp.concatenate(
        [lax.dynamic_index_in_dim(stack, me ^ j, axis) for j in range(len(pieces))], axis
    )


def far_pieces(part):
    low, _, _ = places()
    return [part] + [swap(part, "dp", j * low) for j in range(1, FAR)]


def after(x, *deps):
    return lax.optimization_barrier((x, *deps))[0]


def gather_near(block, *ready):
    half = FAR // 2
    by_one, by_two = after((swap(block, "dp", 1), swap(block, "dp", 2)), *ready)
    return [block, by_one, by_two, swap(by_one[:half], "dp", 2), swap(by_two[half:], "dp", 1)]


def gather_any(block):
    low, _, near = places()
    pieces, bit = [block], 1
    while bit < low:
        pieces = pieces + [swap(p, "dp", bit) for p in pieces]
        bit *= 2
    return in_order(pieces, near, 1)


def to_chunks(shard):
    rows, cols = shard.shape
    half = cols // 2
    mine = lax.dynamic_slice_in_dim(shard, lax.axis_index("tower") * half, half, 1)
    return mine.reshape(rows, half // CHUNK, CHUNK).transpose(1, 0, 2).reshape(-1, CHUNK)


def from_chunks(mine, rows):
    other = swap(mine, "tower", 1)
    low_half = lax.axis_index("tower") == 0
    both = jnp.stack([jnp.where(low_half, mine, other), jnp.where(low_half, other, mine)])
    far, low, total = mine.shape[:3]
    n = total // rows
    both = both.reshape(2, far, low, n, rows, CHUNK).transpose(1, 2, 4, 0, 3, 5)
    return both.reshape(far, low * rows, 2 * n * CHUNK)


def add_low(a, b):
    return (a.astype(f32) + b.astype(f32)).astype(b16)


class Scatter:
    def __init__(self, parts):
        self.mine, *others = parts
        self.first = swap(others[0], "tower", 1)
        self.rest = swap(after(others[1], self.first), "tower", 1)
        self.corner = self.side = self.far = None

    def both(self, k, part=slice(None)):
        got = self.first[part] if k == 3 else self.rest[k, part]
        return self.mine[k, part].astype(f32) + got.astype(f32)

    def corners(self):
        if self.corner is None:
            half = FAR // 2
            self.corner = (
                swap(self.both(3, slice(0, half)).astype(b16), "dp", 1),
                swap(self.both(3, slice(half, FAR)).astype(b16), "dp", 2),
            )
        return self.corner

    def sides(self):
        if self.side is None:
            half = FAR // 2
            for_one, for_two = (x.astype(f32) for x in self.corners())
            none = ((0, 0), (0, 0))
            one = self.both(1) + jnp.pad(for_two, ((half, 0), *none))
            two = self.both(2) + jnp.pad(for_one, ((0, half), *none))
            self.sent = one.astype(b16), two.astype(b16)
            self.side = swap(self.sent[0], "dp", 1), swap(self.sent[1], "dp", 2)
        return self.side

    def fars(self):
        if self.far is None:
            low = lax.axis_size("dp") // FAR
            one, two = self.sides()
            self.own = [self.both(0, j) + one[j].astype(f32) + two[j].astype(f32) for j in range(FAR)]
            self.far = [swap(self.own[j].astype(b16), "dp", j * low) for j in range(1, FAR)]
        return self.far

    def sum(self):
        far = self.fars()
        return self.own[0] + far[0].astype(f32) + far[1].astype(f32) + far[2].astype(f32)


def scatter_any(grad):
    low, far, near = places()
    tower = lax.axis_index("tower")
    halves = grad.reshape((2, FAR, low, -1) + grad.shape[1:])
    got = swap(lax.dynamic_index_in_dim(halves, 1 - tower, 0, keepdims=False), "tower", 1)
    data = add_low(lax.dynamic_index_in_dim(halves, tower, 0, keepdims=False), got)
    blocks = [lax.dynamic_index_in_dim(data, near ^ k, 1, keepdims=False) for k in range(low)]
    bit = low // 2
    while bit:
        blocks = [add_low(blocks[k], swap(blocks[k + bit], "dp", bit)) for k in range(bit)]
        bit //= 2
    own = [lax.dynamic_index_in_dim(blocks[0], far ^ j, 0, keepdims=False) for j in range(FAR)]
    total = own[0].astype(f32)
    for j in range(1, FAR):
        total = total + swap(own[j], "dp", j * low).astype(f32)
    return total


def add_from(x, axis, k):
    return x + swap(x, axis, k)


TILE = 256
PACK = 16
PAIR = 2 * HEAD_DIM
GROUP = 3
Q_BIAS, V_BIAS, O_BIAS, GAIN_1, SHIFT_1, D_BIAS, GAIN_2, SHIFT_2 = range(8)


def dot(a, b):
    return jnp.dot(a, b, preferred_element_type=f32)


def dot_nt(a, b):
    return lax.dot_general(a, b, (((1,), (1,)), ((), ())), preferred_element_type=f32)


def dot_tn(a, b):
    return lax.dot_general(a, b, (((0,), (0,)), ((), ())), preferred_element_type=f32)


def tile_at(t):
    return pl.ds(pl.multiple_of(t * TILE, TILE), TILE)


def sentence_rows(offs, b, seq):
    return pl.ds(pl.multiple_of(offs[b], PACK), seq)


def split_heads(x):
    left = lax.broadcasted_iota(jnp.int32, x.shape, 1) < HEAD_DIM
    zero = jnp.zeros_like(x)
    return jnp.concatenate([jnp.where(left, x, zero), jnp.where(left, zero, x)], 0)


def join_heads(x):
    seq = x.shape[0] // 2
    left = lax.broadcasted_iota(jnp.int32, (seq, PAIR), 1) < HEAD_DIM
    return jnp.where(left, x[:seq], x[seq:])


def by_head(fn, x):
    half = x.shape[0] // 2
    return jnp.concatenate([fn(x[:half]), fn(x[half:])], 0)


def pair_lanes(base, p):
    at = base + p * PAIR
    return slice(at, at + PAIR) if isinstance(p, int) else pl.ds(pl.multiple_of(at, PAIR), PAIR)


def pair_rows(p, size):
    return slice(p * size, (p + 1) * size) if isinstance(p, int) else pl.ds(pl.multiple_of(p * size, PAIR), size)


def over_pairs(count, looped, step):
    def one(g, _):
        step(g * GROUP)
        return 0

    if looped:
        lax.fori_loop(0, count // GROUP, one, 0)
    else:
        for first in range(0, count, GROUP):
            step(first)


def by_length(lens, count, seq, step):
    def one(b, _):
        @pl.when(lens[b] > seq // 2)
        def _():
            step(b, seq)

        @pl.when(lens[b] <= seq // 2)
        def _():
            step(b, seq // 2)

        return 0

    lax.fori_loop(0, count, one, 0)


def norm_rows(hidden):
    center = hidden - jnp.mean(hidden, axis=-1, keepdims=True)
    inverse = lax.rsqrt(jnp.mean(center * center, axis=-1, keepdims=True) + eps_norm)
    return center * inverse, inverse


def norm_back(upstream, normal, inverse, gain):
    scaled = upstream * gain
    inner = scaled - jnp.mean(scaled, axis=-1, keepdims=True)
    return inverse * (inner - normal * jnp.mean(scaled * normal, axis=-1, keepdims=True))


def row_of(vec, i):
    return vec[i : i + 1, :].astype(f32)


def add_row(sums, i, x):
    sums[i : i + 1, :] += jnp.sum(x, axis=0, keepdims=True)


def parts_kernel(place, wqkv, wout, wup, wdown, packed, first, second, third):
    def put(src, dst, at):
        rows, half = src.shape[0], src.shape[1] // 2
        for c in range(half // CHUNK):
            dst[at : at + rows, :] = src[:, pl.ds(pl.multiple_of(place[0] * half + c * CHUNK, 128), CHUNK)]
            at += rows
        return at

    first[put(wqkv, first, 0) :, :] = packed[...]
    put(wup, second, put(wout, second, 0))
    put(wdown, third, 0)


def fetch(place, pieces, targets, sems):
    copies, at = [], 0
    half = FAR // 2
    for weight, rows in targets:
        cols = weight.shape[2] // 2
        for side in range(2):
            tower = place[0] if side == 0 else 1 - place[0]
            block, by_one, by_two, low, high = pieces[5 * side : 5 * side + 5]
            spots = (
                (block, 0, 0, FAR), (by_one, 1, 0, FAR), (by_two, 2, 0, FAR), (low, 3, 0, half), (high, 3, half, half)
            )
            for piece, k, far, size in spots:
                for c in range(cols // CHUNK):
                    row = pl.multiple_of((place[1] ^ k) * rows, PACK)
                    col = pl.multiple_of(tower * cols + c * CHUNK, 128)
                    copies.append(
                        pltpu.make_async_copy(
                            piece.at[:, pl.ds(at + c * rows, rows), :],
                            weight.at[pl.ds(far, size), pl.ds(row, rows), pl.ds(col, CHUNK)],
                            sems.at[len(copies)],
                        )
                    )
        at += cols // CHUNK * rows
    return copies


def deal(place, acc, outs, base=0):
    cols = acc.shape[1]
    if len(outs) == 1:
        outs[0][:, base : base + cols] = acc[...].astype(b16)
        return
    mine, first, rest = outs
    rows = first.shape[1]
    for own in (False, True):
        side = place[0] if own else 1 - place[0]
        for k in range(4):
            target = mine.at[k] if own else first if k == 3 else rest.at[k]

            def block(j, _):
                at = (side * 4 * FAR + (place[2] ^ j) * 4 + (place[1] ^ k)) * rows
                target[j, :, base : base + cols] = acc[pl.ds(pl.multiple_of(at, 8), rows), :].astype(b16)
                return 0

            lax.fori_loop(0, FAR, block, 0)


def flat_of(weight, cols=slice(None)):
    block = weight[:, :, cols]
    return block.reshape(block.shape[0] * block.shape[1], block.shape[2])


def attend_kernel(n_pieces, lens, offs, tiles, place, homes, vec, x_h, y_h, *refs):
    pieces, refs = refs[:n_pieces], refs[n_pieces:]
    if n_pieces:
        wqkv_h, *sinks, x, xs, qkv, probs, ctx, sems, wqkv, got = refs
        copies = fetch(place, pieces, ((wqkv, wqkv.shape[1] // 4),), got)
        for copy in copies:
            copy.start()
    else:
        wqkv, *sinks, x, xs, qkv, probs, ctx, sems = refs
        copies = []
    xs_h, qkv_h, probs_h, ctx_h = sinks
    count, seq, width = x.shape

    def tokens(b, size, do):
        for side, source in enumerate((x_h, y_h)):

            @pl.when(homes[b] == side)
            def _():
                at = pl.ds(0, size)
                do(pltpu.make_async_copy(source.at[homes[count + b], at], x.at[b, at], sems.at[0, b]))

    by_length(lens, count, seq, lambda b, size: tokens(b, size, lambda copy: copy.start()))
    xs[...] = jnp.zeros_like(xs)
    ctx[...] = jnp.zeros_like(ctx)
    by_length(lens, count, seq, lambda b, size: tokens(b, size, lambda copy: copy.wait()))

    def pack(b, _):
        def block(i, _):
            at = pl.multiple_of(offs[b] + i * PACK, PACK)
            xs[pl.ds(at, PACK), :] = x[b, pl.ds(pl.multiple_of(i * PACK, PACK), PACK), :]
            return 0

        return lax.fori_loop(0, (lens[b] + PACK - 1) // PACK, block, 0)

    lax.fori_loop(0, count, pack, 0)

    def leave(source, target, which, do):
        def one(i, _):
            at = pl.ds(pl.multiple_of(i * seq, seq), seq)
            do(pltpu.make_async_copy(source.at[at], target.at[at], sems.at[which, i]))
            return 0

        lax.fori_loop(0, tiles[0] * (TILE // seq) + 1, one, 0)

    def probs_of(b, size):
        at = pl.ds(0, HEADS * size)
        return pltpu.make_async_copy(probs.at[b, at], probs_h.at[b, at], sems.at[4, b])

    leave(xs, xs_h, 1, lambda copy: copy.start())
    for copy in copies:
        copy.wait()
    if n_pieces:
        out = pltpu.make_async_copy(wqkv, wqkv_h, sems.at[5, 0])
        out.start()

    def project(t, _):
        x = xs[tile_at(t), :]
        for c in range(3):
            cols = slice(c * width, (c + 1) * width)
            joined = dot(x, flat_of(wqkv, cols))
            if c == 0:
                joined = (joined + row_of(vec, Q_BIAS)) * (HEAD_DIM ** -0.5)
            if c == 2:
                joined = joined + row_of(vec, V_BIAS)
            qkv[tile_at(t), cols] = joined.astype(b16)
        return 0

    lax.fori_loop(0, tiles[0], project, 0)
    qkv[pl.ds(pl.multiple_of(tiles[0] * TILE, TILE), seq), :] = jnp.zeros((seq, 3 * width), b16)
    leave(qkv, qkv_h, 2, lambda copy: copy.start())

    def attend(b, size):
        rows, key_rows = sentence_rows(offs, b, seq), sentence_rows(offs, b, size)
        valid = lax.broadcasted_iota(jnp.int32, (size, seq), 0) < lens[b]

        def softmax(s):
            s = jnp.where(valid, s, -1000000000.0)
            e = jnp.exp(s - jnp.max(s, axis=0, keepdims=True))
            return (e * (1.0 / jnp.sum(e, axis=0, keepdims=True))).astype(b16)

        def pairs(group):
            spots = range(GROUP)
            queries = [qkv[rows, pair_lanes(0, group + i)] for i in spots]
            keys = [split_heads(qkv[key_rows, pair_lanes(width, group + i)]) for i in spots]
            vals = [split_heads(qkv[key_rows, pair_lanes(2 * width, group + i)]) for i in spots]
            scores = [dot_nt(k, q) for k, q in zip(keys, queries)]
            lows = [by_head(softmax, s) for s in scores]
            outs = [dot_tn(low, v).astype(b16) for low, v in zip(lows, vals)]
            for i, low, out in zip(spots, lows, outs):
                probs[b, pair_rows(group + i, 2 * size), :] = low
                ctx[rows, pair_lanes(0, group + i)] = out

        over_pairs(width // PAIR, size == seq, pairs)
        probs_of(b, size).start()

    by_length(lens, count, seq, attend)
    leave(ctx, ctx_h, 3, lambda copy: copy.start())
    leave(xs, xs_h, 1, lambda copy: copy.wait())
    leave(qkv, qkv_h, 2, lambda copy: copy.wait())
    leave(ctx, ctx_h, 3, lambda copy: copy.wait())
    by_length(lens, count, seq, lambda b, size: probs_of(b, size).wait())
    if n_pieces:
        out.wait()


def inside(offs, lens, b, t):
    row = t * TILE + lax.broadcasted_iota(jnp.int32, (TILE, 1), 0)
    return (row >= offs[b]) & (row < offs[b] + lens[b])


def take_weights(step, place, pieces, refs, count, rows):
    if not pieces:
        return refs[:count], refs[count:], lambda: None, lambda: None
    sinks, refs = refs[:count], refs[count:]
    held, got, sent, refs = refs[-count - 2 : -2], refs[-2], refs[-1], refs[: -count - 2]
    leave = [pltpu.make_async_copy(a, b, sent.at[i]) for i, (a, b) in enumerate(zip(held, sinks))]

    copies = fetch(place, pieces, [(weight, rows) for weight in held], got)
    first = held[0].shape[2] // CHUNK * 5

    @pl.when(step == 0)
    def _():
        for copy in copies:
            copy.start()
        for copy in copies[:first]:
            copy.wait()

    def others():
        @pl.when(step == 0)
        def _():
            for copy in copies[first:]:
                copy.wait()
            for copy in leave:
                copy.start()

    def finish():
        @pl.when(step == pl.num_programs(0) - 1)
        def _():
            for copy in leave:
                copy.wait()

    return held, refs, others, finish


def up_kernel(n_pieces, rows, lens, offs, tiles, place, ctx, xs, vec, ups, *refs):
    t = pl.program_id(0)
    pieces, refs = refs[:n_pieces], refs[n_pieces:]
    (wout, wup), (act, slope, n1, inv1), others, finish = take_weights(t, place, pieces, refs, 2, rows)
    width = n1.shape[1]

    @pl.when(t < tiles[0])
    def _():
        attended = dot(ctx[...], flat_of(wout)) + row_of(vec, O_BIAS)
        normal, inverse = norm_rows(xs[...].astype(f32) + attended)
        n1[...] = normal
        inv1[...] = jnp.broadcast_to(inverse, (TILE, 128))
        low = (normal * row_of(vec, GAIN_1) + row_of(vec, SHIFT_1)).astype(b16)
        others()

        def chunk(c, _):
            cols = pl.ds(pl.multiple_of(c * width, width), width)
            pre = dot(low, flat_of(wup, cols)) + ups[pl.ds(c, 1), :]
            half = 0.5 * (1.0 + lax.erf(pre * (0.5 ** 0.5)))
            act[:, cols] = (pre * half).astype(b16)
            slope[:, cols] = (half + pre * (jnp.exp(-0.5 * pre * pre) * 0.3989422804014327)).astype(b16)
            return 0

        lax.fori_loop(0, ups.shape[0], chunk, 0)

    finish()


def down_kernel(n_pieces, rows, lens, offs, tiles, place, n1, act, vec, *refs):
    t = pl.program_id(0)
    pieces, refs = refs[:n_pieces], refs[n_pieces:]
    (wdown,), (n2, inv2, pooled), others, finish = take_weights(t, place, pieces, refs, 1, rows)
    others()
    width = n1.shape[1]
    count = pooled.shape[0]

    @pl.when(t == 0)
    def _():
        pooled[...] = jnp.zeros_like(pooled)

    @pl.when(t < tiles[0])
    def _():
        total = n1[...] * row_of(vec, GAIN_1) + row_of(vec, SHIFT_1) + row_of(vec, D_BIAS)
        total = total + dot(act[...], flat_of(wdown))
        normal, inverse = norm_rows(total)
        n2[...] = normal
        inv2[...] = jnp.broadcast_to(inverse, (TILE, 128))
        for b in range(count):
            add_row(pooled, b, jnp.where(inside(offs, lens, b, t), normal, 0.0))

    @pl.when(t == pl.num_programs(0) - 1)
    def _():
        for b in range(count):
            size = jnp.full((1, width), lens[b], jnp.int32).astype(f32)
            pooled[b : b + 1, :] = pooled[b : b + 1, :] / size * row_of(vec, GAIN_2) + row_of(vec, SHIFT_2)

    finish()


def accumulate(t, acc, cols, left, right):
    @pl.when(t == 0)
    def _():
        acc[:, cols] = dot_tn(left, right)

    @pl.when(t > 0)
    def _():
        acc[:, cols] += dot_tn(left, right)


def pair_head(lens, place, homes, labels, bias, pooled, partner, head, tops, own, ends):
    count, width = pooled.shape

    for side in range(2):
        for i in range(count):
            at = side * count + i
            away, slot = homes[2 * count + at], homes[4 * count + at]
            row = jnp.where(away == 0, pooled[pl.ds(slot, 1), :], partner[pl.ds(slot, 1), :])
            ends[side, i : i + 1, :] = row
    left, right = ends[0], ends[1]
    own[...] = jnp.where(place[0] == 0, left, right)
    gap = left - right
    soft = jnp.sqrt(gap * gap + gap_soft)
    feats = (left, right, soft)
    row = lax.broadcasted_iota(jnp.int32, (count, 1), 0)
    label = jnp.zeros((count, 1), jnp.int32)
    for b in range(count):
        label = jnp.where(row == b, labels[b], label)
    logits = []
    for c in range(NCLASS):
        terms = [
            jnp.sum(feats[i] * head[c : c + 1, i * width : (i + 1) * width], axis=-1, keepdims=True) for i in range(3)
        ]
        logits.append(terms[0] + terms[1] + terms[2] + bias[c])
    top = jnp.maximum(jnp.maximum(logits[0], logits[1]), logits[2])
    exps = [jnp.exp(x - top) for x in logits]
    norm = exps[0] + exps[1] + exps[2]
    grads = [exps[c] / norm - jnp.where(label == c, 1.0, 0.0) for c in range(NCLASS)]
    back = []
    tops[...] = jnp.zeros_like(tops)
    for i in range(3):
        cols = slice(i * width, (i + 1) * width)
        back.append(sum(grads[c] * head[c : c + 1, cols] for c in range(NCLASS)))
        for c in range(NCLASS):
            tops[c : c + 1, cols] = 0.5 * jnp.sum(grads[c] * feats[i], axis=0, keepdims=True)
    for c in range(NCLASS):
        tops[NCLASS + c : NCLASS + c + 1, 0:128] = jnp.broadcast_to(0.5 * jnp.sum(grads[c], axis=0, keepdims=True), (1, 128))
    slope = gap / soft
    ends[0] = back[0] + slope * back[2]
    ends[1] = back[1] - slope * back[2]
    for b in range(count):
        side = jnp.where(homes[b] == 0, place[0], 1 - place[0])
        row = ends[side, pl.ds(homes[count + b], 1), :]
        size = jnp.full((1, width), lens[b], jnp.int32).astype(f32)
        ends[2, b : b + 1, :] = row / size


def down_back_kernel(
    lens, offs, tiles, place, homes, labels, bias, pooled, partner, head, act, n2, inv2, vec, sum_grad, *refs
):
    *outs, sums, tops, own, acc, ends = refs
    t = pl.program_id(0)
    count, width = pooled.shape

    @pl.when(t == 0)
    def _():
        pair_head(lens, place, homes, labels, bias, pooled, partner, head, tops, own, ends)
        sums[...] = jnp.zeros_like(sums)

    @pl.when(t < tiles[0])
    def _():
        up = jnp.zeros((TILE, width), f32)
        for b in range(count):
            up = jnp.where(inside(offs, lens, b, t), ends[2, b : b + 1, :], up)
        normal = n2[...]
        grad = norm_back(up, normal, inv2[:, 0:1], row_of(vec, GAIN_2))
        sum_grad[...] = grad
        add_row(sums, 0, up * normal)
        add_row(sums, 1, up)
        add_row(sums, 2, grad)
        low = grad.astype(b16)

        accumulate(t, acc, slice(None), act[...], low)

    @pl.when(t == pl.num_programs(0) - 1)
    def _():
        deal(place, acc, outs)


def early(t, copies):
    @pl.when(t == 0)
    def _():
        for copy in copies:
            copy.start()

    def ready(i):
        @pl.when(t == 0)
        def _():
            copies[i].wait()

    return ready


def pre_back_kernel(lens, offs, tiles, place, sum_grad, slope, wdown, pre_low, sums):
    t = pl.program_id(0)
    width = sum_grad.shape[1]
    chunks = slope.shape[1] // width
    split = wdown.shape[0] // chunks

    @pl.when(t == 0)
    def _():
        sums[...] = jnp.zeros_like(sums)

    @pl.when(t < tiles[0])
    def _():
        low = sum_grad[...].astype(b16)
        for c in range(chunks):
            cols = slice(c * width, (c + 1) * width)
            pre = dot_nt(low, flat_of(wdown[c * split : (c + 1) * split])) * slope[:, cols].astype(f32)
            add_row(sums, c, pre)
            pre_low[:, cols] = pre.astype(b16)


def mid_back_kernel(
    lens, offs, tiles, place, sum_grad, pre_low, n1, inv1, ctx, wup, wout, vec, mid, ctx_grad, *refs
):
    *outs, sums, acc = refs
    t = pl.program_id(0)
    hidden = pre_low.shape[1]

    @pl.when(t == 0)
    def _():
        sums[...] = jnp.zeros_like(sums)

    @pl.when(t < tiles[0])
    def _():
        pre = pre_low[...]
        grad = sum_grad[...] + dot_nt(pre, flat_of(wup))
        normal = n1[...]
        add_row(sums, 0, grad * normal)
        add_row(sums, 1, grad)
        middle = norm_back(grad, normal, inv1[:, 0:1], row_of(vec, GAIN_1))
        add_row(sums, 2, middle)
        mid[...] = middle
        low = middle.astype(b16)
        ctx_grad[...] = dot_nt(low, flat_of(wout)).astype(b16)
        first_low = (normal * row_of(vec, GAIN_1) + row_of(vec, SHIFT_1)).astype(b16)
        accumulate(t, acc, slice(0, hidden), first_low, pre)
        accumulate(t, acc, slice(hidden, None), ctx[...], low)

    @pl.when(t == pl.num_programs(0) - 1)
    def _():
        deal(place, acc, outs)


def attend_back_kernel(lens, offs, tiles, place, qkv_h, probs_h, ctx_grad_h, grad_h, sums, grad, qkv, probs, ctx_grad, sems):
    width = ctx_grad.shape[1]
    count, seq = probs.shape[0], probs.shape[2]
    blocks = qkv.shape[0] // seq

    def rows_in_use(do):
        for i in range(blocks):

            @pl.when(i * seq < tiles[0] * TILE + seq)
            def _():
                at = pl.ds(i * seq, seq)
                do(pltpu.make_async_copy(qkv_h.at[at], qkv.at[at], sems.at[i]))
                do(pltpu.make_async_copy(ctx_grad_h.at[at], ctx_grad.at[at], sems.at[blocks + i]))

    def probs_of(b, size):
        at = pl.ds(0, HEADS * size)
        return pltpu.make_async_copy(probs_h.at[b, at], probs.at[b, at], sems.at[2 * blocks + b])

    rows_in_use(lambda copy: copy.start())
    by_length(lens, count, seq, lambda b, size: probs_of(b, size).start())
    grad[...] = jnp.zeros_like(grad)
    sums[...] = jnp.zeros_like(sums)
    rows_in_use(lambda copy: copy.wait())

    def attend(b, size):
        rows, key_rows = sentence_rows(offs, b, seq), sentence_rows(offs, b, size)
        real = lax.broadcasted_iota(jnp.int32, (seq, 1), 0) < lens[b]
        probs_of(b, size).wait()

        def spread(x):
            return jnp.broadcast_to(jnp.sum(x, axis=0, keepdims=True), x.shape)

        def pairs(group):
            spots = range(GROUP)
            ups = [jnp.where(real, ctx_grad[rows, pair_lanes(0, group + i)], jnp.zeros((), b16)) for i in spots]
            queries = [qkv[rows, pair_lanes(0, group + i)] for i in spots]
            keys = [split_heads(qkv[key_rows, pair_lanes(width, group + i)]) for i in spots]
            vals = [split_heads(qkv[key_rows, pair_lanes(2 * width, group + i)]) for i in spots]
            lows = [probs[b, pair_rows(group + i, 2 * size), :] for i in spots]
            prob_grads = [dot_nt(v, up) for v, up in zip(vals, ups)]
            val_grads = [join_heads(dot(low, up)).astype(b16) for low, up in zip(lows, ups)]
            scores = []
            for low, pg in zip(lows, prob_grads):
                pr = low.astype(f32)
                scores.append((pr * (pg - by_head(spread, pg * pr))).astype(b16))
            query_grads = [(dot_tn(s, k) * (HEAD_DIM ** -0.5)).astype(b16) for s, k in zip(scores, keys)]
            key_grads = [join_heads(dot(s, q)).astype(b16) for s, q in zip(scores, queries)]
            for i in spots:
                grad[rows, pair_lanes(0, group + i)] = query_grads[i]
                grad[key_rows, pair_lanes(width, group + i)] = key_grads[i]
                grad[key_rows, pair_lanes(2 * width, group + i)] = val_grads[i]

        over_pairs(width // PAIR, size == seq, pairs)

    by_length(lens, count, seq, attend)

    def result(t):
        return pltpu.make_async_copy(grad.at[tile_at(t)], grad_h.at[tile_at(t)], sems.at[2 * blocks + count + t])

    def total(t, _):
        result(t).start()
        for c in (0, 2):
            add_row(sums, c // 2, grad[tile_at(t), c * width : (c + 1) * width].astype(f32))
        return 0

    def finish(t, _):
        result(t).wait()
        return 0

    lax.fori_loop(0, tiles[0], total, 0)
    lax.fori_loop(0, tiles[0], finish, 0)


def input_kernel(lens, offs, tiles, place, homes, grad, mid, xs, biases, wqkv_h, gx, gy, *refs):
    *outs, buf, acc, tail, wqkv, sems = refs
    count, seq, width = gx.shape
    t = pl.program_id(0)
    ready = early(t, [pltpu.make_async_copy(wqkv_h, wqkv, sems.at[0])])

    @pl.when(t == 0)
    def _():
        gx[...] = jnp.zeros_like(gx)
        gy[...] = jnp.zeros_like(gy)

    @pl.when(t < tiles[0])
    def _():
        accumulate(t, acc, slice(None), xs[...], grad[...])
        ready(0)
        buf[tile_at(t), :] = dot_nt(grad[...], flat_of(wqkv)) + mid[...]

    @pl.when(t == pl.num_programs(0) - 1)
    def _():
        def unpack(b, _):
            blocks = (lens[b] + PACK - 1) // PACK
            for side, target in enumerate((gx, gy)):

                def block(i, _):
                    at = pl.multiple_of(offs[b] + i * PACK, PACK)
                    rows = pl.ds(pl.multiple_of(i * PACK, PACK), PACK)
                    target[homes[count + b], rows, :] = buf[pl.ds(at, PACK), :].astype(target.dtype)
                    return 0

                lax.fori_loop(0, jnp.where(homes[b] == side, blocks, 0), block, 0)
            return 0

        lax.fori_loop(0, count, unpack, 0)
        deal(place, acc, outs)
        if len(outs) > 1:
            cols, lanes = acc.shape[1], tail.shape[1]
            each = biases.shape[1] // lanes
            tail[...] = jnp.zeros_like(tail)
            for r in range(2 * each):
                tail[r : r + 1, :] = biases[r // each : r // each + 1, r % each * lanes : (r % each + 1) * lanes]
            block = tail[...].astype(b16)
            mine, first, rest = outs
            for target in [mine.at[k] for k in range(4)] + [first] + [rest.at[k] for k in range(3)]:
                for spot in range(FAR):
                    target[spot, :, cols : cols + lanes] = block


def small_kernel(spot, sums, tail, *outs):
    width = sums.shape[1] // 3
    *plain, ups, head, classes = outs
    mine = plain[0].shape[1]

    def share(x, size):
        x = jnp.broadcast_to(x, (8, x.shape[1])) if x.shape[0] == 1 else x
        return pltpu.roll(x, lax.rem(x.shape[1] - spot[0] * size, x.shape[1]), axis=1)[:, 0:size]

    count = width // tail.shape[1]
    for p in range(2):
        row = jnp.concatenate([tail[p * count + r : p * count + r + 1, :] for r in range(count)], 1)
        plain[p][...] = share(row, mine)[0:1]
    blocks = [share(sums[0:8, p * width : (p + 1) * width], mine) for p in (0, 2)]
    for out, (block, row) in zip(plain[2:], ((1, 2), (1, 0), (1, 1), (0, 2), (0, 0), (0, 1))):
        out[...] = blocks[block][row : row + 1]
    ups[...] = share(jnp.concatenate([sums[r : r + 1, width : 2 * width] for r in range(4)], 1), 4 * mine)[0:1]
    head[...] = share(sums[8:16, :], 3 * mine)[0:NCLASS]
    classes[...] = jnp.transpose(sums[8:16, 0:128])[0:1, NCLASS : 2 * NCLASS]


class Tiled:
    def __init__(self, array):
        self.array = array


class Flat:
    def __init__(self, array):
        self.array = array


class Scalars:
    def __init__(self, array):
        self.array = array


def spec_of(x):
    if isinstance(x, Scalars):
        return pl.BlockSpec(memory_space=pltpu.SMEM)
    if isinstance(x, Flat):
        return pl.BlockSpec(memory_space=pl.ANY)
    if isinstance(x, Tiled):
        return pl.BlockSpec((TILE, x.array.shape[1]), lambda i, lens, offs, tiles, place: (jnp.minimum(i, tiles[0] - 1), 0))
    return pl.BlockSpec(x.shape, lambda *_: (0,) * len(x.shape), pipeline_mode=pl.Buffered(1))


def bare(x):
    return x.array if isinstance(x, (Tiled, Flat, Scalars)) else x


def shape(dtype, *dims):
    return jax.ShapeDtypeStruct(dims, dtype)


def call(kernel, meta, args, outs, scratch=(), steps=1, micros=0):
    moved = sum(bare(a).size * bare(a).dtype.itemsize for a in (*args, *outs))
    return pl.pallas_call(
        kernel,
        out_shape=[bare(o) for o in outs],
        grid_spec=pltpu.PrefetchScalarGridSpec(
            num_scalar_prefetch=len(meta),
            grid=(steps,),
            in_specs=[spec_of(a) for a in args],
            out_specs=[spec_of(o) for o in outs],
            scratch_shapes=list(scratch),
        ),
        cost_estimate=pl.CostEstimate(flops=int(micros * 1.15e9), transcendentals=0, bytes_accessed=moved),
        compiler_params=pltpu.CompilerParams(vmem_limit_bytes=58 << 20),
    )(*meta, *[bare(a) for a in args])


def pack_small(vectors):
    total = sum(v.shape[0] for v in vectors)
    rows = -(-total // (8 * CHUNK)) * 8
    at, flat = 0, 0.0
    for v in vectors:
        flat = flat + jnp.pad(v.astype(f32), (at, rows * CHUNK - at - v.shape[0]))
        at += v.shape[0]
    return flat.astype(b16).reshape(rows, CHUNK)


def body(
    embeddings, lengths, labels, qkv_weight, query_bias, value_bias, out_weight, out_bias, attn_gain,
    attn_shift, up_weight, up_bias, down_weight, down_bias, ffn_gain, ffn_shift, head_weight, head_bias,
):
    width = embeddings.shape[-1]
    seq_len = embeddings.shape[2]
    count = embeddings.shape[1]
    rows = -(-count * seq_len // TILE) * TILE
    hidden = up_weight.shape[1]
    groups = lax.axis_size("dp")
    low, far, near = places()
    tower = lax.axis_index("tower")
    shard_rows = qkv_weight.shape[0]
    quick = low == 4 and shard_rows % PACK == 0

    other_len = swap(lengths[0].astype(f32), "tower", 1).astype(jnp.int32)
    first_here = tower == 0
    all_len = jnp.where(
        first_here, jnp.concatenate([lengths[0], other_len]), jnp.concatenate([other_len, lengths[0]])
    )
    ids = jnp.arange(2 * count)
    ahead = (all_len[None, :] > all_len[:, None]) | (
        (all_len[None, :] == all_len[:, None]) & (ids[None, :] < ids[:, None])
    )
    rank = jnp.sum(ahead.astype(jnp.int32), axis=1)
    away = (((rank + 1) // 2) % 2 != tower).astype(jnp.int32)
    picked = (away[None, :] == 0) & (rank[None, :] // 2 == jnp.arange(count)[:, None])
    source = jnp.sum(jnp.where(picked, ids[None, :], 0), axis=1)
    sent_len = jnp.sum(jnp.where(picked, all_len[None, :], 0), axis=1)
    homes = jnp.concatenate([(source // count != tower).astype(jnp.int32), source % count, away, rank // 2])
    homes = homes.astype(jnp.int32)

    taken = (sent_len + PACK - 1) // PACK * PACK
    before = jnp.arange(count)[None, :] < jnp.arange(count)[:, None]
    offs = jnp.sum(jnp.where(before, taken[None, :], 0), axis=1)
    tiles = (jnp.sum(taken)[None] + TILE - 1) // TILE
    place = jnp.stack([tower, near, far]).astype(jnp.int32)
    meta = (sent_len, offs, tiles, place)
    steps = rows // TILE

    packed = pack_small((
        query_bias, value_bias, out_bias, attn_gain, attn_shift, down_bias, ffn_gain, ffn_shift, up_bias,
        head_weight.reshape(-1),
    ))
    weights = (qkv_weight, out_weight, up_weight, down_weight)
    if quick:
        sizes = [w.size // 2 // CHUNK for w in weights]
        first_part, up_part, down_part = call(
            parts_kernel, (place,), (*weights, packed),
            (
                shape(b16, sizes[0] + packed.shape[0], CHUNK), shape(b16, sizes[1] + sizes[2], CHUNK),
                shape(b16, sizes[3], CHUNK),
            ),
        )
    else:
        first_part = jnp.concatenate([to_chunks(qkv_weight), packed], 0)
        up_part, down_part = jnp.concatenate([to_chunks(out_weight), to_chunks(up_weight)], 0), to_chunks(down_weight)
    cut = first_part.shape[0] - packed.shape[0]
    low_far = far_pieces(first_part)
    other_tokens = swap(embeddings[0], "tower", 1)
    low_far = after(low_far, other_tokens, homes)
    block_first = in_order(low_far, far, 0)
    far_up = far_pieces(after(up_part, *low_far))
    full = [(FAR, w.shape[0] * low, w.shape[1]) for w in weights]
    if quick:
        near_first = gather_near(block_first)
        far_up = after(far_up, *near_first[3:])
        block_up = in_order(far_up, far, 0)
        far_down = far_pieces(after(down_part, *far_up))
        pieces_first = near_first + [swap(p, "tower", 1) for p in near_first]
        tails = [p[:, cut:] for p in near_first]
        packs = in_order(tails[:3] + [jnp.concatenate(tails[3:], 0)], near, 1)
    else:
        block_up = in_order(far_up, far, 0)
        far_down = far_pieces(down_part)
        whole_first = gather_any(block_first)
        pieces_first = [from_chunks(whole_first[:, :, :cut], shard_rows)]
        packs = whole_first[:, :, cut:]
    packs = packs.reshape(groups, -1).astype(f32)
    cuts = [8 * shard_rows, 8 * shard_rows + up_bias.shape[0]]
    cuts.append(cuts[1] + head_weight.size)
    vec = packs[:, : cuts[0]].reshape(groups, 8, shard_rows).transpose(1, 0, 2).reshape(8, width)
    ups = packs[:, cuts[0] : cuts[1]].reshape(-1, width)
    head_rows = packs[:, cuts[1] : cuts[2]].reshape(-1, NCLASS).T

    ext = rows + seq_len
    dense = 2 * rows * width
    sinks = [
        Flat(shape(b16, ext, width)), Flat(shape(b16, ext, 3 * width)),
        Flat(shape(b16, count, HEADS * seq_len, seq_len)), Flat(shape(b16, ext, width)),
    ]
    scratch = [pltpu.VMEM((count, seq_len, width), b16)]
    scratch += [pltpu.VMEM(o.array.shape, o.array.dtype) for o in sinks]
    scratch.append(pltpu.SemaphoreType.DMA((6, max(ext // seq_len, count))))
    if quick:
        both = [Flat(shape(b16, *full[0]))] + sinks
        pieces_first = after(pieces_first, block_up)
        proj_qkv, xs, qkv, probs, ctx = call(
            partial(attend_kernel, 10), meta,
            (Scalars(homes), vec, Flat(embeddings[0]), Flat(other_tokens), *map(Flat, pieces_first)), both,
            scratch + [pltpu.VMEM(full[0], b16), pltpu.SemaphoreType.DMA((30,))],
            micros=16,
        )
    else:
        (proj_qkv,) = pieces_first
        xs, qkv, probs, ctx = call(
            partial(attend_kernel, 0), meta, (Scalars(homes), vec, Flat(embeddings[0]), Flat(other_tokens), proj_qkv), sinks,
            scratch,
            micros=16,
        )

    wide, slim, thin = shape(b16, rows, hidden), shape(f32, rows, width), shape(f32, rows, 128)
    outs = [Tiled(wide), Tiled(wide), Tiled(slim), Tiled(thin)]
    args = Tiled(ctx), Tiled(xs), vec, ups
    if quick:
        near_up = gather_near(block_up, ctx)
        block_down = in_order(after(far_down, ctx), far, 0)
        pieces_up = near_up + [swap(p, "tower", 1) for p in near_up]
        proj_out, proj_up, act, slope, n1, inv1 = call(
            partial(up_kernel, 10, shard_rows), meta, (*args, *map(Flat, pieces_up)),
            [Flat(shape(b16, *full[1])), Flat(shape(b16, *full[2]))] + outs,
            [
                pltpu.VMEM(full[1], b16), pltpu.VMEM(full[2], b16), pltpu.SemaphoreType.DMA((50,)),
                pltpu.SemaphoreType.DMA((2,)),
            ],
            steps=steps, micros=14,
        )
    else:
        whole_up = gather_any(block_up)
        cut = out_weight.size // 2 // CHUNK
        proj_out = from_chunks(whole_up[:, :, :cut], shard_rows)
        proj_up = from_chunks(whole_up[:, :, cut:], shard_rows)
        act, slope, n1, inv1 = call(
            partial(up_kernel, 0, 0), meta, (*args, proj_out, proj_up), outs, steps=steps, micros=14,
        )
    outs = [Tiled(slim), Tiled(thin), shape(f32, count, width)]
    if quick:
        near_down = gather_near(block_down, act)
        pieces_down = near_down + [swap(p, "tower", 1) for p in near_down]
        proj_down, n2, inv2, pooled = call(
            partial(down_kernel, 10, down_weight.shape[0]), meta, (Tiled(n1), Tiled(act), vec, *map(Flat, pieces_down)),
            [Flat(shape(b16, *full[3]))] + outs,
            [pltpu.VMEM(full[3], b16), pltpu.SemaphoreType.DMA((10,)), pltpu.SemaphoreType.DMA((1,))],
            steps=steps, micros=10,
        )
    else:
        proj_down = from_chunks(gather_any(in_order(far_down, far, 0)), down_weight.shape[0])
        n2, inv2, pooled = call(
            partial(down_kernel, 0, 0), meta, (Tiled(n1), Tiled(act), vec, proj_down), outs, steps=steps, micros=10,
        )

    def dealt(full_rows, cols):
        if quick:
            block = FAR, full_rows // (8 * FAR), cols
            return [shape(b16, 4, *block), shape(b16, *block), shape(b16, 3, *block)]
        return [shape(b16, full_rows, cols)]

    partner = swap(pooled, "tower", 1)
    sums_of = shape(f32, 8, width)
    sum_grad, *down_parts, sums_two, tops, own_pooled = call(
        down_back_kernel, meta,
        (
            Scalars(homes), Scalars(labels), Scalars(head_bias.astype(f32)), pooled, partner, head_rows, Tiled(act), Tiled(n2),
            Tiled(inv2), vec,
        ),
        [Tiled(slim)] + dealt(hidden, width) + [sums_of, shape(f32, 8, 3 * width), shape(f32, count, width)],
        [pltpu.VMEM((hidden, width), f32), pltpu.VMEM((3, count, width), f32)], steps=steps, micros=11,
    )
    if quick:
        down = Scatter(down_parts)
        sum_grad = after(sum_grad, down.first)
    pre_low, sums_up = call(
        pre_back_kernel, meta, (Tiled(sum_grad), Tiled(slope), proj_down), [Tiled(wide), sums_of], steps=steps,
        micros=8,
    )
    if quick:
        pre_low = after(pre_low, down.corners(), down.rest)
    mid, ctx_grad, *up_parts, sums_one = call(
        mid_back_kernel, meta,
        (Tiled(sum_grad), Tiled(pre_low), Tiled(n1), Tiled(inv1), Tiled(ctx), proj_up, proj_out, vec),
        [Tiled(slim), Tiled(shape(b16, ext, width))] + dealt(width, hidden + width) + [sums_of],
        [pltpu.VMEM((width, hidden + width), f32)], steps=steps, micros=20,
    )
    summed = jnp.concatenate([jnp.concatenate([sums_two, sums_up, sums_one], 1), tops], 0)
    came = swap(summed, "tower", 1)
    if quick:
        up = Scatter(after(up_parts, down.sides()))
        up.sides()
        ctx_grad = after(ctx_grad, came, *up.corner, *up.sent)
    qkv_grad, sums_in = call(
        attend_back_kernel, meta, (Flat(qkv), Flat(probs), Flat(ctx_grad)), [Flat(shape(b16, ext, 3 * width)), sums_of],
        [
            pltpu.VMEM(qkv.shape, b16), pltpu.VMEM(qkv.shape, b16), pltpu.VMEM(probs.shape, b16), pltpu.VMEM(ctx_grad.shape, b16),
            pltpu.SemaphoreType.DMA((2 * (ext // seq_len) + count + steps,)),
        ],
        micros=14,
    )
    summed = after(summed + came, qkv_grad)
    came = swap(summed, "dp", low)
    if quick:
        mid = after(mid, qkv_grad, *up.side, *down.fars())
        up.fars()
    lanes = 128
    last_cols = 3 * width + (lanes if quick else 0)
    grad_in, grad_away, *last_parts = call(
        input_kernel, meta, (Scalars(homes), Tiled(qkv_grad), Tiled(mid), Tiled(xs), sums_in, Flat(proj_qkv)),
        [shape(f32, count, seq_len, width), shape(b16, count, seq_len, width)] + dealt(width, last_cols),
        [pltpu.VMEM((rows, width), f32), pltpu.VMEM((width, 3 * width), f32), pltpu.VMEM((24, lanes), f32),
         pltpu.VMEM(full[0], b16), pltpu.SemaphoreType.DMA((1,))],
        steps=steps, micros=16,
    )
    if quick:
        last_parts, up.far, came = after((last_parts, up.far, came))
    summed = summed + came
    came = swap(summed, "dp", 2 * low)
    if quick:
        last = Scatter(last_parts)
        last.sides()
        came = after(came, *last.sent)
        grad_in = grad_in + swap(after(grad_away, *last.corner), "tower", 1).astype(f32)
        last.far = after(last.fars(), grad_in)
        down_out, up_out, last_out = down.sum(), up.sum(), last.sum()
        tail, last_out = last_out[:, 3 * width :], last_out[:, : 3 * width]
    else:
        grad_in = grad_in + swap(grad_away, "tower", 1).astype(f32)
        down_out, up_out, last_out = (scatter_any(*p) for p in (down_parts, up_parts, last_parts))
        tail, bit = add_from(sums_in[0:2].reshape(-1, lanes), "tower", 1), 1
        while bit < groups:
            tail = add_from(tail, "dp", bit)
            bit *= 2
    summed, bit = summed + came, 1
    while bit < low:
        came = swap(summed, "dp", bit)
        if quick and bit == 1:
            came = after(came, *last.side)
        summed, bit = summed + came, 2 * bit
    spot = (tower * groups + lax.axis_index("dp")).astype(jnp.int32)[None]
    mine = width // (2 * groups)
    *plain, up_bias_sum, head_sum, class_sum = pl.pallas_call(
        small_kernel,
        out_shape=[shape(f32, 1, mine)] * 8
        + [shape(f32, 1, 4 * mine), shape(f32, NCLASS, 3 * mine), shape(f32, 1, NCLASS)],
        in_specs=[pl.BlockSpec(memory_space=pltpu.SMEM)] + [pl.BlockSpec(memory_space=pltpu.VMEM)] * 2,
        out_specs=[pl.BlockSpec(memory_space=pltpu.VMEM)] * 11,
    )(spot, summed, tail)
    q_sum, v_sum, o_sum, gain_one, shift_one, d_sum, gain_two, shift_two = [x.reshape(-1) for x in plain]
    return (
        own_pooled[None],
        grad_in[None],
        last_out,
        q_sum, v_sum,
        up_out[:, hidden:],
        o_sum, gain_one, shift_one,
        up_out[:, :hidden],
        up_bias_sum.reshape(-1),
        down_out,
        d_sum, gain_two, shift_two,
        head_sum.T,
        class_sum.reshape(-1),
    )


def solution(mesh):
    rows, vec = P("dp", None), P("dp")
    out_rows, out_vec = P(("tower", "dp"), None), P(("tower", "dp"))
    return jax.shard_map(
        body,
        mesh=mesh,
        in_specs=(
            P("tower", "dp", None, None), P("tower", "dp"), vec,
            rows, vec, vec, rows, vec, vec, vec, rows, vec, rows, vec, vec, vec, rows, P(),
        ),
        out_specs=(
            P("tower", "dp", None), P("tower", "dp", None, None),
            out_rows, out_vec, out_vec, out_rows, out_vec, out_vec, out_vec, out_rows, out_vec, out_rows, out_vec,
            out_vec, out_vec, out_rows, P(),
        ),
        check_vma=False,
    )
```

```python
from functools import partial
import math

import jax
import jax.numpy as jnp
from jax import lax
from jax.experimental import pallas as pl
from jax.experimental.pallas import tpu as pltpu
from jax.sharding import PartitionSpec as P

HEADS = 12
HEAD_DIM = 64
NCLASS = 3
CHUNK = 384
FAR = 4

eps_norm = 1e-12
gap_soft = 0.01
f32 = jnp.float32
b16 = jnp.bfloat16


def swap(x, axis, k):
    return lax.ppermute(x, axis, [(i, i ^ k) for i in range(lax.axis_size(axis))])


def places():
    low = lax.axis_size("dp") // FAR
    me = lax.axis_index("dp")
    return low, me // low, me % low


def in_order(pieces, me, axis):
    stack = jnp.stack(pieces, axis)
    return jnp.concatenate(
        [lax.dynamic_index_in_dim(stack, me ^ j, axis) for j in range(len(pieces))], axis
    )


def far_pieces(part):
    low, _, _ = places()
    return [part] + [swap(part, "dp", j * low) for j in range(1, FAR)]


def after(x, *deps):
    return lax.optimization_barrier((x, *deps))[0]


def gather_near(block, *ready):
    half = FAR // 2
    by_one, by_two = after((swap(block, "dp", 1), swap(block, "dp", 2)), *ready)
    return [block, by_one, by_two, swap(by_one[:half], "dp", 2), swap(by_two[half:], "dp", 1)]


def gather_any(block):
    low, _, near = places()
    pieces, bit = [block], 1
    while bit < low:
        pieces = pieces + [swap(p, "dp", bit) for p in pieces]
        bit *= 2
    return in_order(pieces, near, 1)


def to_chunks(shard):
    rows, cols = shard.shape
    half = cols // 2
    mine = lax.dynamic_slice_in_dim(shard, lax.axis_index("tower") * half, half, 1)
    return mine.reshape(rows, half // CHUNK, CHUNK).transpose(1, 0, 2).reshape(-1, CHUNK)


def from_chunks(mine, rows):
    other = swap(mine, "tower", 1)
    low_half = lax.axis_index("tower") == 0
    both = jnp.stack([jnp.where(low_half, mine, other), jnp.where(low_half, other, mine)])
    far, low, total = mine.shape[:3]
    n = total // rows
    both = both.reshape(2, far, low, n, rows, CHUNK).transpose(1, 2, 4, 0, 3, 5)
    return both.reshape(far, low * rows, 2 * n * CHUNK)


def add_low(a, b):
    return (a.astype(f32) + b.astype(f32)).astype(b16)


class Scatter:
    def __init__(self, parts):
        self.mine, *others = parts
        self.first = swap(others[0], "tower", 1)
        self.rest = swap(after(others[1], self.first), "tower", 1)
        self.corner = self.side = self.far = None

    def both(self, k, part=slice(None)):
        got = self.first[part] if k == 3 else self.rest[k, part]
        return self.mine[k, part].astype(f32) + got.astype(f32)

    def corners(self):
        if self.corner is None:
            half = FAR // 2
            self.corner = (
                swap(self.both(3, slice(0, half)).astype(b16), "dp", 1),
                swap(self.both(3, slice(half, FAR)).astype(b16), "dp", 2),
            )
        return self.corner

    def sides(self):
        if self.side is None:
            half = FAR // 2
            for_one, for_two = (x.astype(f32) for x in self.corners())
            none = ((0, 0), (0, 0))
            one = self.both(1) + jnp.pad(for_two, ((half, 0), *none))
            two = self.both(2) + jnp.pad(for_one, ((0, half), *none))
            self.sent = one.astype(b16), two.astype(b16)
            self.side = swap(self.sent[0], "dp", 1), swap(self.sent[1], "dp", 2)
        return self.side

    def fars(self):
        if self.far is None:
            low = lax.axis_size("dp") // FAR
            one, two = self.sides()
            self.own = [self.both(0, j) + one[j].astype(f32) + two[j].astype(f32) for j in range(FAR)]
            self.far = [swap(self.own[j].astype(b16), "dp", j * low) for j in range(1, FAR)]
        return self.far

    def sum(self):
        far = self.fars()
        return self.own[0] + far[0].astype(f32) + far[1].astype(f32) + far[2].astype(f32)


def scatter_any(grad):
    low, far, near = places()
    tower = lax.axis_index("tower")
    halves = grad.reshape((2, FAR, low, -1) + grad.shape[1:])
    got = swap(lax.dynamic_index_in_dim(halves, 1 - tower, 0, keepdims=False), "tower", 1)
    data = add_low(lax.dynamic_index_in_dim(halves, tower, 0, keepdims=False), got)
    blocks = [lax.dynamic_index_in_dim(data, near ^ k, 1, keepdims=False) for k in range(low)]
    bit = low // 2
    while bit:
        blocks = [add_low(blocks[k], swap(blocks[k + bit], "dp", bit)) for k in range(bit)]
        bit //= 2
    own = [lax.dynamic_index_in_dim(blocks[0], far ^ j, 0, keepdims=False) for j in range(FAR)]
    total = own[0].astype(f32)
    for j in range(1, FAR):
        total = total + swap(own[j], "dp", j * low).astype(f32)
    return total


def add_from(x, axis, k):
    return x + swap(x, axis, k)


TILE = 256
PACK = 16
PAIR = 2 * HEAD_DIM
GROUP = 6
Q_BIAS, V_BIAS, O_BIAS, GAIN_1, SHIFT_1, D_BIAS, GAIN_2, SHIFT_2 = range(8)


def dot(a, b):
    return jnp.dot(a, b, preferred_element_type=f32)


def dot_nt(a, b):
    return lax.dot_general(a, b, (((1,), (1,)), ((), ())), preferred_element_type=f32)


def dot_tn(a, b):
    return lax.dot_general(a, b, (((0,), (0,)), ((), ())), preferred_element_type=f32)


def tile_at(t):
    return pl.ds(pl.multiple_of(t * TILE, TILE), TILE)


def sentence_rows(offs, b, seq):
    return pl.ds(pl.multiple_of(offs[b], PACK), seq)


def split_heads(x):
    left = lax.broadcasted_iota(jnp.int32, x.shape, 1) < HEAD_DIM
    zero = jnp.zeros_like(x)
    return jnp.concatenate([jnp.where(left, x, zero), jnp.where(left, zero, x)], 0)


def join_heads(x):
    seq = x.shape[0] // 2
    left = lax.broadcasted_iota(jnp.int32, (seq, PAIR), 1) < HEAD_DIM
    return jnp.where(left, x[:seq], x[seq:])


def by_head(fn, x):
    half = x.shape[0] // 2
    return jnp.concatenate([fn(x[:half]), fn(x[half:])], 0)


def pair_lanes(base, p):
    at = base + p * PAIR
    return slice(at, at + PAIR) if isinstance(p, int) else pl.ds(pl.multiple_of(at, PAIR), PAIR)


def pair_rows(p, size):
    return slice(p * size, (p + 1) * size) if isinstance(p, int) else pl.ds(pl.multiple_of(p * size, PAIR), size)


def over_pairs(count, looped, step):
    def one(g, _):
        step(g * GROUP)
        return 0

    if looped:
        lax.fori_loop(0, count // GROUP, one, 0)
    else:
        for first in range(0, count, GROUP):
            step(first)


def by_length(lens, count, seq, step):
    def one(b, _):
        @pl.when(lens[b] > seq // 2)
        def _():
            step(b, seq)

        @pl.when(lens[b] <= seq // 2)
        def _():
            step(b, seq // 2)

        return 0

    lax.fori_loop(0, count, one, 0)


def norm_rows(hidden):
    center = hidden - jnp.mean(hidden, axis=-1, keepdims=True)
    inverse = lax.rsqrt(jnp.mean(center * center, axis=-1, keepdims=True) + eps_norm)
    return center * inverse, inverse


def norm_back(upstream, normal, inverse, gain):
    scaled = upstream * gain
    inner = scaled - jnp.mean(scaled, axis=-1, keepdims=True)
    return inverse * (inner - normal * jnp.mean(scaled * normal, axis=-1, keepdims=True))


def row_of(vec, i):
    return vec[i : i + 1, :].astype(f32)


def add_row(sums, i, x):
    sums[i : i + 1, :] += jnp.sum(x, axis=0, keepdims=True)


def parts_kernel(place, wqkv, wout, wup, wdown, packed, first, second, third):
    def put(src, dst, at):
        rows, half = src.shape[0], src.shape[1] // 2
        for c in range(half // CHUNK):
            dst[at : at + rows, :] = src[:, pl.ds(pl.multiple_of(place[0] * half + c * CHUNK, 128), CHUNK)]
            at += rows
        return at

    first[put(wqkv, first, 0) :, :] = packed[...]
    put(wup, second, put(wout, second, 0))
    put(wdown, third, 0)


def fetch(place, pieces, targets, sems):
    copies, at = [], 0
    half = FAR // 2
    for weight, rows in targets:
        cols = weight.shape[2] // 2
        for side in range(2):
            tower = place[0] if side == 0 else 1 - place[0]
            block, by_one, by_two, low, high = pieces[5 * side : 5 * side + 5]
            spots = (
                (block, 0, 0, FAR), (by_one, 1, 0, FAR), (by_two, 2, 0, FAR), (low, 3, 0, half), (high, 3, half, half)
            )
            for piece, k, far, size in spots:
                for c in range(cols // CHUNK):
                    row = pl.multiple_of((place[1] ^ k) * rows, PACK)
                    col = pl.multiple_of(tower * cols + c * CHUNK, 128)
                    copies.append(
                        pltpu.make_async_copy(
                            piece.at[:, pl.ds(at + c * rows, rows), :],
                            weight.at[pl.ds(far, size), pl.ds(row, rows), pl.ds(col, CHUNK)],
                            sems.at[len(copies)],
                        )
                    )
        at += cols // CHUNK * rows
    return copies


def deal(place, acc, outs, base=0):
    cols = acc.shape[1]
    if len(outs) == 1:
        outs[0][:, base : base + cols] = acc[...].astype(b16)
        return
    mine, first, rest = outs
    rows = first.shape[1]
    for own in (False, True):
        side = place[0] if own else 1 - place[0]
        for k in range(4):
            target = mine.at[k] if own else first if k == 3 else rest.at[k]

            def block(j, _):
                at = (side * 4 * FAR + (place[2] ^ j) * 4 + (place[1] ^ k)) * rows
                target[j, :, base : base + cols] = acc[pl.ds(pl.multiple_of(at, 8), rows), :].astype(b16)
                return 0

            lax.fori_loop(0, FAR, block, 0)


def flat_of(weight, cols=slice(None)):
    block = weight[:, :, cols]
    return block.reshape(block.shape[0] * block.shape[1], block.shape[2])


def attend_kernel(n_pieces, lens, offs, tiles, place, homes, vec, x_h, y_h, *refs):
    pieces, refs = refs[:n_pieces], refs[n_pieces:]
    if n_pieces:
        wqkv_h, *sinks, x, xs, qkv, probs, ctx, sems, wqkv, got = refs
        copies = fetch(place, pieces, ((wqkv, wqkv.shape[1] // 4),), got)
        for copy in copies:
            copy.start()
    else:
        wqkv, *sinks, x, xs, qkv, probs, ctx, sems = refs
        copies = []
    xs_h, qkv_h, probs_h, ctx_h = sinks
    count, seq, width = x.shape

    def tokens(b, size, do):
        for side, source in enumerate((x_h, y_h)):

            @pl.when(homes[b] == side)
            def _():
                at = pl.ds(0, size)
                do(pltpu.make_async_copy(source.at[homes[count + b], at], x.at[b, at], sems.at[0, b]))

    by_length(lens, count, seq, lambda b, size: tokens(b, size, lambda copy: copy.start()))
    xs[...] = jnp.zeros_like(xs)
    ctx[...] = jnp.zeros_like(ctx)
    by_length(lens, count, seq, lambda b, size: tokens(b, size, lambda copy: copy.wait()))

    def pack(b, _):
        def block(i, _):
            at = pl.multiple_of(offs[b] + i * PACK, PACK)
            xs[pl.ds(at, PACK), :] = x[b, pl.ds(pl.multiple_of(i * PACK, PACK), PACK), :]
            return 0

        return lax.fori_loop(0, (lens[b] + PACK - 1) // PACK, block, 0)

    lax.fori_loop(0, count, pack, 0)

    def leave(source, target, which, do):
        def one(i, _):
            at = pl.ds(pl.multiple_of(i * seq, seq), seq)
            do(pltpu.make_async_copy(source.at[at], target.at[at], sems.at[which, i]))
            return 0

        lax.fori_loop(0, tiles[0] * (TILE // seq) + 1, one, 0)

    def probs_of(b, size):
        at = pl.ds(0, HEADS * size)
        return pltpu.make_async_copy(probs.at[b, at], probs_h.at[b, at], sems.at[4, b])

    leave(xs, xs_h, 1, lambda copy: copy.start())
    for copy in copies:
        copy.wait()
    if n_pieces:
        out = pltpu.make_async_copy(wqkv, wqkv_h, sems.at[5, 0])
        out.start()

    def project(t, _):
        x = xs[tile_at(t), :]
        for c in range(3):
            cols = slice(c * width, (c + 1) * width)
            joined = dot(x, flat_of(wqkv, cols))
            if c == 0:
                joined = (joined + row_of(vec, Q_BIAS)) * (HEAD_DIM ** -0.5)
            if c == 2:
                joined = joined + row_of(vec, V_BIAS)
            qkv[tile_at(t), cols] = joined.astype(b16)
        return 0

    lax.fori_loop(0, tiles[0], project, 0)
    qkv[pl.ds(pl.multiple_of(tiles[0] * TILE, TILE), seq), :] = jnp.zeros((seq, 3 * width), b16)
    leave(qkv, qkv_h, 2, lambda copy: copy.start())

    def attend(b, size):
        rows, key_rows = sentence_rows(offs, b, seq), sentence_rows(offs, b, size)
        valid = lax.broadcasted_iota(jnp.int32, (size, seq), 0) < lens[b]

        def softmax(s):
            s = jnp.where(valid, s, -1000000000.0)
            e = jnp.exp(s - jnp.max(s, axis=0, keepdims=True))
            return (e * (1.0 / jnp.sum(e, axis=0, keepdims=True))).astype(b16)

        def pairs(group):
            spots = range(GROUP)
            queries = [qkv[rows, pair_lanes(0, group + i)] for i in spots]
            keys = [split_heads(qkv[key_rows, pair_lanes(width, group + i)]) for i in spots]
            vals = [split_heads(qkv[key_rows, pair_lanes(2 * width, group + i)]) for i in spots]
            scores = [dot_nt(k, q) for k, q in zip(keys, queries)]
            lows = [by_head(softmax, s) for s in scores]
            outs = [dot_tn(low, v).astype(b16) for low, v in zip(lows, vals)]
            for i, low, out in zip(spots, lows, outs):
                probs[b, pair_rows(group + i, 2 * size), :] = low
                ctx[rows, pair_lanes(0, group + i)] = out

        over_pairs(width // PAIR, size == seq, pairs)
        probs_of(b, size).start()

    by_length(lens, count, seq, attend)
    leave(ctx, ctx_h, 3, lambda copy: copy.start())
    leave(xs, xs_h, 1, lambda copy: copy.wait())
    leave(qkv, qkv_h, 2, lambda copy: copy.wait())
    leave(ctx, ctx_h, 3, lambda copy: copy.wait())
    by_length(lens, count, seq, lambda b, size: probs_of(b, size).wait())
    if n_pieces:
        out.wait()


def inside(offs, lens, b, t):
    row = t * TILE + lax.broadcasted_iota(jnp.int32, (TILE, 1), 0)
    return (row >= offs[b]) & (row < offs[b] + lens[b])


def take_weights(step, place, pieces, refs, count, rows):
    if not pieces:
        return refs[:count], refs[count:], lambda: None, lambda: None
    sinks, refs = refs[:count], refs[count:]
    held, got, sent, refs = refs[-count - 2 : -2], refs[-2], refs[-1], refs[: -count - 2]
    leave = [pltpu.make_async_copy(a, b, sent.at[i]) for i, (a, b) in enumerate(zip(held, sinks))]

    copies = fetch(place, pieces, [(weight, rows) for weight in held], got)
    first = held[0].shape[2] // CHUNK * 5

    @pl.when(step == 0)
    def _():
        for copy in copies:
            copy.start()
        for copy in copies[:first]:
            copy.wait()

    def others():
        @pl.when(step == 0)
        def _():
            for copy in copies[first:]:
                copy.wait()
            for copy in leave:
                copy.start()

    def finish():
        @pl.when(step == pl.num_programs(0) - 1)
        def _():
            for copy in leave:
                copy.wait()

    return held, refs, others, finish


def up_kernel(n_pieces, rows, lens, offs, tiles, place, ctx, xs, vec, ups, *refs):
    t = pl.program_id(0)
    pieces, refs = refs[:n_pieces], refs[n_pieces:]
    (wout, wup), (act, slope, n1, inv1), others, finish = take_weights(t, place, pieces, refs, 2, rows)
    width = n1.shape[1]

    @pl.when(t < tiles[0])
    def _():
        attended = dot(ctx[...], flat_of(wout)) + row_of(vec, O_BIAS)
        normal, inverse = norm_rows(xs[...].astype(f32) + attended)
        n1[...] = normal
        inv1[...] = jnp.broadcast_to(inverse, (TILE, 128))
        low = (normal * row_of(vec, GAIN_1) + row_of(vec, SHIFT_1)).astype(b16)
        others()

        def chunk(c, _):
            cols = pl.ds(pl.multiple_of(c * width, width), width)
            pre = dot(low, flat_of(wup, cols)) + ups[pl.ds(c, 1), :]
            half = 0.5 * (1.0 + lax.erf(pre * (0.5 ** 0.5)))
            act[:, cols] = (pre * half).astype(b16)
            slope[:, cols] = (half + pre * (jnp.exp(-0.5 * pre * pre) * 0.3989422804014327)).astype(b16)
            return 0

        lax.fori_loop(0, ups.shape[0], chunk, 0)

    finish()


def down_kernel(n_pieces, rows, lens, offs, tiles, place, n1, act, vec, *refs):
    t = pl.program_id(0)
    pieces, refs = refs[:n_pieces], refs[n_pieces:]
    (wdown,), (n2, inv2, pooled), others, finish = take_weights(t, place, pieces, refs, 1, rows)
    others()
    width = n1.shape[1]
    count = pooled.shape[0]

    @pl.when(t == 0)
    def _():
        pooled[...] = jnp.zeros_like(pooled)

    @pl.when(t < tiles[0])
    def _():
        total = n1[...] * row_of(vec, GAIN_1) + row_of(vec, SHIFT_1) + row_of(vec, D_BIAS)
        total = total + dot(act[...], flat_of(wdown))
        normal, inverse = norm_rows(total)
        n2[...] = normal
        inv2[...] = jnp.broadcast_to(inverse, (TILE, 128))
        for b in range(count):
            add_row(pooled, b, jnp.where(inside(offs, lens, b, t), normal, 0.0))

    @pl.when(t == pl.num_programs(0) - 1)
    def _():
        for b in range(count):
            size = jnp.full((1, width), lens[b], jnp.int32).astype(f32)
            pooled[b : b + 1, :] = pooled[b : b + 1, :] / size * row_of(vec, GAIN_2) + row_of(vec, SHIFT_2)

    finish()


def accumulate(t, acc, cols, left, right):
    @pl.when(t == 0)
    def _():
        acc[:, cols] = dot_tn(left, right)

    @pl.when(t > 0)
    def _():
        acc[:, cols] += dot_tn(left, right)


def pair_head(lens, place, homes, labels, bias, pooled, partner, head, tops, own, ends):
    count, width = pooled.shape

    for side in range(2):
        for i in range(count):
            at = side * count + i
            away, slot = homes[2 * count + at], homes[4 * count + at]
            row = jnp.where(away == 0, pooled[pl.ds(slot, 1), :], partner[pl.ds(slot, 1), :])
            ends[side, i : i + 1, :] = row
    left, right = ends[0], ends[1]
    own[...] = jnp.where(place[0] == 0, left, right)
    gap = left - right
    soft = jnp.sqrt(gap * gap + gap_soft)
    feats = (left, right, soft)
    row = lax.broadcasted_iota(jnp.int32, (count, 1), 0)
    label = jnp.zeros((count, 1), jnp.int32)
    for b in range(count):
        label = jnp.where(row == b, labels[b], label)
    logits = []
    for c in range(NCLASS):
        terms = [
            jnp.sum(feats[i] * head[c : c + 1, i * width : (i + 1) * width], axis=-1, keepdims=True) for i in range(3)
        ]
        logits.append(terms[0] + terms[1] + terms[2] + bias[c])
    top = jnp.maximum(jnp.maximum(logits[0], logits[1]), logits[2])
    exps = [jnp.exp(x - top) for x in logits]
    norm = exps[0] + exps[1] + exps[2]
    grads = [exps[c] / norm - jnp.where(label == c, 1.0, 0.0) for c in range(NCLASS)]
    back = []
    tops[...] = jnp.zeros_like(tops)
    for i in range(3):
        cols = slice(i * width, (i + 1) * width)
        back.append(sum(grads[c] * head[c : c + 1, cols] for c in range(NCLASS)))
        for c in range(NCLASS):
            tops[c : c + 1, cols] = 0.5 * jnp.sum(grads[c] * feats[i], axis=0, keepdims=True)
    for c in range(NCLASS):
        tops[NCLASS + c : NCLASS + c + 1, 0:128] = jnp.broadcast_to(0.5 * jnp.sum(grads[c], axis=0, keepdims=True), (1, 128))
    slope = gap / soft
    ends[0] = back[0] + slope * back[2]
    ends[1] = back[1] - slope * back[2]
    for b in range(count):
        side = jnp.where(homes[b] == 0, place[0], 1 - place[0])
        row = ends[side, pl.ds(homes[count + b], 1), :]
        size = jnp.full((1, width), lens[b], jnp.int32).astype(f32)
        ends[2, b : b + 1, :] = row / size


def down_back_kernel(
    lens, offs, tiles, place, homes, labels, bias, pooled, partner, head, act, n2, inv2, vec, sum_grad, *refs
):
    *outs, sums, tops, own, acc, ends = refs
    t = pl.program_id(0)
    count, width = pooled.shape

    @pl.when(t == 0)
    def _():
        pair_head(lens, place, homes, labels, bias, pooled, partner, head, tops, own, ends)
        sums[...] = jnp.zeros_like(sums)

    @pl.when(t < tiles[0])
    def _():
        up = jnp.zeros((TILE, width), f32)
        for b in range(count):
            up = jnp.where(inside(offs, lens, b, t), ends[2, b : b + 1, :], up)
        normal = n2[...]
        grad = norm_back(up, normal, inv2[:, 0:1], row_of(vec, GAIN_2))
        sum_grad[...] = grad
        add_row(sums, 0, up * normal)
        add_row(sums, 1, up)
        add_row(sums, 2, grad)
        low = grad.astype(b16)

        accumulate(t, acc, slice(None), act[...], low)

    @pl.when(t == pl.num_programs(0) - 1)
    def _():
        deal(place, acc, outs)


def early(t, copies):
    @pl.when(t == 0)
    def _():
        for copy in copies:
            copy.start()

    def ready(i):
        @pl.when(t == 0)
        def _():
            copies[i].wait()

    return ready


def pre_back_kernel(lens, offs, tiles, place, sum_grad, slope, wdown, pre_low, sums):
    t = pl.program_id(0)
    width = sum_grad.shape[1]
    chunks = slope.shape[1] // width
    split = wdown.shape[0] // chunks

    @pl.when(t == 0)
    def _():
        sums[...] = jnp.zeros_like(sums)

    @pl.when(t < tiles[0])
    def _():
        low = sum_grad[...].astype(b16)
        for c in range(chunks):
            cols = slice(c * width, (c + 1) * width)
            pre = dot_nt(low, flat_of(wdown[c * split : (c + 1) * split])) * slope[:, cols].astype(f32)
            add_row(sums, c, pre)
            pre_low[:, cols] = pre.astype(b16)


def mid_back_kernel(
    lens, offs, tiles, place, sum_grad, pre_low, n1, inv1, ctx, wup, wout, vec, mid, ctx_grad, *refs
):
    *outs, sums, acc = refs
    t = pl.program_id(0)
    hidden = pre_low.shape[1]

    @pl.when(t == 0)
    def _():
        sums[...] = jnp.zeros_like(sums)

    @pl.when(t < tiles[0])
    def _():
        pre = pre_low[...]
        grad = sum_grad[...] + dot_nt(pre, flat_of(wup))
        normal = n1[...]
        add_row(sums, 0, grad * normal)
        add_row(sums, 1, grad)
        middle = norm_back(grad, normal, inv1[:, 0:1], row_of(vec, GAIN_1))
        add_row(sums, 2, middle)
        mid[...] = middle
        low = middle.astype(b16)
        ctx_grad[...] = dot_nt(low, flat_of(wout)).astype(b16)
        first_low = (normal * row_of(vec, GAIN_1) + row_of(vec, SHIFT_1)).astype(b16)
        accumulate(t, acc, slice(0, hidden), first_low, pre)
        accumulate(t, acc, slice(hidden, None), ctx[...], low)

    @pl.when(t == pl.num_programs(0) - 1)
    def _():
        deal(place, acc, outs)


def attend_back_kernel(lens, offs, tiles, place, qkv_h, probs_h, ctx_grad_h, grad_h, sums, grad, qkv, probs, ctx_grad, sems):
    width = ctx_grad.shape[1]
    count, seq = probs.shape[0], probs.shape[2]
    blocks = qkv.shape[0] // seq

    def rows_in_use(do):
        for i in range(blocks):

            @pl.when(i * seq < tiles[0] * TILE + seq)
            def _():
                at = pl.ds(i * seq, seq)
                do(pltpu.make_async_copy(qkv_h.at[at], qkv.at[at], sems.at[i]))
                do(pltpu.make_async_copy(ctx_grad_h.at[at], ctx_grad.at[at], sems.at[blocks + i]))

    def probs_of(b, size):
        at = pl.ds(0, HEADS * size)
        return pltpu.make_async_copy(probs_h.at[b, at], probs.at[b, at], sems.at[2 * blocks + b])

    rows_in_use(lambda copy: copy.start())
    by_length(lens, count, seq, lambda b, size: probs_of(b, size).start())
    grad[...] = jnp.zeros_like(grad)
    sums[...] = jnp.zeros_like(sums)
    rows_in_use(lambda copy: copy.wait())

    def attend(b, size):
        rows, key_rows = sentence_rows(offs, b, seq), sentence_rows(offs, b, size)
        real = lax.broadcasted_iota(jnp.int32, (seq, 1), 0) < lens[b]
        probs_of(b, size).wait()

        def spread(x):
            return jnp.broadcast_to(jnp.sum(x, axis=0, keepdims=True), x.shape)

        def pairs(group):
            spots = range(GROUP)
            ups = [jnp.where(real, ctx_grad[rows, pair_lanes(0, group + i)], jnp.zeros((), b16)) for i in spots]
            queries = [qkv[rows, pair_lanes(0, group + i)] for i in spots]
            keys = [split_heads(qkv[key_rows, pair_lanes(width, group + i)]) for i in spots]
            vals = [split_heads(qkv[key_rows, pair_lanes(2 * width, group + i)]) for i in spots]
            lows = [probs[b, pair_rows(group + i, 2 * size), :] for i in spots]
            prob_grads = [dot_nt(v, up) for v, up in zip(vals, ups)]
            val_grads = [join_heads(dot(low, up)).astype(b16) for low, up in zip(lows, ups)]
            scores = []
            for low, pg in zip(lows, prob_grads):
                pr = low.astype(f32)
                scores.append((pr * (pg - by_head(spread, pg * pr))).astype(b16))
            query_grads = [(dot_tn(s, k) * (HEAD_DIM ** -0.5)).astype(b16) for s, k in zip(scores, keys)]
            key_grads = [join_heads(dot(s, q)).astype(b16) for s, q in zip(scores, queries)]
            for i in spots:
                grad[rows, pair_lanes(0, group + i)] = query_grads[i]
                grad[key_rows, pair_lanes(width, group + i)] = key_grads[i]
                grad[key_rows, pair_lanes(2 * width, group + i)] = val_grads[i]

        over_pairs(width // PAIR, size == seq, pairs)

    by_length(lens, count, seq, attend)

    def result(t):
        return pltpu.make_async_copy(grad.at[tile_at(t)], grad_h.at[tile_at(t)], sems.at[2 * blocks + count + t])

    def total(t, _):
        result(t).start()
        for c in (0, 2):
            add_row(sums, c // 2, grad[tile_at(t), c * width : (c + 1) * width].astype(f32))
        return 0

    def finish(t, _):
        result(t).wait()
        return 0

    lax.fori_loop(0, tiles[0], total, 0)
    lax.fori_loop(0, tiles[0], finish, 0)


def input_kernel(lens, offs, tiles, place, homes, grad, mid, xs, biases, wqkv_h, gx, gy, *refs):
    *outs, buf, acc, tail, wqkv, sems = refs
    count, seq, width = gx.shape
    t = pl.program_id(0)
    ready = early(t, [pltpu.make_async_copy(wqkv_h, wqkv, sems.at[0])])

    @pl.when(t == 0)
    def _():
        gx[...] = jnp.zeros_like(gx)
        gy[...] = jnp.zeros_like(gy)

    @pl.when(t < tiles[0])
    def _():
        accumulate(t, acc, slice(None), xs[...], grad[...])
        ready(0)
        buf[tile_at(t), :] = dot_nt(grad[...], flat_of(wqkv)) + mid[...]

    @pl.when(t == pl.num_programs(0) - 1)
    def _():
        def unpack(b, _):
            blocks = (lens[b] + PACK - 1) // PACK
            for side, target in enumerate((gx, gy)):

                def block(i, _):
                    at = pl.multiple_of(offs[b] + i * PACK, PACK)
                    rows = pl.ds(pl.multiple_of(i * PACK, PACK), PACK)
                    target[homes[count + b], rows, :] = buf[pl.ds(at, PACK), :].astype(target.dtype)
                    return 0

                lax.fori_loop(0, jnp.where(homes[b] == side, blocks, 0), block, 0)
            return 0

        lax.fori_loop(0, count, unpack, 0)
        deal(place, acc, outs)
        if len(outs) > 1:
            cols, lanes = acc.shape[1], tail.shape[1]
            each = biases.shape[1] // lanes
            tail[...] = jnp.zeros_like(tail)
            for r in range(2 * each):
                tail[r : r + 1, :] = biases[r // each : r // each + 1, r % each * lanes : (r % each + 1) * lanes]
            block = tail[...].astype(b16)
            mine, first, rest = outs
            for target in [mine.at[k] for k in range(4)] + [first] + [rest.at[k] for k in range(3)]:
                for spot in range(FAR):
                    target[spot, :, cols : cols + lanes] = block


def small_kernel(spot, sums, tail, *outs):
    width = sums.shape[1] // 3
    *plain, ups, head, classes = outs
    mine = plain[0].shape[1]

    def share(x, size):
        x = jnp.broadcast_to(x, (8, x.shape[1])) if x.shape[0] == 1 else x
        return pltpu.roll(x, lax.rem(x.shape[1] - spot[0] * size, x.shape[1]), axis=1)[:, 0:size]

    count = width // tail.shape[1]
    for p in range(2):
        row = jnp.concatenate([tail[p * count + r : p * count + r + 1, :] for r in range(count)], 1)
        plain[p][...] = share(row, mine)[0:1]
    blocks = [share(sums[0:8, p * width : (p + 1) * width], mine) for p in (0, 2)]
    for out, (block, row) in zip(plain[2:], ((1, 2), (1, 0), (1, 1), (0, 2), (0, 0), (0, 1))):
        out[...] = blocks[block][row : row + 1]
    ups[...] = share(jnp.concatenate([sums[r : r + 1, width : 2 * width] for r in range(4)], 1), 4 * mine)[0:1]
    head[...] = share(sums[8:16, :], 3 * mine)[0:NCLASS]
    classes[...] = jnp.transpose(sums[8:16, 0:128])[0:1, NCLASS : 2 * NCLASS]


class Tiled:
    def __init__(self, array):
        self.array = array


class Flat:
    def __init__(self, array):
        self.array = array


class Scalars:
    def __init__(self, array):
        self.array = array


def spec_of(x):
    if isinstance(x, Scalars):
        return pl.BlockSpec(memory_space=pltpu.SMEM)
    if isinstance(x, Flat):
        return pl.BlockSpec(memory_space=pl.ANY)
    if isinstance(x, Tiled):
        return pl.BlockSpec((TILE, x.array.shape[1]), lambda i, lens, offs, tiles, place: (jnp.minimum(i, tiles[0] - 1), 0))
    return pl.BlockSpec(x.shape, lambda *_: (0,) * len(x.shape), pipeline_mode=pl.Buffered(1))


def bare(x):
    return x.array if isinstance(x, (Tiled, Flat, Scalars)) else x


def shape(dtype, *dims):
    return jax.ShapeDtypeStruct(dims, dtype)


def call(kernel, meta, args, outs, scratch=(), steps=1, micros=0):
    moved = sum(bare(a).size * bare(a).dtype.itemsize for a in (*args, *outs))
    return pl.pallas_call(
        kernel,
        out_shape=[bare(o) for o in outs],
        grid_spec=pltpu.PrefetchScalarGridSpec(
            num_scalar_prefetch=len(meta),
            grid=(steps,),
            in_specs=[spec_of(a) for a in args],
            out_specs=[spec_of(o) for o in outs],
            scratch_shapes=list(scratch),
        ),
        cost_estimate=pl.CostEstimate(flops=int(micros * 1.15e9), transcendentals=0, bytes_accessed=moved),
        compiler_params=pltpu.CompilerParams(vmem_limit_bytes=58 << 20),
    )(*meta, *[bare(a) for a in args])


def pack_small(vectors):
    total = sum(v.shape[0] for v in vectors)
    rows = -(-total // (8 * CHUNK)) * 8
    at, flat = 0, 0.0
    for v in vectors:
        flat = flat + jnp.pad(v.astype(f32), (at, rows * CHUNK - at - v.shape[0]))
        at += v.shape[0]
    return flat.astype(b16).reshape(rows, CHUNK)


def body(
    embeddings, lengths, labels, qkv_weight, query_bias, value_bias, out_weight, out_bias, attn_gain,
    attn_shift, up_weight, up_bias, down_weight, down_bias, ffn_gain, ffn_shift, head_weight, head_bias,
):
    width = embeddings.shape[-1]
    seq_len = embeddings.shape[2]
    count = embeddings.shape[1]
    rows = -(-count * seq_len // TILE) * TILE
    hidden = up_weight.shape[1]
    groups = lax.axis_size("dp")
    low, far, near = places()
    tower = lax.axis_index("tower")
    shard_rows = qkv_weight.shape[0]
    quick = low == 4 and shard_rows % PACK == 0

    other_len = swap(lengths[0].astype(f32), "tower", 1).astype(jnp.int32)
    first_here = tower == 0
    all_len = jnp.where(
        first_here, jnp.concatenate([lengths[0], other_len]), jnp.concatenate([other_len, lengths[0]])
    )
    ids = jnp.arange(2 * count)
    ahead = (all_len[None, :] > all_len[:, None]) | (
        (all_len[None, :] == all_len[:, None]) & (ids[None, :] < ids[:, None])
    )
    rank = jnp.sum(ahead.astype(jnp.int32), axis=1)
    away = (((rank + 1) // 2) % 2 != tower).astype(jnp.int32)
    picked = (away[None, :] == 0) & (rank[None, :] // 2 == jnp.arange(count)[:, None])
    source = jnp.sum(jnp.where(picked, ids[None, :], 0), axis=1)
    sent_len = jnp.sum(jnp.where(picked, all_len[None, :], 0), axis=1)
    homes = jnp.concatenate([(source // count != tower).astype(jnp.int32), source % count, away, rank // 2])
    homes = homes.astype(jnp.int32)

    taken = (sent_len + PACK - 1) // PACK * PACK
    before = jnp.arange(count)[None, :] < jnp.arange(count)[:, None]
    offs = jnp.sum(jnp.where(before, taken[None, :], 0), axis=1)
    tiles = (jnp.sum(taken)[None] + TILE - 1) // TILE
    place = jnp.stack([tower, near, far]).astype(jnp.int32)
    meta = (sent_len, offs, tiles, place)
    steps = rows // TILE

    packed = pack_small((
        query_bias, value_bias, out_bias, attn_gain, attn_shift, down_bias, ffn_gain, ffn_shift, up_bias,
        head_weight.reshape(-1),
    ))
    weights = (qkv_weight, out_weight, up_weight, down_weight)
    if quick:
        sizes = [w.size // 2 // CHUNK for w in weights]
        first_part, up_part, down_part = call(
            parts_kernel, (place,), (*weights, packed),
            (
                shape(b16, sizes[0] + packed.shape[0], CHUNK), shape(b16, sizes[1] + sizes[2], CHUNK),
                shape(b16, sizes[3], CHUNK),
            ),
        )
    else:
        first_part = jnp.concatenate([to_chunks(qkv_weight), packed], 0)
        up_part, down_part = jnp.concatenate([to_chunks(out_weight), to_chunks(up_weight)], 0), to_chunks(down_weight)
    cut = first_part.shape[0] - packed.shape[0]
    low_far = far_pieces(first_part)
    other_tokens = swap(embeddings[0], "tower", 1)
    low_far = after(low_far, other_tokens, homes)
    block_first = in_order(low_far, far, 0)
    far_up = far_pieces(after(up_part, *low_far))
    full = [(FAR, w.shape[0] * low, w.shape[1]) for w in weights]
    if quick:
        near_first = gather_near(block_first)
        far_up = after(far_up, *near_first[3:])
        block_up = in_order(far_up, far, 0)
        far_down = far_pieces(after(down_part, *far_up))
        pieces_first = near_first + [swap(p, "tower", 1) for p in near_first]
        tails = [p[:, cut:] for p in near_first]
        packs = in_order(tails[:3] + [jnp.concatenate(tails[3:], 0)], near, 1)
    else:
        block_up = in_order(far_up, far, 0)
        far_down = far_pieces(down_part)
        whole_first = gather_any(block_first)
        pieces_first = [from_chunks(whole_first[:, :, :cut], shard_rows)]
        packs = whole_first[:, :, cut:]
    packs = packs.reshape(groups, -1).astype(f32)
    cuts = [8 * shard_rows, 8 * shard_rows + up_bias.shape[0]]
    cuts.append(cuts[1] + head_weight.size)
    vec = packs[:, : cuts[0]].reshape(groups, 8, shard_rows).transpose(1, 0, 2).reshape(8, width)
    ups = packs[:, cuts[0] : cuts[1]].reshape(-1, width)
    head_rows = packs[:, cuts[1] : cuts[2]].reshape(-1, NCLASS).T

    ext = rows + seq_len
    dense = 2 * rows * width
    sinks = [
        Flat(shape(b16, ext, width)), Flat(shape(b16, ext, 3 * width)),
        Flat(shape(b16, count, HEADS * seq_len, seq_len)), Flat(shape(b16, ext, width)),
    ]
    scratch = [pltpu.VMEM((count, seq_len, width), b16)]
    scratch += [pltpu.VMEM(o.array.shape, o.array.dtype) for o in sinks]
    scratch.append(pltpu.SemaphoreType.DMA((6, max(ext // seq_len, count))))
    if quick:
        both = [Flat(shape(b16, *full[0]))] + sinks
        pieces_first = after(pieces_first, block_up)
        proj_qkv, xs, qkv, probs, ctx = call(
            partial(attend_kernel, 10), meta,
            (Scalars(homes), vec, Flat(embeddings[0]), Flat(other_tokens), *map(Flat, pieces_first)), both,
            scratch + [pltpu.VMEM(full[0], b16), pltpu.SemaphoreType.DMA((30,))],
            micros=4,
        )
    else:
        (proj_qkv,) = pieces_first
        xs, qkv, probs, ctx = call(
            partial(attend_kernel, 0), meta, (Scalars(homes), vec, Flat(embeddings[0]), Flat(other_tokens), proj_qkv), sinks,
            scratch,
            micros=4,
        )

    wide, slim, thin = shape(b16, rows, hidden), shape(f32, rows, width), shape(f32, rows, 128)
    outs = [Tiled(wide), Tiled(wide), Tiled(slim), Tiled(thin)]
    args = Tiled(ctx), Tiled(xs), vec, ups
    if quick:
        near_up = gather_near(block_up, ctx)
        block_down = in_order(after(far_down, ctx), far, 0)
        pieces_up = near_up + [swap(p, "tower", 1) for p in near_up]
        proj_out, proj_up, act, slope, n1, inv1 = call(
            partial(up_kernel, 10, shard_rows), meta, (*args, *map(Flat, pieces_up)),
            [Flat(shape(b16, *full[1])), Flat(shape(b16, *full[2]))] + outs,
            [
                pltpu.VMEM(full[1], b16), pltpu.VMEM(full[2], b16), pltpu.SemaphoreType.DMA((50,)),
                pltpu.SemaphoreType.DMA((2,)),
            ],
            steps=steps, micros=14,
        )
    else:
        whole_up = gather_any(block_up)
        cut = out_weight.size // 2 // CHUNK
        proj_out = from_chunks(whole_up[:, :, :cut], shard_rows)
        proj_up = from_chunks(whole_up[:, :, cut:], shard_rows)
        act, slope, n1, inv1 = call(
            partial(up_kernel, 0, 0), meta, (*args, proj_out, proj_up), outs, steps=steps, micros=14,
        )
    outs = [Tiled(slim), Tiled(thin), shape(f32, count, width)]
    if quick:
        near_down = gather_near(block_down, act)
        pieces_down = near_down + [swap(p, "tower", 1) for p in near_down]
        proj_down, n2, inv2, pooled = call(
            partial(down_kernel, 10, down_weight.shape[0]), meta, (Tiled(n1), Tiled(act), vec, *map(Flat, pieces_down)),
            [Flat(shape(b16, *full[3]))] + outs,
            [pltpu.VMEM(full[3], b16), pltpu.SemaphoreType.DMA((10,)), pltpu.SemaphoreType.DMA((1,))],
            steps=steps, micros=10,
        )
    else:
        proj_down = from_chunks(gather_any(in_order(far_down, far, 0)), down_weight.shape[0])
        n2, inv2, pooled = call(
            partial(down_kernel, 0, 0), meta, (Tiled(n1), Tiled(act), vec, proj_down), outs, steps=steps, micros=10,
        )

    def dealt(full_rows, cols):
        if quick:
            block = FAR, full_rows // (8 * FAR), cols
            return [shape(b16, 4, *block), shape(b16, *block), shape(b16, 3, *block)]
        return [shape(b16, full_rows, cols)]

    partner = swap(pooled, "tower", 1)
    sums_of = shape(f32, 8, width)
    sum_grad, *down_parts, sums_two, tops, own_pooled = call(
        down_back_kernel, meta,
        (
            Scalars(homes), Scalars(labels), Scalars(head_bias.astype(f32)), pooled, partner, head_rows, Tiled(act), Tiled(n2),
            Tiled(inv2), vec,
        ),
        [Tiled(slim)] + dealt(hidden, width) + [sums_of, shape(f32, 8, 3 * width), shape(f32, count, width)],
        [pltpu.VMEM((hidden, width), f32), pltpu.VMEM((3, count, width), f32)], steps=steps, micros=11,
    )
    if quick:
        down = Scatter(down_parts)
        sum_grad = after(sum_grad, down.first)
    pre_low, sums_up = call(
        pre_back_kernel, meta, (Tiled(sum_grad), Tiled(slope), proj_down), [Tiled(wide), sums_of], steps=steps,
        micros=8,
    )
    if quick:
        pre_low = after(pre_low, down.corners(), down.rest)
    mid, ctx_grad, *up_parts, sums_one = call(
        mid_back_kernel, meta,
        (Tiled(sum_grad), Tiled(pre_low), Tiled(n1), Tiled(inv1), Tiled(ctx), proj_up, proj_out, vec),
        [Tiled(slim), Tiled(shape(b16, ext, width))] + dealt(width, hidden + width) + [sums_of],
        [pltpu.VMEM((width, hidden + width), f32)], steps=steps, micros=20,
    )
    summed = jnp.concatenate([jnp.concatenate([sums_two, sums_up, sums_one], 1), tops], 0)
    came = swap(summed, "tower", 1)
    if quick:
        up = Scatter(after(up_parts, down.sides()))
        up.sides()
        ctx_grad = after(ctx_grad, came, *up.corner, *up.sent)
    qkv_grad, sums_in = call(
        attend_back_kernel, meta, (Flat(qkv), Flat(probs), Flat(ctx_grad)), [Flat(shape(b16, ext, 3 * width)), sums_of],
        [
            pltpu.VMEM(qkv.shape, b16), pltpu.VMEM(qkv.shape, b16), pltpu.VMEM(probs.shape, b16), pltpu.VMEM(ctx_grad.shape, b16),
            pltpu.SemaphoreType.DMA((2 * (ext // seq_len) + count + steps,)),
        ],
        micros=14,
    )
    summed = after(summed + came, qkv_grad)
    came = swap(summed, "dp", low)
    if quick:
        mid = after(mid, qkv_grad, *up.side, *down.fars())
        up.fars()
    lanes = 128
    last_cols = 3 * width + (lanes if quick else 0)
    grad_in, grad_away, *last_parts = call(
        input_kernel, meta, (Scalars(homes), Tiled(qkv_grad), Tiled(mid), Tiled(xs), sums_in, Flat(proj_qkv)),
        [shape(f32, count, seq_len, width), shape(b16, count, seq_len, width)] + dealt(width, last_cols),
        [pltpu.VMEM((rows, width), f32), pltpu.VMEM((width, 3 * width), f32), pltpu.VMEM((24, lanes), f32),
         pltpu.VMEM(full[0], b16), pltpu.SemaphoreType.DMA((1,))],
        steps=steps, micros=16,
    )
    if quick:
        last_parts, up.far, came = after((last_parts, up.far, came))
    summed = summed + came
    came = swap(summed, "dp", 2 * low)
    if quick:
        last = Scatter(last_parts)
        last.sides()
        came = after(came, *last.sent)
        grad_in = grad_in + swap(after(grad_away, *last.corner), "tower", 1).astype(f32)
        last.far = after(last.fars(), grad_in)
        down_out, up_out, last_out = down.sum(), up.sum(), last.sum()
        tail, last_out = last_out[:, 3 * width :], last_out[:, : 3 * width]
    else:
        grad_in = grad_in + swap(grad_away, "tower", 1).astype(f32)
        down_out, up_out, last_out = (scatter_any(*p) for p in (down_parts, up_parts, last_parts))
        tail, bit = add_from(sums_in[0:2].reshape(-1, lanes), "tower", 1), 1
        while bit < groups:
            tail = add_from(tail, "dp", bit)
            bit *= 2
    summed, bit = summed + came, 1
    while bit < low:
        came = swap(summed, "dp", bit)
        if quick and bit == 1:
            came = after(came, *last.side)
        summed, bit = summed + came, 2 * bit
    spot = (tower * groups + lax.axis_index("dp")).astype(jnp.int32)[None]
    mine = width // (2 * groups)
    *plain, up_bias_sum, head_sum, class_sum = pl.pallas_call(
        small_kernel,
        out_shape=[shape(f32, 1, mine)] * 8
        + [shape(f32, 1, 4 * mine), shape(f32, NCLASS, 3 * mine), shape(f32, 1, NCLASS)],
        in_specs=[pl.BlockSpec(memory_space=pltpu.SMEM)] + [pl.BlockSpec(memory_space=pltpu.VMEM)] * 2,
        out_specs=[pl.BlockSpec(memory_space=pltpu.VMEM)] * 11,
    )(spot, summed, tail)
    q_sum, v_sum, o_sum, gain_one, shift_one, d_sum, gain_two, shift_two = [x.reshape(-1) for x in plain]
    return (
        own_pooled[None],
        grad_in[None],
        last_out,
        q_sum, v_sum,
        up_out[:, hidden:],
        o_sum, gain_one, shift_one,
        up_out[:, :hidden],
        up_bias_sum.reshape(-1),
        down_out,
        d_sum, gain_two, shift_two,
        head_sum.T,
        class_sum.reshape(-1),
    )


def solution(mesh):
    rows, vec = P("dp", None), P("dp")
    out_rows, out_vec = P(("tower", "dp"), None), P(("tower", "dp"))
    return jax.shard_map(
        body,
        mesh=mesh,
        in_specs=(
            P("tower", "dp", None, None), P("tower", "dp"), vec,
            rows, vec, vec, rows, vec, vec, vec, rows, vec, rows, vec, vec, vec, rows, P(),
        ),
        out_specs=(
            P("tower", "dp", None), P("tower", "dp", None, None),
            out_rows, out_vec, out_vec, out_rows, out_vec, out_vec, out_vec, out_rows, out_vec, out_rows, out_vec,
            out_vec, out_vec, out_rows, P(),
        ),
        check_vma=False,
    )
```

```python
from functools import partial
import math

import jax
import jax.numpy as jnp
from jax import lax
from jax.experimental import pallas as pl
from jax.experimental.pallas import tpu as pltpu
from jax.sharding import PartitionSpec as P

HEADS = 12
HEAD_DIM = 64
NCLASS = 3
CHUNK = 384
FAR = 4

eps_norm = 1e-12
gap_soft = 0.01
f32 = jnp.float32
b16 = jnp.bfloat16


def swap(x, axis, k):
    return lax.ppermute(x, axis, [(i, i ^ k) for i in range(lax.axis_size(axis))])


def places():
    low = lax.axis_size("dp") // FAR
    me = lax.axis_index("dp")
    return low, me // low, me % low


def in_order(pieces, me, axis):
    stack = jnp.stack(pieces, axis)
    return jnp.concatenate(
        [lax.dynamic_index_in_dim(stack, me ^ j, axis) for j in range(len(pieces))], axis
    )


def far_pieces(part):
    low, _, _ = places()
    return [part] + [swap(part, "dp", j * low) for j in range(1, FAR)]


def after(x, *deps):
    return lax.optimization_barrier((x, *deps))[0]


def gather_near(block, *ready):
    half = FAR // 2
    by_one, by_two = after((swap(block, "dp", 1), swap(block, "dp", 2)), *ready)
    return [block, by_one, by_two, swap(by_one[:half], "dp", 2), swap(by_two[half:], "dp", 1)]


def gather_any(block):
    low, _, near = places()
    pieces, bit = [block], 1
    while bit < low:
        pieces = pieces + [swap(p, "dp", bit) for p in pieces]
        bit *= 2
    return in_order(pieces, near, 1)


def to_chunks(shard):
    rows, cols = shard.shape
    half = cols // 2
    mine = lax.dynamic_slice_in_dim(shard, lax.axis_index("tower") * half, half, 1)
    return mine.reshape(rows, half // CHUNK, CHUNK).transpose(1, 0, 2).reshape(-1, CHUNK)


def from_chunks(mine, rows):
    other = swap(mine, "tower", 1)
    low_half = lax.axis_index("tower") == 0
    both = jnp.stack([jnp.where(low_half, mine, other), jnp.where(low_half, other, mine)])
    far, low, total = mine.shape[:3]
    n = total // rows
    both = both.reshape(2, far, low, n, rows, CHUNK).transpose(1, 2, 4, 0, 3, 5)
    return both.reshape(far, low * rows, 2 * n * CHUNK)


def add_low(a, b):
    return (a.astype(f32) + b.astype(f32)).astype(b16)


class Scatter:
    def __init__(self, parts):
        self.mine, *others = parts
        self.first = swap(others[0], "tower", 1)
        self.rest = swap(after(others[1], self.first), "tower", 1)
        self.corner = self.side = self.far = None

    def both(self, k, part=slice(None)):
        got = self.first[part] if k == 3 else self.rest[k, part]
        return self.mine[k, part].astype(f32) + got.astype(f32)

    def corners(self):
        if self.corner is None:
            half = FAR // 2
            self.corner = (
                swap(self.both(3, slice(0, half)).astype(b16), "dp", 1),
                swap(self.both(3, slice(half, FAR)).astype(b16), "dp", 2),
            )
        return self.corner

    def sides(self):
        if self.side is None:
            half = FAR // 2
            for_one, for_two = (x.astype(f32) for x in self.corners())
            none = ((0, 0), (0, 0))
            one = self.both(1) + jnp.pad(for_two, ((half, 0), *none))
            two = self.both(2) + jnp.pad(for_one, ((0, half), *none))
            self.sent = one.astype(b16), two.astype(b16)
            self.side = swap(self.sent[0], "dp", 1), swap(self.sent[1], "dp", 2)
        return self.side

    def fars(self):
        if self.far is None:
            low = lax.axis_size("dp") // FAR
            one, two = self.sides()
            self.own = [self.both(0, j) + one[j].astype(f32) + two[j].astype(f32) for j in range(FAR)]
            self.far = [swap(self.own[j].astype(b16), "dp", j * low) for j in range(1, FAR)]
        return self.far

    def sum(self):
        far = self.fars()
        return self.own[0] + far[0].astype(f32) + far[1].astype(f32) + far[2].astype(f32)


def scatter_any(grad):
    low, far, near = places()
    tower = lax.axis_index("tower")
    halves = grad.reshape((2, FAR, low, -1) + grad.shape[1:])
    got = swap(lax.dynamic_index_in_dim(halves, 1 - tower, 0, keepdims=False), "tower", 1)
    data = add_low(lax.dynamic_index_in_dim(halves, tower, 0, keepdims=False), got)
    blocks = [lax.dynamic_index_in_dim(data, near ^ k, 1, keepdims=False) for k in range(low)]
    bit = low // 2
    while bit:
        blocks = [add_low(blocks[k], swap(blocks[k + bit], "dp", bit)) for k in range(bit)]
        bit //= 2
    own = [lax.dynamic_index_in_dim(blocks[0], far ^ j, 0, keepdims=False) for j in range(FAR)]
    total = own[0].astype(f32)
    for j in range(1, FAR):
        total = total + swap(own[j], "dp", j * low).astype(f32)
    return total


def add_from(x, axis, k):
    return x + swap(x, axis, k)


TILE = 256
PACK = 16
PAIR = 2 * HEAD_DIM
GROUP = 6
Q_BIAS, V_BIAS, O_BIAS, GAIN_1, SHIFT_1, D_BIAS, GAIN_2, SHIFT_2 = range(8)


def dot(a, b):
    return jnp.dot(a, b, preferred_element_type=f32)


def dot_nt(a, b):
    return lax.dot_general(a, b, (((1,), (1,)), ((), ())), preferred_element_type=f32)


def dot_tn(a, b):
    return lax.dot_general(a, b, (((0,), (0,)), ((), ())), preferred_element_type=f32)


def tile_at(t):
    return pl.ds(pl.multiple_of(t * TILE, TILE), TILE)


def sentence_rows(offs, b, seq):
    return pl.ds(pl.multiple_of(offs[b], PACK), seq)


def split_heads(x):
    left = lax.broadcasted_iota(jnp.int32, x.shape, 1) < HEAD_DIM
    zero = jnp.zeros_like(x)
    return jnp.concatenate([jnp.where(left, x, zero), jnp.where(left, zero, x)], 0)


def join_heads(x):
    seq = x.shape[0] // 2
    left = lax.broadcasted_iota(jnp.int32, (seq, PAIR), 1) < HEAD_DIM
    return jnp.where(left, x[:seq], x[seq:])


def by_head(fn, x):
    half = x.shape[0] // 2
    return jnp.concatenate([fn(x[:half]), fn(x[half:])], 0)


def pair_lanes(base, p):
    at = base + p * PAIR
    return slice(at, at + PAIR) if isinstance(p, int) else pl.ds(pl.multiple_of(at, PAIR), PAIR)


def pair_rows(p, size):
    return slice(p * size, (p + 1) * size) if isinstance(p, int) else pl.ds(pl.multiple_of(p * size, PAIR), size)


def over_pairs(count, looped, step):
    def one(g, _):
        step(g * GROUP)
        return 0

    if looped:
        lax.fori_loop(0, count // GROUP, one, 0)
    else:
        for first in range(0, count, GROUP):
            step(first)


def by_length(lens, count, seq, step):
    def one(b, _):
        @pl.when(lens[b] > seq // 2)
        def _():
            step(b, seq)

        @pl.when(lens[b] <= seq // 2)
        def _():
            step(b, seq // 2)

        return 0

    lax.fori_loop(0, count, one, 0)


def norm_rows(hidden):
    center = hidden - jnp.mean(hidden, axis=-1, keepdims=True)
    inverse = lax.rsqrt(jnp.mean(center * center, axis=-1, keepdims=True) + eps_norm)
    return center * inverse, inverse


def norm_back(upstream, normal, inverse, gain):
    scaled = upstream * gain
    inner = scaled - jnp.mean(scaled, axis=-1, keepdims=True)
    return inverse * (inner - normal * jnp.mean(scaled * normal, axis=-1, keepdims=True))


def row_of(vec, i):
    return vec[i : i + 1, :].astype(f32)


def add_row(sums, i, x):
    sums[i : i + 1, :] += jnp.sum(x, axis=0, keepdims=True)


def parts_kernel(place, wqkv, wout, wup, wdown, packed, first, second, third):
    def put(src, dst, at):
        rows, half = src.shape[0], src.shape[1] // 2
        for c in range(half // CHUNK):
            dst[at : at + rows, :] = src[:, pl.ds(pl.multiple_of(place[0] * half + c * CHUNK, 128), CHUNK)]
            at += rows
        return at

    first[put(wqkv, first, 0) :, :] = packed[...]
    put(wup, second, put(wout, second, 0))
    put(wdown, third, 0)


def fetch(place, pieces, targets, sems):
    copies, at = [], 0
    half = FAR // 2
    for weight, rows in targets:
        cols = weight.shape[2] // 2
        for side in range(2):
            tower = place[0] if side == 0 else 1 - place[0]
            block, by_one, by_two, low, high = pieces[5 * side : 5 * side + 5]
            spots = (
                (block, 0, 0, FAR), (by_one, 1, 0, FAR), (by_two, 2, 0, FAR), (low, 3, 0, half), (high, 3, half, half)
            )
            for piece, k, far, size in spots:
                for c in range(cols // CHUNK):
                    row = pl.multiple_of((place[1] ^ k) * rows, PACK)
                    col = pl.multiple_of(tower * cols + c * CHUNK, 128)
                    copies.append(
                        pltpu.make_async_copy(
                            piece.at[:, pl.ds(at + c * rows, rows), :],
                            weight.at[pl.ds(far, size), pl.ds(row, rows), pl.ds(col, CHUNK)],
                            sems.at[len(copies)],
                        )
                    )
        at += cols // CHUNK * rows
    return copies


def deal(place, acc, outs, base=0, looped=True):
    cols = acc.shape[1]
    if len(outs) == 1:
        outs[0][:, base : base + cols] = acc[...].astype(b16)
        return
    mine, first, rest = outs
    rows = first.shape[1]
    for own in (False, True):
        side = place[0] if own else 1 - place[0]
        for k in range(4):
            target = mine.at[k] if own else first if k == 3 else rest.at[k]

            def block(j, _):
                at = (side * 4 * FAR + (place[2] ^ j) * 4 + (place[1] ^ k)) * rows
                target[j, :, base : base + cols] = acc[pl.ds(pl.multiple_of(at, 8), rows), :].astype(b16)
                return 0

            if looped:
                lax.fori_loop(0, FAR, block, 0)
            else:
                for j in range(FAR):
                    block(j, 0)


def flat_of(weight, cols=slice(None)):
    block = weight[:, :, cols]
    return block.reshape(block.shape[0] * block.shape[1], block.shape[2])


def attend_kernel(n_pieces, lens, offs, tiles, place, homes, vec, x_h, y_h, *refs):
    pieces, refs = refs[:n_pieces], refs[n_pieces:]
    if n_pieces:
        wqkv_h, *sinks, x, xs, qkv, probs, ctx, sems, wqkv, got = refs
        copies = fetch(place, pieces, ((wqkv, wqkv.shape[1] // 4),), got)
        for copy in copies:
            copy.start()
    else:
        wqkv, *sinks, x, xs, qkv, probs, ctx, sems = refs
        copies = []
    xs_h, qkv_h, probs_h, ctx_h = sinks
    count, seq, width = x.shape

    def tokens(b, size, do):
        for side, source in enumerate((x_h, y_h)):

            @pl.when(homes[b] == side)
            def _():
                at = pl.ds(0, size)
                do(pltpu.make_async_copy(source.at[homes[count + b], at], x.at[b, at], sems.at[0, b]))

    by_length(lens, count, seq, lambda b, size: tokens(b, size, lambda copy: copy.start()))
    xs[...] = jnp.zeros_like(xs)
    ctx[...] = jnp.zeros_like(ctx)
    by_length(lens, count, seq, lambda b, size: tokens(b, size, lambda copy: copy.wait()))

    def pack(b, _):
        def block(i, _):
            at = pl.multiple_of(offs[b] + i * PACK, PACK)
            xs[pl.ds(at, PACK), :] = x[b, pl.ds(pl.multiple_of(i * PACK, PACK), PACK), :]
            return 0

        return lax.fori_loop(0, (lens[b] + PACK - 1) // PACK, block, 0)

    lax.fori_loop(0, count, pack, 0)

    def leave(source, target, which, do):
        def one(i, _):
            at = pl.ds(pl.multiple_of(i * seq, seq), seq)
            do(pltpu.make_async_copy(source.at[at], target.at[at], sems.at[which, i]))
            return 0

        lax.fori_loop(0, tiles[0] * (TILE // seq) + 1, one, 0)

    def probs_of(b, size):
        at = pl.ds(0, HEADS * size)
        return pltpu.make_async_copy(probs.at[b, at], probs_h.at[b, at], sems.at[4, b])

    leave(xs, xs_h, 1, lambda copy: copy.start())
    for copy in copies:
        copy.wait()
    if n_pieces:
        out = pltpu.make_async_copy(wqkv, wqkv_h, sems.at[5, 0])
        out.start()

    def project(t, _):
        x = xs[tile_at(t), :]
        for c in range(3):
            cols = slice(c * width, (c + 1) * width)
            joined = dot(x, flat_of(wqkv, cols))
            if c == 0:
                joined = (joined + row_of(vec, Q_BIAS)) * (HEAD_DIM ** -0.5)
            if c == 2:
                joined = joined + row_of(vec, V_BIAS)
            qkv[tile_at(t), cols] = joined.astype(b16)
        return 0

    lax.fori_loop(0, tiles[0], project, 0)
    qkv[pl.ds(pl.multiple_of(tiles[0] * TILE, TILE), seq), :] = jnp.zeros((seq, 3 * width), b16)
    leave(qkv, qkv_h, 2, lambda copy: copy.start())

    def attend(b, size):
        rows, key_rows = sentence_rows(offs, b, seq), sentence_rows(offs, b, size)
        valid = lax.broadcasted_iota(jnp.int32, (size, seq), 0) < lens[b]

        def softmax(s):
            s = jnp.where(valid, s, -1000000000.0)
            e = jnp.exp(s - jnp.max(s, axis=0, keepdims=True))
            return (e * (1.0 / jnp.sum(e, axis=0, keepdims=True))).astype(b16)

        def pairs(group):
            spots = range(GROUP)
            queries = [qkv[rows, pair_lanes(0, group + i)] for i in spots]
            keys = [split_heads(qkv[key_rows, pair_lanes(width, group + i)]) for i in spots]
            vals = [split_heads(qkv[key_rows, pair_lanes(2 * width, group + i)]) for i in spots]
            scores = [dot_nt(k, q) for k, q in zip(keys, queries)]
            lows = [by_head(softmax, s) for s in scores]
            outs = [dot_tn(low, v).astype(b16) for low, v in zip(lows, vals)]
            for i, low, out in zip(spots, lows, outs):
                probs[b, pair_rows(group + i, 2 * size), :] = low
                ctx[rows, pair_lanes(0, group + i)] = out

        over_pairs(width // PAIR, size == seq, pairs)
        probs_of(b, size).start()

    by_length(lens, count, seq, attend)
    leave(ctx, ctx_h, 3, lambda copy: copy.start())
    leave(xs, xs_h, 1, lambda copy: copy.wait())
    leave(qkv, qkv_h, 2, lambda copy: copy.wait())
    leave(ctx, ctx_h, 3, lambda copy: copy.wait())
    by_length(lens, count, seq, lambda b, size: probs_of(b, size).wait())
    if n_pieces:
        out.wait()


def inside(offs, lens, b, t):
    row = t * TILE + lax.broadcasted_iota(jnp.int32, (TILE, 1), 0)
    return (row >= offs[b]) & (row < offs[b] + lens[b])


def take_weights(step, place, pieces, refs, count, rows):
    if not pieces:
        return refs[:count], refs[count:], lambda: None, lambda: None
    sinks, refs = refs[:count], refs[count:]
    held, got, sent, refs = refs[-count - 2 : -2], refs[-2], refs[-1], refs[: -count - 2]
    leave = [pltpu.make_async_copy(a, b, sent.at[i]) for i, (a, b) in enumerate(zip(held, sinks))]

    copies = fetch(place, pieces, [(weight, rows) for weight in held], got)
    first = held[0].shape[2] // CHUNK * 5

    @pl.when(step == 0)
    def _():
        for copy in copies:
            copy.start()
        for copy in copies[:first]:
            copy.wait()

    def others():
        @pl.when(step == 0)
        def _():
            for copy in copies[first:]:
                copy.wait()
            for copy in leave:
                copy.start()

    def finish():
        @pl.when(step == pl.num_programs(0) - 1)
        def _():
            for copy in leave:
                copy.wait()

    return held, refs, others, finish


def up_kernel(n_pieces, rows, lens, offs, tiles, place, ctx, xs, vec, ups, *refs):
    t = pl.program_id(0)
    pieces, refs = refs[:n_pieces], refs[n_pieces:]
    (wout, wup), (act, slope, n1, inv1), others, finish = take_weights(t, place, pieces, refs, 2, rows)
    width = n1.shape[1]

    @pl.when(t < tiles[0])
    def _():
        attended = dot(ctx[...], flat_of(wout)) + row_of(vec, O_BIAS)
        normal, inverse = norm_rows(xs[...].astype(f32) + attended)
        n1[...] = normal
        inv1[...] = jnp.broadcast_to(inverse, (TILE, 128))
        low = (normal * row_of(vec, GAIN_1) + row_of(vec, SHIFT_1)).astype(b16)
        others()

        def chunk(c, _):
            cols = pl.ds(pl.multiple_of(c * width, width), width)
            pre = dot(low, flat_of(wup, cols)) + ups[pl.ds(c, 1), :]
            half = 0.5 * (1.0 + lax.erf(pre * (0.5 ** 0.5)))
            act[:, cols] = (pre * half).astype(b16)
            slope[:, cols] = (half + pre * (jnp.exp(-0.5 * pre * pre) * 0.3989422804014327)).astype(b16)
            return 0

        lax.fori_loop(0, ups.shape[0], chunk, 0)

    finish()


def down_kernel(n_pieces, rows, lens, offs, tiles, place, n1, act, vec, *refs):
    t = pl.program_id(0)
    pieces, refs = refs[:n_pieces], refs[n_pieces:]
    (wdown,), (n2, inv2, pooled), others, finish = take_weights(t, place, pieces, refs, 1, rows)
    others()
    width = n1.shape[1]
    count = pooled.shape[0]

    @pl.when(t == 0)
    def _():
        pooled[...] = jnp.zeros_like(pooled)

    @pl.when(t < tiles[0])
    def _():
        total = n1[...] * row_of(vec, GAIN_1) + row_of(vec, SHIFT_1) + row_of(vec, D_BIAS)
        total = total + dot(act[...], flat_of(wdown))
        normal, inverse = norm_rows(total)
        n2[...] = normal
        inv2[...] = jnp.broadcast_to(inverse, (TILE, 128))
        for b in range(count):
            add_row(pooled, b, jnp.where(inside(offs, lens, b, t), normal, 0.0))

    @pl.when(t == pl.num_programs(0) - 1)
    def _():
        for b in range(count):
            size = jnp.full((1, width), lens[b], jnp.int32).astype(f32)
            pooled[b : b + 1, :] = pooled[b : b + 1, :] / size * row_of(vec, GAIN_2) + row_of(vec, SHIFT_2)

    finish()


def accumulate(t, acc, cols, left, right):
    @pl.when(t == 0)
    def _():
        acc[:, cols] = dot_tn(left, right)

    @pl.when(t > 0)
    def _():
        acc[:, cols] += dot_tn(left, right)


def pair_head(lens, place, homes, labels, bias, pooled, partner, head, tops, own, ends):
    count, width = pooled.shape

    for side in range(2):
        for i in range(count):
            at = side * count + i
            away, slot = homes[2 * count + at], homes[4 * count + at]
            row = jnp.where(away == 0, pooled[pl.ds(slot, 1), :], partner[pl.ds(slot, 1), :])
            ends[side, i : i + 1, :] = row
    left, right = ends[0], ends[1]
    own[...] = jnp.where(place[0] == 0, left, right)
    gap = left - right
    soft = jnp.sqrt(gap * gap + gap_soft)
    feats = (left, right, soft)
    row = lax.broadcasted_iota(jnp.int32, (count, 1), 0)
    label = jnp.zeros((count, 1), jnp.int32)
    for b in range(count):
        label = jnp.where(row == b, labels[b], label)
    logits = []
    for c in range(NCLASS):
        terms = [
            jnp.sum(feats[i] * head[c : c + 1, i * width : (i + 1) * width], axis=-1, keepdims=True) for i in range(3)
        ]
        logits.append(terms[0] + terms[1] + terms[2] + bias[c])
    top = jnp.maximum(jnp.maximum(logits[0], logits[1]), logits[2])
    exps = [jnp.exp(x - top) for x in logits]
    norm = exps[0] + exps[1] + exps[2]
    grads = [exps[c] / norm - jnp.where(label == c, 1.0, 0.0) for c in range(NCLASS)]
    back = []
    tops[...] = jnp.zeros_like(tops)
    for i in range(3):
        cols = slice(i * width, (i + 1) * width)
        back.append(sum(grads[c] * head[c : c + 1, cols] for c in range(NCLASS)))
        for c in range(NCLASS):
            tops[c : c + 1, cols] = 0.5 * jnp.sum(grads[c] * feats[i], axis=0, keepdims=True)
    for c in range(NCLASS):
        tops[NCLASS + c : NCLASS + c + 1, 0:128] = jnp.broadcast_to(0.5 * jnp.sum(grads[c], axis=0, keepdims=True), (1, 128))
    slope = gap / soft
    ends[0] = back[0] + slope * back[2]
    ends[1] = back[1] - slope * back[2]
    for b in range(count):
        side = jnp.where(homes[b] == 0, place[0], 1 - place[0])
        row = ends[side, pl.ds(homes[count + b], 1), :]
        size = jnp.full((1, width), lens[b], jnp.int32).astype(f32)
        ends[2, b : b + 1, :] = row / size


def down_back_kernel(
    lens, offs, tiles, place, homes, labels, bias, pooled, partner, head, act, n2, inv2, vec, sum_grad, *refs
):
    *outs, sums, tops, own, acc, ends = refs
    t = pl.program_id(0)
    count, width = pooled.shape

    @pl.when(t == 0)
    def _():
        pair_head(lens, place, homes, labels, bias, pooled, partner, head, tops, own, ends)
        sums[...] = jnp.zeros_like(sums)

    @pl.when(t < tiles[0])
    def _():
        up = jnp.zeros((TILE, width), f32)
        for b in range(count):
            up = jnp.where(inside(offs, lens, b, t), ends[2, b : b + 1, :], up)
        normal = n2[...]
        grad = norm_back(up, normal, inv2[:, 0:1], row_of(vec, GAIN_2))
        sum_grad[...] = grad
        add_row(sums, 0, up * normal)
        add_row(sums, 1, up)
        add_row(sums, 2, grad)
        low = grad.astype(b16)

        accumulate(t, acc, slice(None), act[...], low)

    @pl.when(t == pl.num_programs(0) - 1)
    def _():
        deal(place, acc, outs)


def early(t, copies):
    @pl.when(t == 0)
    def _():
        for copy in copies:
            copy.start()

    def ready(i):
        @pl.when(t == 0)
        def _():
            copies[i].wait()

    return ready


def pre_back_kernel(lens, offs, tiles, place, sum_grad, slope, wdown, pre_low, sums):
    t = pl.program_id(0)
    width = sum_grad.shape[1]
    chunks = slope.shape[1] // width
    split = wdown.shape[0] // chunks

    @pl.when(t == 0)
    def _():
        sums[...] = jnp.zeros_like(sums)

    @pl.when(t < tiles[0])
    def _():
        low = sum_grad[...].astype(b16)
        for c in range(chunks):
            cols = slice(c * width, (c + 1) * width)
            pre = dot_nt(low, flat_of(wdown[c * split : (c + 1) * split])) * slope[:, cols].astype(f32)
            add_row(sums, c, pre)
            pre_low[:, cols] = pre.astype(b16)


def mid_back_kernel(
    lens, offs, tiles, place, sum_grad, pre_low, n1, inv1, ctx, wup, wout, vec, mid, ctx_grad, *refs
):
    *outs, sums, acc = refs
    t = pl.program_id(0)
    hidden = pre_low.shape[1]

    @pl.when(t == 0)
    def _():
        sums[...] = jnp.zeros_like(sums)

    @pl.when(t < tiles[0])
    def _():
        pre = pre_low[...]
        grad = sum_grad[...] + dot_nt(pre, flat_of(wup))
        normal = n1[...]
        add_row(sums, 0, grad * normal)
        add_row(sums, 1, grad)
        middle = norm_back(grad, normal, inv1[:, 0:1], row_of(vec, GAIN_1))
        add_row(sums, 2, middle)
        mid[...] = middle
        low = middle.astype(b16)
        ctx_grad[...] = dot_nt(low, flat_of(wout)).astype(b16)
        first_low = (normal * row_of(vec, GAIN_1) + row_of(vec, SHIFT_1)).astype(b16)
        accumulate(t, acc, slice(0, hidden), first_low, pre)
        accumulate(t, acc, slice(hidden, None), ctx[...], low)

    @pl.when(t == pl.num_programs(0) - 1)
    def _():
        deal(place, acc, outs)


def attend_back_kernel(lens, offs, tiles, place, qkv_h, probs_h, ctx_grad_h, grad_h, sums, grad, qkv, probs, ctx_grad, sems):
    width = ctx_grad.shape[1]
    count, seq = probs.shape[0], probs.shape[2]
    blocks = qkv.shape[0] // seq

    def rows_in_use(do):
        for i in range(blocks):

            @pl.when(i * seq < tiles[0] * TILE + seq)
            def _():
                at = pl.ds(i * seq, seq)
                do(pltpu.make_async_copy(qkv_h.at[at], qkv.at[at], sems.at[i]))
                do(pltpu.make_async_copy(ctx_grad_h.at[at], ctx_grad.at[at], sems.at[blocks + i]))

    def probs_of(b, size):
        at = pl.ds(0, HEADS * size)
        return pltpu.make_async_copy(probs_h.at[b, at], probs.at[b, at], sems.at[2 * blocks + b])

    rows_in_use(lambda copy: copy.start())
    by_length(lens, count, seq, lambda b, size: probs_of(b, size).start())
    grad[...] = jnp.zeros_like(grad)
    sums[...] = jnp.zeros_like(sums)
    rows_in_use(lambda copy: copy.wait())

    def attend(b, size):
        rows, key_rows = sentence_rows(offs, b, seq), sentence_rows(offs, b, size)
        real = lax.broadcasted_iota(jnp.int32, (seq, 1), 0) < lens[b]
        probs_of(b, size).wait()

        def spread(x):
            return jnp.broadcast_to(jnp.sum(x, axis=0, keepdims=True), x.shape)

        def pairs(group):
            spots = range(GROUP)
            ups = [jnp.where(real, ctx_grad[rows, pair_lanes(0, group + i)], jnp.zeros((), b16)) for i in spots]
            queries = [qkv[rows, pair_lanes(0, group + i)] for i in spots]
            keys = [split_heads(qkv[key_rows, pair_lanes(width, group + i)]) for i in spots]
            vals = [split_heads(qkv[key_rows, pair_lanes(2 * width, group + i)]) for i in spots]
            lows = [probs[b, pair_rows(group + i, 2 * size), :] for i in spots]
            prob_grads = [dot_nt(v, up) for v, up in zip(vals, ups)]
            val_grads = [join_heads(dot(low, up)).astype(b16) for low, up in zip(lows, ups)]
            scores = []
            for low, pg in zip(lows, prob_grads):
                pr = low.astype(f32)
                scores.append((pr * (pg - by_head(spread, pg * pr))).astype(b16))
            query_grads = [(dot_tn(s, k) * (HEAD_DIM ** -0.5)).astype(b16) for s, k in zip(scores, keys)]
            key_grads = [join_heads(dot(s, q)).astype(b16) for s, q in zip(scores, queries)]
            for i in spots:
                grad[rows, pair_lanes(0, group + i)] = query_grads[i]
                grad[key_rows, pair_lanes(width, group + i)] = key_grads[i]
                grad[key_rows, pair_lanes(2 * width, group + i)] = val_grads[i]

        over_pairs(width // PAIR, size == seq, pairs)

    by_length(lens, count, seq, attend)

    def result(t):
        return pltpu.make_async_copy(grad.at[tile_at(t)], grad_h.at[tile_at(t)], sems.at[2 * blocks + count + t])

    def total(t, _):
        result(t).start()
        for c in (0, 2):
            add_row(sums, c // 2, grad[tile_at(t), c * width : (c + 1) * width].astype(f32))
        return 0

    def finish(t, _):
        result(t).wait()
        return 0

    lax.fori_loop(0, tiles[0], total, 0)
    lax.fori_loop(0, tiles[0], finish, 0)


def input_kernel(lens, offs, tiles, place, homes, grad, mid, xs, biases, wqkv_h, gx, gy, *refs):
    *outs, buf, acc, tail, wqkv, sems = refs
    count, seq, width = gx.shape
    t = pl.program_id(0)
    ready = early(t, [pltpu.make_async_copy(wqkv_h, wqkv, sems.at[0])])

    @pl.when(t == 0)
    def _():
        gx[...] = jnp.zeros_like(gx)
        gy[...] = jnp.zeros_like(gy)

    @pl.when(t < tiles[0])
    def _():
        accumulate(t, acc, slice(None), xs[...], grad[...])
        ready(0)
        buf[tile_at(t), :] = dot_nt(grad[...], flat_of(wqkv)) + mid[...]

    @pl.when(t == pl.num_programs(0) - 1)
    def _():
        def unpack(b, _):
            blocks = (lens[b] + PACK - 1) // PACK
            for side, target in enumerate((gx, gy)):

                def block(i, _):
                    at = pl.multiple_of(offs[b] + i * PACK, PACK)
                    rows = pl.ds(pl.multiple_of(i * PACK, PACK), PACK)
                    target[homes[count + b], rows, :] = buf[pl.ds(at, PACK), :].astype(target.dtype)
                    return 0

                lax.fori_loop(0, jnp.where(homes[b] == side, blocks, 0), block, 0)
            return 0

        lax.fori_loop(0, count, unpack, 0)
        deal(place, acc, outs, looped=False)
        if len(outs) > 1:
            cols, lanes = acc.shape[1], tail.shape[1]
            each = biases.shape[1] // lanes
            tail[...] = jnp.zeros_like(tail)
            for r in range(2 * each):
                tail[r : r + 1, :] = biases[r // each : r // each + 1, r % each * lanes : (r % each + 1) * lanes]
            block = tail[...].astype(b16)
            mine, first, rest = outs
            for target in [mine.at[k] for k in range(4)] + [first] + [rest.at[k] for k in range(3)]:
                for spot in range(FAR):
                    target[spot, :, cols : cols + lanes] = block


def small_kernel(spot, sums, tail, *outs):
    width = sums.shape[1] // 3
    *plain, ups, head, classes = outs
    mine = plain[0].shape[1]

    def share(x, size):
        x = jnp.broadcast_to(x, (8, x.shape[1])) if x.shape[0] == 1 else x
        return pltpu.roll(x, lax.rem(x.shape[1] - spot[0] * size, x.shape[1]), axis=1)[:, 0:size]

    count = width // tail.shape[1]
    for p in range(2):
        row = jnp.concatenate([tail[p * count + r : p * count + r + 1, :] for r in range(count)], 1)
        plain[p][...] = share(row, mine)[0:1]
    blocks = [share(sums[0:8, p * width : (p + 1) * width], mine) for p in (0, 2)]
    for out, (block, row) in zip(plain[2:], ((1, 2), (1, 0), (1, 1), (0, 2), (0, 0), (0, 1))):
        out[...] = blocks[block][row : row + 1]
    ups[...] = share(jnp.concatenate([sums[r : r + 1, width : 2 * width] for r in range(4)], 1), 4 * mine)[0:1]
    head[...] = share(sums[8:16, :], 3 * mine)[0:NCLASS]
    classes[...] = jnp.transpose(sums[8:16, 0:128])[0:1, NCLASS : 2 * NCLASS]


class Tiled:
    def __init__(self, array):
        self.array = array


class Flat:
    def __init__(self, array):
        self.array = array


class Scalars:
    def __init__(self, array):
        self.array = array


def spec_of(x):
    if isinstance(x, Scalars):
        return pl.BlockSpec(memory_space=pltpu.SMEM)
    if isinstance(x, Flat):
        return pl.BlockSpec(memory_space=pl.ANY)
    if isinstance(x, Tiled):
        return pl.BlockSpec((TILE, x.array.shape[1]), lambda i, lens, offs, tiles, place: (jnp.minimum(i, tiles[0] - 1), 0))
    return pl.BlockSpec(x.shape, lambda *_: (0,) * len(x.shape), pipeline_mode=pl.Buffered(1))


def bare(x):
    return x.array if isinstance(x, (Tiled, Flat, Scalars)) else x


def shape(dtype, *dims):
    return jax.ShapeDtypeStruct(dims, dtype)


def call(kernel, meta, args, outs, scratch=(), steps=1, micros=0):
    moved = sum(bare(a).size * bare(a).dtype.itemsize for a in (*args, *outs))
    return pl.pallas_call(
        kernel,
        out_shape=[bare(o) for o in outs],
        grid_spec=pltpu.PrefetchScalarGridSpec(
            num_scalar_prefetch=len(meta),
            grid=(steps,),
            in_specs=[spec_of(a) for a in args],
            out_specs=[spec_of(o) for o in outs],
            scratch_shapes=list(scratch),
        ),
        cost_estimate=pl.CostEstimate(flops=int(micros * 1.15e9), transcendentals=0, bytes_accessed=moved),
        compiler_params=pltpu.CompilerParams(vmem_limit_bytes=58 << 20),
    )(*meta, *[bare(a) for a in args])


def pack_small(vectors):
    total = sum(v.shape[0] for v in vectors)
    rows = -(-total // (8 * CHUNK)) * 8
    at, flat = 0, 0.0
    for v in vectors:
        flat = flat + jnp.pad(v.astype(f32), (at, rows * CHUNK - at - v.shape[0]))
        at += v.shape[0]
    return flat.astype(b16).reshape(rows, CHUNK)


def body(
    embeddings, lengths, labels, qkv_weight, query_bias, value_bias, out_weight, out_bias, attn_gain,
    attn_shift, up_weight, up_bias, down_weight, down_bias, ffn_gain, ffn_shift, head_weight, head_bias,
):
    width = embeddings.shape[-1]
    seq_len = embeddings.shape[2]
    count = embeddings.shape[1]
    rows = -(-count * seq_len // TILE) * TILE
    hidden = up_weight.shape[1]
    groups = lax.axis_size("dp")
    low, far, near = places()
    tower = lax.axis_index("tower")
    shard_rows = qkv_weight.shape[0]
    quick = low == 4 and shard_rows % PACK == 0

    other_len = swap(lengths[0].astype(f32), "tower", 1).astype(jnp.int32)
    first_here = tower == 0
    all_len = jnp.where(
        first_here, jnp.concatenate([lengths[0], other_len]), jnp.concatenate([other_len, lengths[0]])
    )
    ids = jnp.arange(2 * count)
    ahead = (all_len[None, :] > all_len[:, None]) | (
        (all_len[None, :] == all_len[:, None]) & (ids[None, :] < ids[:, None])
    )
    rank = jnp.sum(ahead.astype(jnp.int32), axis=1)
    away = (((rank + 1) // 2) % 2 != tower).astype(jnp.int32)
    picked = (away[None, :] == 0) & (rank[None, :] // 2 == jnp.arange(count)[:, None])
    source = jnp.sum(jnp.where(picked, ids[None, :], 0), axis=1)
    sent_len = jnp.sum(jnp.where(picked, all_len[None, :], 0), axis=1)
    homes = jnp.concatenate([(source // count != tower).astype(jnp.int32), source % count, away, rank // 2])
    homes = homes.astype(jnp.int32)

    taken = (sent_len + PACK - 1) // PACK * PACK
    before = jnp.arange(count)[None, :] < jnp.arange(count)[:, None]
    offs = jnp.sum(jnp.where(before, taken[None, :], 0), axis=1)
    tiles = (jnp.sum(taken)[None] + TILE - 1) // TILE
    place = jnp.stack([tower, near, far]).astype(jnp.int32)
    meta = (sent_len, offs, tiles, place)
    steps = rows // TILE

    packed = pack_small((
        query_bias, value_bias, out_bias, attn_gain, attn_shift, down_bias, ffn_gain, ffn_shift, up_bias,
        head_weight.reshape(-1),
    ))
    weights = (qkv_weight, out_weight, up_weight, down_weight)
    if quick:
        sizes = [w.size // 2 // CHUNK for w in weights]
        first_part, up_part, down_part = call(
            parts_kernel, (place,), (*weights, packed),
            (
                shape(b16, sizes[0] + packed.shape[0], CHUNK), shape(b16, sizes[1] + sizes[2], CHUNK),
                shape(b16, sizes[3], CHUNK),
            ),
        )
    else:
        first_part = jnp.concatenate([to_chunks(qkv_weight), packed], 0)
        up_part, down_part = jnp.concatenate([to_chunks(out_weight), to_chunks(up_weight)], 0), to_chunks(down_weight)
    cut = first_part.shape[0] - packed.shape[0]
    low_far = far_pieces(first_part)
    other_tokens = swap(embeddings[0], "tower", 1)
    low_far = after(low_far, other_tokens, homes)
    block_first = in_order(low_far, far, 0)
    far_up = far_pieces(after(up_part, *low_far))
    full = [(FAR, w.shape[0] * low, w.shape[1]) for w in weights]
    if quick:
        near_first = gather_near(block_first)
        far_up = after(far_up, *near_first[3:])
        block_up = in_order(far_up, far, 0)
        far_down = far_pieces(after(down_part, *far_up))
        pieces_first = near_first + [swap(p, "tower", 1) for p in near_first]
        tails = [p[:, cut:] for p in near_first]
        packs = in_order(tails[:3] + [jnp.concatenate(tails[3:], 0)], near, 1)
    else:
        block_up = in_order(far_up, far, 0)
        far_down = far_pieces(down_part)
        whole_first = gather_any(block_first)
        pieces_first = [from_chunks(whole_first[:, :, :cut], shard_rows)]
        packs = whole_first[:, :, cut:]
    packs = packs.reshape(groups, -1).astype(f32)
    cuts = [8 * shard_rows, 8 * shard_rows + up_bias.shape[0]]
    cuts.append(cuts[1] + head_weight.size)
    vec = packs[:, : cuts[0]].reshape(groups, 8, shard_rows).transpose(1, 0, 2).reshape(8, width)
    ups = packs[:, cuts[0] : cuts[1]].reshape(-1, width)
    head_rows = packs[:, cuts[1] : cuts[2]].reshape(-1, NCLASS).T

    ext = rows + seq_len
    dense = 2 * rows * width
    sinks = [
        Flat(shape(b16, ext, width)), Flat(shape(b16, ext, 3 * width)),
        Flat(shape(b16, count, HEADS * seq_len, seq_len)), Flat(shape(b16, ext, width)),
    ]
    scratch = [pltpu.VMEM((count, seq_len, width), b16)]
    scratch += [pltpu.VMEM(o.array.shape, o.array.dtype) for o in sinks]
    scratch.append(pltpu.SemaphoreType.DMA((6, max(ext // seq_len, count))))
    if quick:
        both = [Flat(shape(b16, *full[0]))] + sinks
        pieces_first = after(pieces_first, block_up)
        proj_qkv, xs, qkv, probs, ctx = call(
            partial(attend_kernel, 10), meta,
            (Scalars(homes), vec, Flat(embeddings[0]), Flat(other_tokens), *map(Flat, pieces_first)), both,
            scratch + [pltpu.VMEM(full[0], b16), pltpu.SemaphoreType.DMA((30,))],
            micros=4,
        )
    else:
        (proj_qkv,) = pieces_first
        xs, qkv, probs, ctx = call(
            partial(attend_kernel, 0), meta, (Scalars(homes), vec, Flat(embeddings[0]), Flat(other_tokens), proj_qkv), sinks,
            scratch,
            micros=4,
        )

    wide, slim, thin = shape(b16, rows, hidden), shape(f32, rows, width), shape(f32, rows, 128)
    outs = [Tiled(wide), Tiled(wide), Tiled(slim), Tiled(thin)]
    args = Tiled(ctx), Tiled(xs), vec, ups
    if quick:
        near_up = gather_near(block_up, ctx)
        block_down = in_order(after(far_down, ctx), far, 0)
        pieces_up = near_up + [swap(p, "tower", 1) for p in near_up]
        proj_out, proj_up, act, slope, n1, inv1 = call(
            partial(up_kernel, 10, shard_rows), meta, (*args, *map(Flat, pieces_up)),
            [Flat(shape(b16, *full[1])), Flat(shape(b16, *full[2]))] + outs,
            [
                pltpu.VMEM(full[1], b16), pltpu.VMEM(full[2], b16), pltpu.SemaphoreType.DMA((50,)),
                pltpu.SemaphoreType.DMA((2,)),
            ],
            steps=steps, micros=14,
        )
    else:
        whole_up = gather_any(block_up)
        cut = out_weight.size // 2 // CHUNK
        proj_out = from_chunks(whole_up[:, :, :cut], shard_rows)
        proj_up = from_chunks(whole_up[:, :, cut:], shard_rows)
        act, slope, n1, inv1 = call(
            partial(up_kernel, 0, 0), meta, (*args, proj_out, proj_up), outs, steps=steps, micros=14,
        )
    outs = [Tiled(slim), Tiled(thin), shape(f32, count, width)]
    if quick:
        near_down = gather_near(block_down, act)
        pieces_down = near_down + [swap(p, "tower", 1) for p in near_down]
        proj_down, n2, inv2, pooled = call(
            partial(down_kernel, 10, down_weight.shape[0]), meta, (Tiled(n1), Tiled(act), vec, *map(Flat, pieces_down)),
            [Flat(shape(b16, *full[3]))] + outs,
            [pltpu.VMEM(full[3], b16), pltpu.SemaphoreType.DMA((10,)), pltpu.SemaphoreType.DMA((1,))],
            steps=steps, micros=10,
        )
    else:
        proj_down = from_chunks(gather_any(in_order(far_down, far, 0)), down_weight.shape[0])
        n2, inv2, pooled = call(
            partial(down_kernel, 0, 0), meta, (Tiled(n1), Tiled(act), vec, proj_down), outs, steps=steps, micros=10,
        )

    def dealt(full_rows, cols):
        if quick:
            block = FAR, full_rows // (8 * FAR), cols
            return [shape(b16, 4, *block), shape(b16, *block), shape(b16, 3, *block)]
        return [shape(b16, full_rows, cols)]

    partner = swap(pooled, "tower", 1)
    sums_of = shape(f32, 8, width)
    sum_grad, *down_parts, sums_two, tops, own_pooled = call(
        down_back_kernel, meta,
        (
            Scalars(homes), Scalars(labels), Scalars(head_bias.astype(f32)), pooled, partner, head_rows, Tiled(act), Tiled(n2),
            Tiled(inv2), vec,
        ),
        [Tiled(slim)] + dealt(hidden, width) + [sums_of, shape(f32, 8, 3 * width), shape(f32, count, width)],
        [pltpu.VMEM((hidden, width), f32), pltpu.VMEM((3, count, width), f32)], steps=steps, micros=11,
    )
    if quick:
        down = Scatter(down_parts)
        sum_grad = after(sum_grad, down.first)
    pre_low, sums_up = call(
        pre_back_kernel, meta, (Tiled(sum_grad), Tiled(slope), proj_down), [Tiled(wide), sums_of], steps=steps,
        micros=8,
    )
    if quick:
        pre_low = after(pre_low, down.corners(), down.rest)
    mid, ctx_grad, *up_parts, sums_one = call(
        mid_back_kernel, meta,
        (Tiled(sum_grad), Tiled(pre_low), Tiled(n1), Tiled(inv1), Tiled(ctx), proj_up, proj_out, vec),
        [Tiled(slim), Tiled(shape(b16, ext, width))] + dealt(width, hidden + width) + [sums_of],
        [pltpu.VMEM((width, hidden + width), f32)], steps=steps, micros=20,
    )
    summed = jnp.concatenate([jnp.concatenate([sums_two, sums_up, sums_one], 1), tops], 0)
    came = swap(summed, "tower", 1)
    if quick:
        up = Scatter(after(up_parts, down.sides()))
        up.sides()
        ctx_grad = after(ctx_grad, came, *up.corner, *up.sent)
    qkv_grad, sums_in = call(
        attend_back_kernel, meta, (Flat(qkv), Flat(probs), Flat(ctx_grad)), [Flat(shape(b16, ext, 3 * width)), sums_of],
        [
            pltpu.VMEM(qkv.shape, b16), pltpu.VMEM(qkv.shape, b16), pltpu.VMEM(probs.shape, b16), pltpu.VMEM(ctx_grad.shape, b16),
            pltpu.SemaphoreType.DMA((2 * (ext // seq_len) + count + steps,)),
        ],
        micros=14,
    )
    summed = after(summed + came, qkv_grad)
    came = swap(summed, "dp", low)
    if quick:
        mid = after(mid, qkv_grad, *up.side, *down.fars())
        up.fars()
    lanes = 128
    last_cols = 3 * width + (lanes if quick else 0)
    grad_in, grad_away, *last_parts = call(
        input_kernel, meta, (Scalars(homes), Tiled(qkv_grad), Tiled(mid), Tiled(xs), sums_in, Flat(proj_qkv)),
        [shape(f32, count, seq_len, width), shape(b16, count, seq_len, width)] + dealt(width, last_cols),
        [pltpu.VMEM((rows, width), f32), pltpu.VMEM((width, 3 * width), f32), pltpu.VMEM((24, lanes), f32),
         pltpu.VMEM(full[0], b16), pltpu.SemaphoreType.DMA((1,))],
        steps=steps, micros=16,
    )
    if quick:
        last_parts, up.far, came = after((last_parts, up.far, came))
    summed = summed + came
    came = swap(summed, "dp", 2 * low)
    if quick:
        last = Scatter(last_parts)
        last.sides()
        came = after(came, *last.sent)
        grad_in = grad_in + swap(after(grad_away, *last.corner), "tower", 1).astype(f32)
        last.far = after(last.fars(), grad_in)
        down_out, up_out, last_out = down.sum(), up.sum(), last.sum()
        tail, last_out = last_out[:, 3 * width :], last_out[:, : 3 * width]
    else:
        grad_in = grad_in + swap(grad_away, "tower", 1).astype(f32)
        down_out, up_out, last_out = (scatter_any(*p) for p in (down_parts, up_parts, last_parts))
        tail, bit = add_from(sums_in[0:2].reshape(-1, lanes), "tower", 1), 1
        while bit < groups:
            tail = add_from(tail, "dp", bit)
            bit *= 2
    summed, bit = summed + came, 1
    while bit < low:
        came = swap(summed, "dp", bit)
        if quick and bit == 1:
            came = after(came, *last.side)
        summed, bit = summed + came, 2 * bit
    spot = (tower * groups + lax.axis_index("dp")).astype(jnp.int32)[None]
    mine = width // (2 * groups)
    *plain, up_bias_sum, head_sum, class_sum = pl.pallas_call(
        small_kernel,
        out_shape=[shape(f32, 1, mine)] * 8
        + [shape(f32, 1, 4 * mine), shape(f32, NCLASS, 3 * mine), shape(f32, 1, NCLASS)],
        in_specs=[pl.BlockSpec(memory_space=pltpu.SMEM)] + [pl.BlockSpec(memory_space=pltpu.VMEM)] * 2,
        out_specs=[pl.BlockSpec(memory_space=pltpu.VMEM)] * 11,
    )(spot, summed, tail)
    q_sum, v_sum, o_sum, gain_one, shift_one, d_sum, gain_two, shift_two = [x.reshape(-1) for x in plain]
    return (
        own_pooled[None],
        grad_in[None],
        last_out,
        q_sum, v_sum,
        up_out[:, hidden:],
        o_sum, gain_one, shift_one,
        up_out[:, :hidden],
        up_bias_sum.reshape(-1),
        down_out,
        d_sum, gain_two, shift_two,
        head_sum.T,
        class_sum.reshape(-1),
    )


def solution(mesh):
    rows, vec = P("dp", None), P("dp")
    out_rows, out_vec = P(("tower", "dp"), None), P(("tower", "dp"))
    return jax.shard_map(
        body,
        mesh=mesh,
        in_specs=(
            P("tower", "dp", None, None), P("tower", "dp"), vec,
            rows, vec, vec, rows, vec, vec, vec, rows, vec, rows, vec, vec, vec, rows, P(),
        ),
        out_specs=(
            P("tower", "dp", None), P("tower", "dp", None, None),
            out_rows, out_vec, out_vec, out_rows, out_vec, out_vec, out_vec, out_rows, out_vec, out_rows, out_vec,
            out_vec, out_vec, out_rows, P(),
        ),
        check_vma=False,
    )
```
